32 devices in a mesh: tm: 2 (over x), height: 16 (over z, y, core).
Axes of the slice: x: 2, y: 2, z: 4, core: 2. Of those that a mesh axis runs over, the one named last changes fastest.
Arguments:
- pixels: bfloat16 [4, 3, 128, 1024], P('tm', None, 'height'), may hold values from -6 to 6
- conv_weight: bfloat16 [3, 3, 3, 48, 128], replicated, may hold values from -0.15625 to 0.15625
- conv_bias: float32 [128], replicated, may hold values from -3 to 3
- down_weight: bfloat16 [2, 2, 128, 256], replicated, may hold values from -0.25 to 0.25
- down_bias: float32 [256], replicated, may hold values from -3 to 3
- cotangent: bfloat16 [4, 16, 128, 256], P('tm', 'height'), may hold values from -6 to 6
Outputs:
- features: bfloat16 [4, 16, 128, 256], P('tm', 'height')
- grad_conv: float32 [3, 3, 3, 48, 128], replicated
- grad_conv_bias: float32 [128], replicated
- grad_down: float32 [2, 2, 128, 256], replicated
- grad_down_bias: float32 [256], replicated
- grad_pixels: float32 [4, 3, 128, 1024], P('tm', None, 'height')
The draws below stay inside these ranges and needn't reach their ends.
All inputs are finite; a program needn't handle non-finite values.
Results may differ from the reference program's by a relative error of at most 0.012.
Values may be sent and summed in bfloat16 or wider, within the bound.
No kernel may reach another device: no remote copies, remote signals or barrier semaphores. Data moves between devices by JAX's collectives and lax.ppermute only.
A program may use at most 64 MiB of HBM per device.

```python
import math
import jax
import jax.numpy as jnp
import numpy as np
from jax import lax

COLS = 256
COEFFS = 48
C1 = 128
C2 = 256
FRAMES = 4
ROWS = 32
HEIGHT_PX = 128
WIDTH_PX = 1024
HALF_ROWS = 16
HALF_COLS = 128


def levels(stream_key, shape, split, low, largest):
    def one(position, shards_of):
        draws = jax.random.uniform(jax.random.fold_in(jax.random.fold_in(stream_key, 6), position), (shards_of,), jnp.float32, low / len(split), largest / len(split))
        return jnp.repeat(jnp.exp(draws), shape[position] // shards_of).reshape((-1,) + (1,) * (len(shape) - position - 1))

    level = one(*split[0])
    for cut in split[1:]:
        level = level * one(*cut)
    return level


def normal_values(stream_key, shape, spread, most, cuts=(), dtype=jnp.bfloat16):
    values = spread * jax.random.normal(stream_key, shape, jnp.float32)
    if cuts:
        values = values * levels(stream_key, shape, cuts, -0.22, 0.18)
    return jnp.clip(values, -most, most).astype(dtype)


def setup_inputs(seed: int = 0) -> dict:
    splits = jax.random.split(jax.random.key(seed), 7)
    return {
        "pixels": normal_values(splits[0], (FRAMES, 3, HEIGHT_PX, WIDTH_PX), 1.0, 6.0, ((0, 2), (2, 16))),
        "conv_weight": normal_values(splits[1], (3, 3, 3, COEFFS, C1), (27 * COEFFS) ** -0.5, 0.15625),
        "conv_bias": normal_values(splits[2], (C1,), 0.5, 3.0, (), jnp.float32),
        "down_weight": normal_values(splits[3], (2, 2, C1, C2), (4 * C1) ** -0.5, 0.25),
        "down_bias": normal_values(splits[4], (C2,), 0.5, 3.0, (), jnp.float32),
        "cotangent": normal_values(splits[5], (FRAMES, HALF_ROWS, HALF_COLS, C2), 1.0, 6.0, ((0, 2), (1, 16))),
    }


haar_matrix = np.kron(np.array([[1.0, 1.0], [1.0, -1.0]]), np.array([[1.0, 1.0], [1.0, -1.0]])) * 0.5

def analyse(pixels):
    frame_count, colors, height_px, width_px = pixels.shape
    table = jnp.asarray(haar_matrix, jnp.float32)
    blocks = pixels.astype(jnp.float32).reshape(frame_count, colors, height_px // 4, 4, width_px // 4, 4)
    result = jnp.einsum('fkrucv,iu,jv->fkijrc', blocks, table, table)
    return result.reshape(frame_count, colors * 16, height_px // 4, width_px // 4)

def synthesise(dcoeffs):
    frame_count, channels, height_cells, width_cells = dcoeffs.shape
    table = jnp.asarray(haar_matrix, jnp.float32)
    parts = dcoeffs.reshape(frame_count, channels // 16, 4, 4, height_cells, width_cells)
    result = jnp.einsum('fkijrc,iu,jv->fkrucv', parts, table, table)
    return result.reshape(frame_count, channels // 16, height_cells * 4, width_cells * 4)

def reference(pixels, conv_weight, conv_bias, down_weight, down_bias, cotangent):
    coeffs = analyse(pixels).astype(jnp.bfloat16)
    frame_count, channels, height_cells, width_cells = coeffs.shape
    outer = conv_weight.shape[-1]
    extended = jnp.pad(coeffs, ((2, 0), (0, 0), (1, 1), (1, 1))).astype(jnp.float32)
    weight32 = conv_weight.astype(jnp.float32)
    pre = jnp.zeros((frame_count, height_cells, width_cells, outer), jnp.float32) + conv_bias
    windows = []
    for tap_time in range(3):
        for tap_row in range(3):
            for tap_col in range(3):
                window = extended[tap_time:tap_time + frame_count, :, tap_row:tap_row + height_cells, tap_col:tap_col + width_cells]
                windows.append((tap_time, tap_row, tap_col))
                pre = pre + jnp.einsum('fkrc,ko->frco', window, weight32[tap_time, tap_row, tap_col])
    act = jax.nn.silu(pre).astype(jnp.bfloat16)
    down32 = down_weight.astype(jnp.float32)
    grouped = act.astype(jnp.float32).reshape(frame_count, height_cells // 2, 2, width_cells // 2, 2, outer)
    features = (jnp.einsum('fqupvk,uvko->fqpo', grouped, down32) + down_bias).astype(jnp.bfloat16)
    cot32 = cotangent.astype(jnp.float32)
    dact = jnp.einsum('fqpo,uvko->fqupvk', cot32, down32).reshape(frame_count, height_cells, width_cells, outer)
    sig = jax.nn.sigmoid(pre)
    slope = (dact * sig * (1.0 + pre * (1.0 - sig))).astype(jnp.bfloat16)
    slope32 = slope.astype(jnp.float32)
    scale = 1.0 / math.sqrt(FRAMES * ROWS * COLS)
    grad_down = scale * jnp.einsum('fqupvk,fqpo->uvko', grouped, cot32)
    grad_down_bias = scale * lax.optimization_barrier(jnp.sum(cot32, axis=(0, 1, 2)))
    pieces = []
    for tap_time, tap_row, tap_col in windows:
        window = extended[tap_time:tap_time + frame_count, :, tap_row:tap_row + height_cells, tap_col:tap_col + width_cells]
        pieces.append(jnp.einsum('fkrc,frco->ko', window, slope32))
    grad_conv = scale * jnp.stack(pieces).reshape(3, 3, 3, channels, outer)
    grad_conv_bias = scale * lax.optimization_barrier(jnp.sum(slope32, axis=(0, 1, 2)))
    later = jnp.pad(slope32, ((0, 2), (1, 1), (1, 1), (0, 0)))
    dcoeffs = jnp.zeros((frame_count, channels, height_cells, width_cells), jnp.float32)
    for tap_time, tap_row, tap_col in windows:
        window = later[2 - tap_time:2 - tap_time + frame_count, 2 - tap_row:2 - tap_row + height_cells, 2 - tap_col:2 - tap_col + width_cells]
        dcoeffs = dcoeffs + jnp.einsum('frco,ko->fkrc', window, weight32[tap_time, tap_row, tap_col])
    grad_pixels = synthesise(dcoeffs)
    return (features, grad_conv, grad_conv_bias, grad_down, grad_down_bias, grad_pixels)
```

```python
import functools
import math

import jax
import jax.numpy as jnp
import numpy as np
from jax import lax
from jax.experimental import pallas as pl
from jax.experimental.pallas import tpu as pltpu
from jax.sharding import Mesh, PartitionSpec as P

BF16, F32 = jnp.bfloat16, jnp.float32
HAAR = np.kron(np.array([[1.0, 1.0], [1.0, -1.0]]), np.array([[1.0, 1.0], [1.0, -1.0]])) * 0.5
VMEM = pl.BlockSpec(memory_space=pltpu.VMEM)
SMEM = pl.BlockSpec(memory_space=pltpu.SMEM)
NN = (((1,), (0,)), ((), ()))
NT = (((1,), (1,)), ((), ()))
SLOT = 16


def mm(a, b, dims=NN):
    return lax.dot_general(a, b, dims, preferred_element_type=F32)


def split(x):
    high = x.astype(BF16)
    return high, (x - high.astype(F32)).astype(BF16)


def column_table(width_cells):
    half = width_cells // 2
    table = np.zeros((4 * width_cells, 4, 2, half), np.float32)
    for parity in range(2):
        for pair in range(half):
            for v in range(4):
                table[8 * pair + 4 * parity + v, :, parity, pair] = HAAR[:, v]
    return table.reshape(4 * width_cells, 4 * width_cells)


def row_table(frames, colors, rows):
    table = np.zeros((frames, rows, SLOT, frames, colors, rows, 4), np.float32)
    for f in range(frames):
        for r in range(rows):
            for k in range(colors):
                table[f, r, 4 * k : 4 * k + 4, f, k, r, :] = HAAR
    return table.reshape(frames * rows * SLOT, frames * colors * rows * 4)


def channel_table(channels):
    table = np.zeros((4 * SLOT, channels), np.float32)
    for channel in range(channels):
        k, i, j = channel // 16, channel // 4 % 4, channel % 4
        table[SLOT * j + 4 * k + i, channel] = 1.0
    return table


def weights_kernel(weight, order, forward, backward, turned):
    slots = 4 * SLOT
    for a in range(3):
        for b in range(3):
            for d in range(3):
                tap = mm(order[...], weight[9 * a + 3 * b + d])
                backward[slots * (3 * a + b) : slots * (3 * a + b + 1), 128 * d : 128 * (d + 1)] = (
                    tap.astype(BF16)
                )
                at = slots * (3 * b + d)
                turned[at : at + slots, :] = tap
        forward[a] = turned[...].T.astype(BF16)


def main_kernel(
    dims,
    place,
    own,
    earlier,
    inner,
    outer,
    table,
    rows_own,
    rows_halo,
    order_back,
    forward,
    backward,
    conv_bias,
    down_weight,
    down_bias,
    cotangent,
    features,
    keep,
    give,
    pixels_own,
    pixels_early,
    send_inner,
    send_outer,
    x,
    acts,
    packed,
    spread,
):
    frames, rows, colors, pair, channels = dims
    slots = 4 * SLOT
    core, plane = place[0], place[1]
    inner_row = jnp.where(core == 0, rows + 1, 0)
    outer_row = jnp.where(core == 0, 0, rows + 1)
    lane = lax.broadcasted_iota(jnp.int32, (1, pair), 1)

    def left(value):
        return jnp.where(lane == pair - 1, 0.0, pltpu.roll(value, pair - 1, 1))

    def right(value):
        return jnp.where(lane == 0, 0.0, pltpu.roll(value, 1, 1))

    def fill(pixels, rows_table, where):
        columns = mm(pixels[...], table[...])
        high, low = split(columns)
        cells = mm(rows_table[...], high) + mm(rows_table[...], low)
        for j in range(4):
            even = cells[:, 2 * j * pair : (2 * j + 1) * pair]
            odd = cells[:, (2 * j + 1) * pair : (2 * j + 2) * pair]
            even, odd = even.astype(BF16).astype(F32), odd.astype(BF16).astype(F32)
            for d, (one, two) in enumerate(((right(odd), even), (even, odd), (odd, left(even)))):
                one, two = one.astype(BF16), two.astype(BF16)
                at = slots * d + SLOT * j
                for block, (f, r) in enumerate(where):
                    take = slice(SLOT * block, SLOT * (block + 1))
                    x[f, r, at : at + SLOT, :pair] = one[take]
                    x[f, r, at : at + SLOT, pair:] = two[take]

    fill(earlier, rows_own, [(f, 1 + r) for f in range(2) for r in range(rows)])
    fill(own, rows_own, [(2 + f, 1 + r) for f in range(frames) for r in range(rows)])
    fill(inner, rows_halo, [(f, inner_row) for f in range(frames + 2)])
    fill(outer, rows_halo, [(f, outer_row) for f in range(frames + 2)])

    bias = jnp.broadcast_to(conv_bias[...], (128, 128)).T
    bias = jnp.concatenate([bias] * (2 * pair // 128), axis=1)

    def window(f, r):
        return x[f, r : r + 3].reshape(3 * 3 * slots, 2 * pair)

    spread[...] = jnp.zeros_like(spread)
    down_total = None
    conv_total = [None] * 3
    ones = jnp.ones((8, 2 * pair), BF16)
    slope_total = None
    cot_total = None
    for f in range(frames):
        for q in range(rows // 2):
            cot = cotangent[f, q]
            dact = mm(down_weight[...], cot, NT)
            for u in range(2):
                r = 2 * q + u
                pre = bias
                for a in range(3):
                    pre = pre + mm(forward[a], window(f + a, r))
                sig = jax.nn.sigmoid(pre)
                act = pre * sig
                acts[(2 * u) * 128 : (2 * u + 1) * 128] = act[:, :pair].astype(BF16)
                acts[(2 * u + 1) * 128 : (2 * u + 2) * 128] = act[:, pair:].astype(BF16)
                here = jnp.concatenate(
                    [
                        dact[2 * u * 128 : (2 * u + 1) * 128],
                        dact[(2 * u + 1) * 128 : (2 * u + 2) * 128],
                    ],
                    axis=1,
                )
                slope = here * sig * (1.0 + pre * (1.0 - sig))
                slope16 = slope.astype(BF16)
                even, odd = slope16[:, :pair].astype(F32), slope16[:, pair:].astype(F32)
                for a in range(3):
                    part = mm(window(f + a, r), slope16, NT)
                    conv_total[a] = part if conv_total[a] is None else conv_total[a] + part
                part = mm(ones, slope16, NT)
                slope_total = part if slope_total is None else slope_total + part
                shifted = jnp.concatenate(
                    [
                        jnp.concatenate([odd, left(even)], axis=1).astype(BF16),
                        slope16,
                        jnp.concatenate([right(odd), even], axis=1).astype(BF16),
                    ],
                    axis=0,
                )
                reach = mm(backward[...], shifted)
                for a in range(3):
                    for b in range(3):
                        at = slots * (3 * a + b)
                        spread[f + a, r + b] += reach[at : at + slots]
            part = mm(acts[...], cot)
            down_total = part if down_total is None else down_total + part
            part = mm(ones[:, :pair], cot)
            cot_total = part if cot_total is None else cot_total + part
            turned = jnp.concatenate(
                [acts[128 * n : 128 * (n + 1)].astype(F32).T.astype(BF16) for n in range(4)], axis=1
            )
            features[f, q] = (mm(turned, down_weight[...]) + down_bias[...]).astype(BF16)

    flat = packed
    at = 0
    for a in range(3):
        for t in range(9):
            part = conv_total[a][slots * t : slots * (t + 1)]
            high, low = split(part)
            flat[at : at + channels] = mm(order_back[...], high) + mm(order_back[...], low)
            at += channels
    for half in range(2):
        flat[at : at + 512] = down_total[:, 128 * half : 128 * (half + 1)]
        at += 512
    sums = [slope_total[0:1], cot_total[0:1, :128], cot_total[0:1, 128:]]
    highs = [value.astype(BF16).astype(F32) for value in sums]
    lows = [value - high for value, high in zip(sums, highs)]
    flat[at : at + 8] = jnp.concatenate(highs + lows + [jnp.zeros((2, 128), F32)], axis=0)
    at += 8
    if at < packed.shape[0]:
        flat[at:] = jnp.zeros((packed.shape[0] - at, 128), F32)
    chunk = keep.shape[1]
    for m in range(4):
        slot = jnp.bitwise_xor(plane, m)
        keep[m] = flat[pl.ds(pl.multiple_of((4 * core + slot) * chunk, 8), chunk)]
        give[m] = flat[pl.ds(pl.multiple_of((4 * (1 - core) + slot) * chunk, 8), chunk)].astype(BF16)

    def synthesise(blocks, rows_table):
        cells = jnp.concatenate(
            [
                jnp.concatenate([spread[f, r, SLOT * j : SLOT * (j + 1)] for j in range(4)], axis=1)
                for f, r in blocks
            ],
            axis=0,
        ).astype(BF16)
        high, low = split(mm(cells, table[...], NT))
        back = (((0,), (0,)), ((), ()))
        return mm(rows_table[...], high, back) + mm(rows_table[...], low, back)

    pixels_early[...] = synthesise([(f, 1 + r) for f in range(2) for r in range(rows)], rows_own)
    pixels_own[...] = synthesise(
        [(2 + f, 1 + r) for f in range(frames) for r in range(rows)], rows_own
    )
    send_inner[...] = synthesise([(f, inner_row) for f in range(frames + 2)], rows_halo).astype(BF16)
    send_outer[...] = synthesise([(f, outer_row) for f in range(frames + 2)], rows_halo).astype(BF16)


def finish_kernel(scale, channels, place, mine, others, theirs, conv, conv_bias, down, down_bias, flat):
    core, plane = place[0], place[1]
    chunk = mine.shape[0]
    for m in range(4):
        slot = jnp.bitwise_xor(plane, m)
        value = mine[...] if m == 0 else others[m - 1]
        flat[pl.ds(pl.multiple_of((4 * core + slot) * chunk, 8), chunk)] = value.astype(F32) * scale
        flat[pl.ds(pl.multiple_of((4 * (1 - core) + slot) * chunk, 8), chunk)] = (
            theirs[m].astype(F32) * scale
        )
    at = 0
    for t in range(27):
        conv[t] = flat[at : at + channels]
        at += channels
    for half in range(2):
        down[:, 128 * half : 128 * (half + 1)] = flat[at : at + 512]
        at += 512
    sums = flat[at : at + 8]
    sums = sums[0:3] + sums[3:6]
    conv_bias[...] = sums[0:1]
    down_bias[:, :128] = sums[1:2]
    down_bias[:, 128:] = sums[2:3]


def local(axes, pixels, conv_weight, conv_bias, down_weight, down_bias, cotangent):
    times, heights = axes["tm"], axes["height"]
    frames, colors, pixel_rows, pixel_columns = pixels.shape
    rows, columns = pixel_rows // 4, pixel_columns // 4
    pair = columns // 2
    channels, width = conv_weight.shape[3:]
    width2 = down_weight.shape[3]
    core = lax.axis_index("core")
    plane = 2 * lax.axis_index("tm_lo") + lax.axis_index("y")
    place = jnp.stack([core, plane]).astype(jnp.int32)
    count_tm, count_height = lax.axis_size(times), lax.axis_size(heights)
    slots = 4 * SLOT

    def along_tm(value, step):
        pairs = [(i, i + step) for i in range(count_tm) if 0 <= i + step < count_tm]
        return lax.ppermute(value, times, pairs)

    def swap_inner(value):
        return lax.ppermute(value, "core", [(0, 1), (1, 0)])

    def swap_outer(value):
        pairs = [(i, i + 1) for i in range(1, count_height - 1, 2)]
        return lax.ppermute(value, heights, pairs + [(j, i) for i, j in pairs])

    def exchange(value, axes, mask):
        size = lax.axis_size(axes)
        return lax.ppermute(value, axes, [(i, i ^ mask) for i in range(size)])

    order = channel_table(channels)
    forward, backward = pl.pallas_call(
        weights_kernel,
        out_shape=(
            jax.ShapeDtypeStruct((3, width, 9 * slots), BF16),
            jax.ShapeDtypeStruct((9 * slots, 3 * width), BF16),
        ),
        in_specs=[VMEM, VMEM],
        out_specs=(VMEM, VMEM),
        scratch_shapes=[pltpu.VMEM((9 * slots, width), F32)],
        name="weights",
    )(conv_weight.reshape(27, channels, width), jnp.asarray(order, BF16))

    own = pixels.reshape(frames * colors * pixel_rows, pixel_columns)
    recent = pixels[frames - 2 :].reshape(2 * colors * pixel_rows, pixel_columns)
    earlier = along_tm(recent, 1)
    tall = jnp.concatenate([earlier, own], axis=0)
    tall = tall.reshape((frames + 2) * colors, pixel_rows, pixel_columns)
    top, bottom = tall[:, :4], tall[:, pixel_rows - 4 :]
    flat_halo = ((frames + 2) * colors * 4, pixel_columns)
    inner = swap_inner(jnp.where(core == 0, bottom, top).reshape(flat_halo))
    outer = swap_outer(jnp.where(core == 0, top, bottom).reshape(flat_halo))

    data_rows = 27 * channels + 4 * width * width2 // 128 + 8
    chunk = -(-data_rows // 64) * 8
    features, keep, give, pixels_own, pixels_early, send_inner, send_outer = pl.pallas_call(
        functools.partial(main_kernel, (frames, rows, colors, pair, channels)),
        out_shape=(
            jax.ShapeDtypeStruct((frames, rows // 2, pair, width2), BF16),
            jax.ShapeDtypeStruct((4, chunk, 128), F32),
            jax.ShapeDtypeStruct((4, chunk, 128), BF16),
            jax.ShapeDtypeStruct(own.shape, F32),
            jax.ShapeDtypeStruct(recent.shape, F32),
            jax.ShapeDtypeStruct(flat_halo, BF16),
            jax.ShapeDtypeStruct(flat_halo, BF16),
        ),
        in_specs=[SMEM] + [VMEM] * 14,
        out_specs=(VMEM,) * 7,
        scratch_shapes=[
            pltpu.VMEM((frames + 2, rows + 2, 3 * slots, columns), BF16),
            pltpu.VMEM((4 * width, pair), BF16),
            pltpu.VMEM((8 * chunk, 128), F32),
            pltpu.VMEM((frames + 2, rows + 2, slots, columns), F32),
        ],
        name="main",
    )(
        place,
        own,
        earlier,
        inner,
        outer,
        jnp.asarray(column_table(columns), BF16),
        jnp.asarray(row_table(frames, colors, rows), BF16),
        jnp.asarray(row_table(frames + 2, colors, 1), BF16),
        jnp.asarray(order.T, BF16),
        forward,
        backward,
        conv_bias.reshape(1, width),
        down_weight.reshape(4 * width, width2),
        down_bias.reshape(1, width2),
        cotangent,
    )

    total = keep + swap_inner(give).astype(F32)
    planes = ("tm_lo", "y")
    parts = [exchange(total[m].astype(BF16), planes, m) for m in (1, 2, 3)]
    mine = total[0] + sum(part.astype(F32) for part in parts)
    for axis in axes["rest"]:
        sent = mine.astype(BF16)
        parts = [exchange(sent, axis, m) for m in range(1, lax.axis_size(axis))]
        mine = mine + sum(part.astype(F32) for part in parts)
    mine = mine.astype(BF16)
    others = jnp.stack([exchange(mine, planes, m) for m in (1, 2, 3)])
    theirs = swap_inner(jnp.concatenate([mine[None], others]))
    count = frames * count_tm * rows * count_height * columns
    grad_conv, grad_conv_bias, grad_down, grad_down_bias = pl.pallas_call(
        functools.partial(finish_kernel, 1.0 / math.sqrt(count), channels),
        out_shape=(
            jax.ShapeDtypeStruct((27, channels, width), F32),
            jax.ShapeDtypeStruct((1, width), F32),
            jax.ShapeDtypeStruct((4 * width, width2), F32),
            jax.ShapeDtypeStruct((1, width2), F32),
        ),
        in_specs=[SMEM, VMEM, VMEM, VMEM],
        out_specs=(VMEM,) * 4,
        scratch_shapes=[pltpu.VMEM((8 * chunk, 128), F32)],
        name="finish",
    )(place, mine, others, theirs)

    from_inner = swap_inner(send_inner).reshape((frames + 2) * colors, 4, pixel_columns)
    from_outer = swap_outer(send_outer).reshape((frames + 2) * colors, 4, pixel_columns)
    above = jnp.where(core == 0, from_outer, from_inner).astype(F32)
    below = jnp.where(core == 0, from_inner, from_outer).astype(F32)
    gap = pixel_rows - 4
    halo = jnp.pad(above, ((0, 0), (0, gap), (0, 0))) + jnp.pad(below, ((0, 0), (gap, 0), (0, 0)))
    early = pixels_early.reshape(2 * colors, pixel_rows, pixel_columns) + halo[: 2 * colors]
    late = pixels_own.reshape(frames * colors, pixel_rows, pixel_columns) + halo[2 * colors :]
    following = along_tm(early.astype(BF16), -1).astype(F32)
    skipped = jnp.zeros(((frames - 2) * colors, pixel_rows, pixel_columns), F32)
    grad_pixels = late + jnp.concatenate([skipped, following], axis=0)
    return (
        features,
        grad_conv.reshape(conv_weight.shape),
        grad_conv_bias.reshape(width),
        grad_down.reshape(down_weight.shape),
        grad_down_bias.reshape(width2),
        grad_pixels.reshape(pixels.shape),
    )


def factors(size):
    parts = []
    while size > 1:
        part = 4 if size % 4 == 0 else 2
        assert size % part == 0
        parts.append(part)
        size //= part
    return parts


def solution(mesh):
    count_tm, count_height = mesh.shape["tm"], mesh.shape["height"]
    tm_parts, height_parts = factors(count_tm // 2), factors(count_height // 4)
    tm_names = tuple(f"tm_{n}" for n in range(len(tm_parts)))
    height_names = tuple(f"z_{n}" for n in range(len(height_parts)))
    axes = {
        "tm": tm_names + ("tm_lo",),
        "height": height_names + ("y", "core"),
        "rest": tm_names + height_names,
    }
    fine = Mesh(
        mesh.devices.reshape(tm_parts + [2] + height_parts + [2, 2]), axes["tm"] + axes["height"]
    )
    tm, height = axes["tm"], axes["height"]
    return jax.shard_map(
        functools.partial(local, axes),
        mesh=fine,
        in_specs=(P(tm, None, height, None), P(), P(), P(), P(), P(tm, height, None, None)),
        out_specs=(
            P(tm, height, None, None),
            P(),
            P(),
            P(),
            P(),
            P(tm, None, height, None),
        ),
        check_vma=False,
    )
```

```python
import functools
import math

import jax
import jax.numpy as jnp
import numpy as np
from jax import lax
from jax.experimental import pallas as pl
from jax.experimental.pallas import tpu as pltpu
from jax.sharding import Mesh, PartitionSpec as P


BF16, F32 = jnp.bfloat16, jnp.float32
HAAR = np.kron(np.array([[1.0, 1.0], [1.0, -1.0]]), np.array([[1.0, 1.0], [1.0, -1.0]])) * 0.5
VMEM = pl.BlockSpec(memory_space=pltpu.VMEM)
SMEM = pl.BlockSpec(memory_space=pltpu.SMEM)
ANY = pl.BlockSpec(memory_space=pl.ANY)
NN = (((1,), (0,)), ((), ()))
NT = (((1,), (1,)), ((), ()))
COLORS, CH, WIDTH = 3, 48, 128
TAPS = 3 * CH


def mm(a, b, dims=NN):
    return lax.dot_general(a, b, dims, preferred_element_type=F32)


def split(x):
    high = x.astype(BF16)
    return high, (x - high.astype(F32)).astype(BF16)


def call(body, outs, ins, scratch=(), flops=0, grant=24, **more):
    shapes = [jax.ShapeDtypeStruct(shape, dtype) for shape, dtype in outs]
    return pl.pallas_call(
        body,
        out_shape=shapes,
        scratch_shapes=list(scratch),
        cost_estimate=pl.CostEstimate(flops=flops, bytes_accessed=1 << 20, transcendentals=0),
        compiler_params=pltpu.CompilerParams(vmem_limit_bytes=grant << 20),
        in_specs=ins,
        **{"out_specs": [VMEM] * len(outs), **more},
    )


def column_table(quarter):
    table = np.zeros((8 * quarter, 4, 2, quarter), np.float32)
    for parity in range(2):
        for pair in range(quarter):
            for v in range(4):
                table[8 * pair + 4 * parity + v, :, parity, pair] = HAAR[:, v]
    return table.reshape(8 * quarter, 8 * quarter)


def row_table(frames, rows):
    table = np.zeros((frames, rows, COLORS, 4, 4, 4, frames, COLORS, rows, 4), np.float32)
    for f in range(frames):
        for r in range(rows):
            for k in range(COLORS):
                for j in range(4):
                    table[f, r, k, :, j, j, f, k, r, :] = HAAR
    return table.reshape(frames * rows * CH, 4 * frames * COLORS * rows * 4)


def shifts(pair):
    lane = lax.broadcasted_iota(jnp.int32, (1, pair), 1)

    def left(value):
        return jnp.where(lane == pair - 1, 0.0, pltpu.roll(value, pair - 1, 1))

    def right(value):
        return jnp.where(lane == 0, 0.0, pltpu.roll(value, 1, 1))

    return left, right


def analyse(groups, table, rows_tables, x, places, pair):
    left, right = shifts(pair)
    low_half = lax.broadcasted_iota(jnp.int32, (1, pair), 1) < pair // 2
    size, width = groups[0].shape
    stacked = [group[:, half * width // 2 : (half + 1) * width // 2] for group in groups for half in range(2)]
    columns = mm(jnp.concatenate(stacked, axis=0), table[...])
    for n, (rows_table, where) in enumerate(zip(rows_tables, places)):
        blocks = []
        for j in range(4):
            one = columns[2 * n * size : (2 * n + 1) * size, pair * j : pair * (j + 1)]
            two = columns[(2 * n + 1) * size : (2 * n + 2) * size, pair * j : pair * (j + 1)]
            even = jnp.where(low_half, one, pltpu.roll(two, pair // 2, 1))
            odd = jnp.where(low_half, pltpu.roll(one, pair // 2, 1), two)
            blocks.append(jnp.concatenate([even, odd], axis=1))
        high, low = split(jnp.concatenate(blocks, axis=0))
        cells = (mm(rows_table[...], high) + mm(rows_table[...], low)).astype(BF16)
        even, odd = cells[:, :pair].astype(F32), cells[:, pair:].astype(F32)
        taps = (
            jnp.concatenate([right(odd), even], axis=1).astype(BF16),
            cells,
            jnp.concatenate([odd, left(even)], axis=1).astype(BF16),
        )
        for block, (f, r) in enumerate(where):
            for d in range(3):
                x[f, r, CH * d : CH * (d + 1)] = taps[d][CH * block : CH * (block + 1)]


def synthesise(groups, table, rows_tables, pair):
    low_half = lax.broadcasted_iota(jnp.int32, (1, pair), 1) < pair // 2
    stacked = []
    for cells, rows_table in zip(groups, rows_tables):
        turned = mm(rows_table[...], cells.astype(BF16), (((0,), (0,)), ((), ())))
        size = turned.shape[0] // 4
        ones, twos = [], []
        for j in range(4):
            even = turned[size * j : size * (j + 1), :pair]
            odd = turned[size * j : size * (j + 1), pair:]
            ones.append(jnp.where(low_half, even, pltpu.roll(odd, pair // 2, 1)))
            twos.append(jnp.where(low_half, pltpu.roll(even, pair // 2, 1), odd))
        stacked += [jnp.concatenate(ones, axis=1), jnp.concatenate(twos, axis=1)]
    pixels = mm(jnp.concatenate(stacked, axis=0).astype(BF16), table[...], NT)
    size = stacked[0].shape[0]
    return [
        jnp.concatenate(
            [pixels[2 * n * size : (2 * n + 1) * size], pixels[(2 * n + 1) * size : (2 * n + 2) * size]],
            axis=1,
        )
        for n in range(len(groups))
    ]


def weights_kernel(weight, inside, outside, backward):
    for a in range(3):
        for b in range(3):
            for d in range(3):
                at = CH * (3 * a + b)
                backward[at : at + CH, WIDTH * d : WIDTH * (d + 1)] = weight[9 * a + 3 * b + d]
        taps = weight[9 * a : 9 * a + 9].reshape(3 * TAPS, WIDTH).astype(F32)
        at = slice(WIDTH * a, WIDTH * (a + 1))
        inside[0, at] = taps[TAPS:].T.astype(BF16)
        inside[1, at] = taps[: 2 * TAPS].T.astype(BF16)
        outside[0, at] = taps[:TAPS].T.astype(BF16)
        outside[1, at] = taps[2 * TAPS :].T.astype(BF16)


def pack_kernel(dims, place, own, earlier, inner, outer):
    frames, rows, _ = dims
    core = place[0]
    at = 0
    for part, count in ((earlier, 2), (own, frames)):
        count *= COLORS
        pixels = part[...].astype(F32).reshape(count, 4 * rows, part.shape[1])
        top, bottom = pixels[:, :4], pixels[:, 4 * rows - 4 :]
        size = 4 * count
        for target, first, second in ((inner, bottom, top), (outer, top, bottom)):
            chosen = jnp.where(core == 0, first, second)
            target[at : at + size] = chosen.reshape(size, part.shape[1]).astype(BF16)
        at += size


def taps_of(frame, frames):
    return [(f, frame - f) for f in range(frames) if 0 <= frame - f < 3]


def convolve(total, weights, values, frame, frames):
    used = taps_of(frame, frames)
    first = min(a for _, a in used)
    last = max(a for _, a in used)
    part = mm(weights[WIDTH * first : WIDTH * (last + 1)], values)
    for f, a in used:
        here = part[WIDTH * (a - first) : WIDTH * (a - first + 1)]
        total[f] = here if total[f] is None else total[f] + here


def early_kernel(
    dims, own, earlier, table, rows_own, inside, conv_bias, down_weight, cotangent, x, pre, dact
):
    frames, rows, pair = dims
    places = [
        [(f, r) for f in range(2) for r in range(rows)],
        [(2 + f, r) for f in range(frames) for r in range(rows)],
    ]
    analyse([earlier[...], own[...]], table, [rows_own, rows_own], x, places, pair)
    bias = jnp.broadcast_to(conv_bias[...], (WIDTH, WIDTH)).T
    bias = jnp.concatenate([bias] * (2 * pair // WIDTH), axis=1)
    for r in range(rows):
        total = [bias] * frames
        for frame in range(frames + 2):
            values = x[frame].reshape(rows * TAPS, 2 * pair)
            convolve(total, inside[r], values, frame, frames)
        for f in range(frames):
            pre[f, r] = total[f]
    for f in range(frames):
        dact[f] = mm(down_weight[...], cotangent[f, 0], NT)


def main_kernel(
    dims,
    place,
    inner,
    outer,
    table,
    rows_halo,
    x_own,
    pre_own,
    dact,
    outside,
    cotangent,
    keep,
    give,
    acts,
    slopes,
    x,
    packed,
):
    frames, rows, pair = dims
    core, plane = place[0], place[1]
    inner_row = jnp.where(core == 0, rows + 1, 0)
    outer_row = jnp.where(core == 0, 0, rows + 1)
    for frame in range(frames + 2):
        x[frame, 1 : rows + 1] = x_own[frame]
    places = [
        [(f, inner_row) for f in range(frames + 2)],
        [(f, outer_row) for f in range(frames + 2)],
    ]
    analyse([inner[...], outer[...]], table, [rows_halo, rows_halo], x, places, pair)

    for r in range(rows):
        total = [pre_own[f, r] for f in range(frames)]
        edge = 0 if r == 0 else rows + 1
        for frame in range(frames + 2):
            convolve(total, outside[r], x[frame, edge], frame, frames)
        for f in range(frames):
            pre = total[f]
            sig = jax.nn.sigmoid(pre)
            act = pre * sig
            at = 2 * WIDTH * r
            acts[f, at : at + WIDTH] = act[:, :pair].astype(BF16)
            acts[f, at + WIDTH : at + 2 * WIDTH] = act[:, pair:].astype(BF16)
            here = jnp.concatenate(
                [dact[f, at : at + WIDTH], dact[f, at + WIDTH : at + 2 * WIDTH]], axis=1
            )
            slope = here * sig * (1.0 + pre * (1.0 - sig))
            slopes[WIDTH * f : WIDTH * (f + 1), 2 * pair * r : 2 * pair * (r + 1)] = slope.astype(BF16)

    conv_total = [None] * 3
    for frame in range(frames + 2):
        used = taps_of(frame, frames)
        first, last = used[0][0], used[-1][0]
        values = jnp.concatenate(
            [x[frame, r : r + 3].reshape(3 * TAPS, 2 * pair) for r in range(rows)], axis=1
        )
        part = mm(values, slopes[WIDTH * first : WIDTH * (last + 1)], NT)
        for f, a in used:
            here = part[:, WIDTH * (f - first) : WIDTH * (f - first + 1)]
            conv_total[a] = here if conv_total[a] is None else conv_total[a] + here
    down_total = None
    cot_total = None
    ones = jnp.ones((8, 2 * pair * rows), BF16)
    for f in range(frames):
        part = mm(acts[f], cotangent[f, 0])
        down_total = part if down_total is None else down_total + part
        part = mm(ones[:, :pair], cotangent[f, 0])
        cot_total = part if cot_total is None else cot_total + part
    slope_total = mm(ones, slopes[...], NT)
    slope_total = sum(slope_total[0:1, WIDTH * f : WIDTH * (f + 1)] for f in range(frames))

    chunk = keep.shape[1]
    half = 27 * CH // 2
    conv = jnp.concatenate(conv_total, axis=0)
    sums = [slope_total, cot_total[0:1, :WIDTH], cot_total[0:1, WIDTH:]]
    highs = [value.astype(BF16).astype(F32) for value in sums]
    lows = [value - high for value, high in zip(sums, highs)]
    sums = jnp.concatenate(highs + lows + [jnp.zeros((2, WIDTH), F32)], axis=0)
    down_rows = 2 * rows * WIDTH
    for h in range(2):
        packed[h, :half] = conv[half * h : half * (h + 1)]
        packed[h, half : half + down_rows] = down_total[:, WIDTH * h : WIDTH * (h + 1)]
        packed[h, half + down_rows : half + down_rows + 8] = sums if h == 0 else jnp.zeros_like(sums)
        rest = 4 * chunk - half - down_rows - 8
        if rest:
            packed[h, half + down_rows + 8 :] = jnp.zeros((rest, WIDTH), F32)
    for m in range(4):
        at = pl.multiple_of(jnp.bitwise_xor(plane, m) * chunk, 8)
        keep[m] = packed[core, pl.ds(at, chunk)]
        give[m] = packed[1 - core, pl.ds(at, chunk)].astype(BF16)


def late_kernel(
    dims,
    place,
    acts,
    slopes,
    backward,
    down_weight,
    down_bias,
    table,
    rows_own,
    rows_halo,
    features,
    pixels_own,
    pixels_early,
    send_inner,
    send_outer,
    spread,
):
    frames, rows, pair = dims
    core = place[0]
    inner_row = jnp.where(core == 0, rows + 1, 0)
    outer_row = jnp.where(core == 0, 0, rows + 1)
    left, right = shifts(pair)
    spread[...] = jnp.zeros_like(spread)
    for f in range(frames):
        for r in range(rows):
            slope = slopes[WIDTH * f : WIDTH * (f + 1), 2 * pair * r : 2 * pair * (r + 1)]
            even, odd = slope[:, :pair].astype(F32), slope[:, pair:].astype(F32)
            shifted = jnp.concatenate(
                [
                    jnp.concatenate([odd, left(even)], axis=1).astype(BF16),
                    slope,
                    jnp.concatenate([right(odd), even], axis=1).astype(BF16),
                ],
                axis=0,
            )
            reach = mm(backward[...], shifted)
            for a in range(3):
                for b in range(3):
                    at = CH * (3 * a + b)
                    spread[f + a, r + b] += reach[at : at + CH]

    def rows_of(blocks):
        return jnp.concatenate([spread[f, r] for f, r in blocks], axis=0)

    groups = [
        rows_of([(f, 1 + r) for f in range(2) for r in range(rows)]),
        rows_of([(2 + f, 1 + r) for f in range(frames) for r in range(rows)]),
        rows_of([(f, inner_row) for f in range(frames + 2)]),
        rows_of([(f, outer_row) for f in range(frames + 2)]),
    ]
    tables = [rows_own, rows_own, rows_halo, rows_halo]
    early, own, inner, outer = synthesise(groups, table, tables, pair)
    pixels_early[...] = early
    pixels_own[...] = own
    send_inner[...] = inner.astype(BF16)
    send_outer[...] = outer.astype(BF16)
    for f in range(frames):
        turned = jnp.concatenate(
            [acts[f, WIDTH * n : WIDTH * (n + 1)].astype(F32).T.astype(BF16) for n in range(4)], axis=1
        )
        features[f, 0] = (mm(turned, down_weight[...]) + down_bias[...]).astype(BF16)


def finish_kernel(scale, other, place, *refs):
    pieces, (conv, conv_bias, down, down_bias, flat, sums, sems) = refs[:4], refs[-7:]
    if other:
        pieces = [refs[0].at[m] for m in range(4)]
    core, plane = place[0], place[1]
    which = 1 - core if other else core
    chunk = pieces[0].shape[0]
    for m in range(4):
        at = pl.multiple_of(jnp.bitwise_xor(plane, m) * chunk, 8)
        flat[pl.ds(at, chunk)] = pieces[m][...].astype(F32) * scale
    half, down_rows = conv.shape[0] // 2, down.shape[0]
    at = pl.multiple_of(half * which, 8)
    copies = [
        pltpu.make_async_copy(flat.at[pl.ds(0, half)], conv.at[pl.ds(at, half)], sems.at[0]),
        pltpu.make_async_copy(
            flat.at[pl.ds(half, down_rows)],
            down.at[:, pl.ds(pl.multiple_of(WIDTH * which, WIDTH), WIDTH)],
            sems.at[1],
        ),
    ]
    for copy in copies:
        copy.start()

    @pl.when(which == 0)
    def _():
        at = half + down_rows
        total = flat[at : at + 8]
        total = total[0:3] + total[3:6]
        for n in range(3):
            sums[n] = total[n : n + 1]
        targets = [conv_bias, down_bias.at[:, pl.ds(0, WIDTH)], down_bias.at[:, pl.ds(WIDTH, WIDTH)]]
        small = [
            pltpu.make_async_copy(sums.at[n], target, sems.at[2 + n]) for n, target in enumerate(targets)
        ]
        for copy in small:
            copy.start()
        for copy in small:
            copy.wait()

    for copy in copies:
        copy.wait()


def local(axes, pixels, conv_weight, conv_bias, down_weight, down_bias, cotangent):
    times, heights = axes["tm"], axes["height"]
    frames, colors, pixel_rows, pixel_columns = pixels.shape
    rows, columns = pixel_rows // 4, pixel_columns // 4
    assert frames == 2 and rows == 2 and colors == COLORS
    assert conv_weight.shape[3:] == (CH, WIDTH)
    pair = columns // 2
    width2 = down_weight.shape[3]
    core = lax.axis_index("core")
    plane = 2 * lax.axis_index("tm_lo") + lax.axis_index("y")
    place = jnp.stack([core, plane]).astype(jnp.int32)
    count_tm, count_height = lax.axis_size(times), lax.axis_size(heights)
    dims = (frames, rows, pair)

    def along_tm(value, step):
        pairs = [(i, i + step) for i in range(count_tm) if 0 <= i + step < count_tm]
        return lax.ppermute(value, times, pairs)

    def swap_inner(value):
        return lax.ppermute(value, "core", [(0, 1), (1, 0)])

    def swap_outer(value):
        pairs = [(i, i + 1) for i in range(1, count_height - 1, 2)]
        return lax.ppermute(value, heights, pairs + [(j, i) for i, j in pairs])

    def exchange(value, axes, mask):
        size = lax.axis_size(axes)
        return lax.ppermute(value, axes, [(i, i ^ mask) for i in range(size)])

    table = jnp.asarray(column_table(pair // 2), BF16)
    rows_own = jnp.asarray(row_table(frames, rows), BF16)
    rows_halo = jnp.asarray(row_table(frames + 2, 1), BF16)

    own = pixels.reshape(frames * colors * pixel_rows, pixel_columns)
    earlier = along_tm(own, 1)
    inside, outside, backward = call(
        weights_kernel,
        [((2, 3 * WIDTH, 2 * TAPS), BF16), ((2, 3 * WIDTH, TAPS), BF16), ((9 * CH, 3 * WIDTH), BF16)],
        [VMEM],
        flops=10**9,
    )(conv_weight.reshape(27, CH, WIDTH))
    frame_shape = (2 * colors, pixel_rows, pixel_columns)
    flat_halo = ((frames + 2) * colors * 4, pixel_columns)
    send_inner, send_outer = call(
        functools.partial(pack_kernel, dims),
        [(flat_halo, BF16), (flat_halo, BF16)],
        [SMEM, VMEM, VMEM],
    )(place, own, earlier)
    inner = swap_inner(send_inner)
    outer = swap_outer(send_outer)

    down_flat = down_weight.reshape(4 * WIDTH, width2)
    x_own, pre_own, dact = call(
        functools.partial(early_kernel, dims),
        [
            ((frames + 2, rows, TAPS, columns), BF16),
            ((frames, rows, WIDTH, columns), F32),
            ((frames, 4 * WIDTH, pair), F32),
        ],
        [VMEM] * 8,
        flops=10**9,
    )(own, earlier, table, rows_own, inside, conv_bias.reshape(1, WIDTH), down_flat, cotangent)

    data_rows = 27 * CH // 2 + 4 * WIDTH + 8
    chunk = -(-data_rows // 32) * 8
    keep, give, acts, slopes = call(
        functools.partial(main_kernel, dims),
        [
            ((4, chunk, WIDTH), F32),
            ((4, chunk, WIDTH), BF16),
            ((frames, 4 * WIDTH, pair), BF16),
            ((frames * WIDTH, rows * columns), BF16),
        ],
        [SMEM] + [VMEM] * 9,
        [
            pltpu.VMEM((frames + 2, rows + 2, TAPS, columns), BF16),
            pltpu.VMEM((2, 4 * chunk, WIDTH), F32),
        ],
        flops=10**9,
    )(place, inner, outer, table, rows_halo, x_own, pre_own, dact, outside, cotangent)

    features, pixels_own, pixels_early, send_inner, send_outer = call(
        functools.partial(late_kernel, dims),
        [
            ((frames, rows // 2, pair, width2), BF16),
            (own.shape, F32),
            (own.shape, F32),
            (flat_halo, BF16),
            (flat_halo, BF16),
        ],
        [SMEM] + [VMEM] * 8,
        [pltpu.VMEM((frames + 2, rows + 2, CH, columns), F32)],
        flops=10**9,
    )(
        place,
        acts,
        slopes,
        backward,
        down_flat,
        down_bias.reshape(1, width2),
        table,
        rows_own,
        rows_halo,
    )

    total = keep + swap_inner(give).astype(F32)
    planes = ("tm_lo", "y")
    parts = [exchange(total[m].astype(BF16), planes, m) for m in (1, 2, 3)]
    mine = total[0] + sum(part.astype(F32) for part in parts)
    for axis in axes["rest"]:
        sent = mine.astype(BF16)
        parts = [exchange(sent, axis, m) for m in range(1, lax.axis_size(axis))]
        mine = mine + sum(part.astype(F32) for part in parts)
    mine = mine.astype(BF16)
    pieces = [mine] + [exchange(mine, planes, m) for m in (1, 2, 3)]
    theirs = swap_inner(jnp.stack(pieces))
    count = frames * count_tm * rows * count_height * columns
    scale = 1.0 / math.sqrt(count)
    outs = [
        ((27 * CH, WIDTH), F32),
        ((1, WIDTH), F32),
        ((4 * WIDTH, width2), F32),
        ((1, width2), F32),
    ]
    scratch = [
        pltpu.VMEM((4 * chunk, WIDTH), F32),
        pltpu.VMEM((3, 1, WIDTH), F32),
        pltpu.SemaphoreType.DMA((5,)),
    ]
    grads = call(
        functools.partial(finish_kernel, scale, False),
        outs,
        [SMEM] + [VMEM] * 4,
        scratch,
        out_specs=[ANY] * 4,
    )(place, *pieces)
    grad_conv, grad_conv_bias, grad_down, grad_down_bias = call(
        functools.partial(finish_kernel, scale, True),
        outs,
        [SMEM, VMEM] + [ANY] * 4,
        scratch,
        out_specs=[ANY] * 4,
        input_output_aliases={2: 0, 3: 1, 4: 2, 5: 3},
    )(place, theirs, *grads)

    from_inner = swap_inner(send_inner).reshape((frames + 2) * colors, 4, pixel_columns)
    from_outer = swap_outer(send_outer).reshape((frames + 2) * colors, 4, pixel_columns)
    above = jnp.where(core == 0, from_outer, from_inner).astype(F32)
    below = jnp.where(core == 0, from_inner, from_outer).astype(F32)
    halo = jnp.concatenate([above, below], axis=1)
    early = pixels_early.reshape(frame_shape) + halo[: 2 * colors]
    late = pixels_own.reshape(frame_shape) + halo[2 * colors :]
    grad_pixels = late + along_tm(early.astype(BF16), -1).astype(F32)
    return (
        features,
        grad_conv.reshape(conv_weight.shape),
        grad_conv_bias.reshape(WIDTH),
        grad_down.reshape(down_weight.shape),
        grad_down_bias.reshape(width2),
        grad_pixels.reshape(pixels.shape),
    )


def factors(size):
    parts = []
    while size > 1:
        part = 4 if size % 4 == 0 else 2
        assert size % part == 0
        parts.append(part)
        size //= part
    return parts


def solution(mesh):
    count_tm, count_height = mesh.shape["tm"], mesh.shape["height"]
    tm_parts, height_parts = factors(count_tm // 2), factors(count_height // 4)
    tm_names = tuple(f"tm_{n}" for n in range(len(tm_parts)))
    height_names = tuple(f"z_{n}" for n in range(len(height_parts)))
    axes = {
        "tm": tm_names + ("tm_lo",),
        "height": height_names + ("y", "core"),
        "rest": tm_names + height_names,
    }
    fine = Mesh(
        mesh.devices.reshape(tm_parts + [2] + height_parts + [2, 2]), axes["tm"] + axes["height"]
    )
    tm, height = axes["tm"], axes["height"]

    def body(*args):
        return local(axes, *args)

    return jax.shard_map(
        body,
        mesh=fine,
        in_specs=(P(tm, None, height, None), P(), P(), P(), P(), P(tm, height, None, None)),
        out_specs=(
            P(tm, height, None, None),
            P(),
            P(),
            P(),
            P(),
            P(tm, None, height, None),
        ),
        check_vma=False,
    )
```

```python
import functools
import math

import jax
import jax.numpy as jnp
import numpy as np
from jax import lax
from jax.experimental import pallas as pl
from jax.experimental.pallas import tpu as pltpu
from jax.sharding import Mesh, PartitionSpec as P


BF16, F32 = jnp.bfloat16, jnp.float32
HAAR = np.kron(np.array([[1.0, 1.0], [1.0, -1.0]]), np.array([[1.0, 1.0], [1.0, -1.0]])) * 0.5
VMEM = pl.BlockSpec(memory_space=pltpu.VMEM)
HBM = pl.BlockSpec(memory_space=pltpu.HBM)
NN = (((1,), (0,)), ((), ()))
NT = (((1,), (1,)), ((), ()))
COLORS, CH, WIDTH = 3, 48, 128
TAPS = 3 * CH


def mm(a, b, dims=NN):
    return lax.dot_general(a, b, dims, preferred_element_type=F32)


def split(x):
    high = x.astype(BF16)
    return high, (x - high.astype(F32)).astype(BF16)


def position():
    return lax.axis_index("core"), 2 * lax.axis_index("tm_lo") + lax.axis_index("y")


def call(body, outs, ins, scratch=(), flops=0, grant=24, **more):
    shapes = [jax.ShapeDtypeStruct(shape, dtype) for shape, dtype in outs]
    return pl.pallas_call(
        body,
        out_shape=shapes,
        scratch_shapes=list(scratch),
        cost_estimate=pl.CostEstimate(flops=flops, bytes_accessed=1 << 20, transcendentals=0),
        compiler_params=pltpu.CompilerParams(vmem_limit_bytes=grant << 20),
        in_specs=ins,
        **{"out_specs": [VMEM] * len(outs), **more},
    )


def column_table(quarter):
    table = np.zeros((8 * quarter, 4, 2, quarter), np.float32)
    for parity in range(2):
        for pair in range(quarter):
            for v in range(4):
                table[8 * pair + 4 * parity + v, :, parity, pair] = HAAR[:, v]
    return table.reshape(8 * quarter, 8 * quarter)


def row_table(frames, rows):
    table = np.zeros((frames, rows, COLORS, 4, 4, 4, frames, COLORS, rows, 4), np.float32)
    for f in range(frames):
        for r in range(rows):
            for k in range(COLORS):
                for j in range(4):
                    table[f, r, k, :, j, j, f, k, r, :] = HAAR
    return table.reshape(frames * rows * CH, 4 * frames * COLORS * rows * 4)


def choose_table(frames, rows):
    table = np.zeros((2, 2, frames + 2, COLORS, 4, frames + 2, COLORS, 4 * rows), np.float32)
    for core in range(2):
        for way in range(2):
            at = 4 * rows - 4 if core == way else 0
            for f in range(frames + 2):
                for k in range(COLORS):
                    for u in range(4):
                        table[core, way, f, k, u, f, k, at + u] = 1.0
    return table.reshape(2, 2 * (frames + 2) * COLORS * 4, (frames + 2) * COLORS * 4 * rows)


def shifts(pair):
    lane = lax.broadcasted_iota(jnp.int32, (1, pair), 1)

    def left(value):
        return jnp.where(lane == pair - 1, 0.0, pltpu.roll(value, pair - 1, 1))

    def right(value):
        return jnp.where(lane == 0, 0.0, pltpu.roll(value, 1, 1))

    return left, right


def analyse(groups, table, rows_tables, x, places, pair):
    left, right = shifts(pair)
    low_half = lax.broadcasted_iota(jnp.int32, (1, pair), 1) < pair // 2
    size, width = groups[0].shape
    stacked = [group[:, half * width // 2 : (half + 1) * width // 2] for group in groups for half in range(2)]
    columns = mm(jnp.concatenate(stacked, axis=0), table[...])
    for n, (rows_table, where) in enumerate(zip(rows_tables, places)):
        blocks = []
        for j in range(4):
            one = columns[2 * n * size : (2 * n + 1) * size, pair * j : pair * (j + 1)]
            two = columns[(2 * n + 1) * size : (2 * n + 2) * size, pair * j : pair * (j + 1)]
            even = jnp.where(low_half, one, pltpu.roll(two, pair // 2, 1))
            odd = jnp.where(low_half, pltpu.roll(one, pair // 2, 1), two)
            blocks.append(jnp.concatenate([even, odd], axis=1))
        high, low = split(jnp.concatenate(blocks, axis=0))
        cells = (mm(rows_table[...], high) + mm(rows_table[...], low)).astype(BF16)
        even, odd = cells[:, :pair].astype(F32), cells[:, pair:].astype(F32)
        taps = (
            jnp.concatenate([right(odd), even], axis=1).astype(BF16),
            cells,
            jnp.concatenate([odd, left(even)], axis=1).astype(BF16),
        )
        for block, (f, r) in enumerate(where):
            for d in range(3):
                x[f, r, CH * d : CH * (d + 1)] = taps[d][CH * block : CH * (block + 1)]


def synthesise(groups, table, rows_tables, pair):
    low_half = lax.broadcasted_iota(jnp.int32, (1, pair), 1) < pair // 2
    stacked = []
    for cells, rows_table in zip(groups, rows_tables):
        turned = mm(rows_table[...], cells.astype(BF16), (((0,), (0,)), ((), ())))
        size = turned.shape[0] // 4
        ones, twos = [], []
        for j in range(4):
            even = turned[size * j : size * (j + 1), :pair]
            odd = turned[size * j : size * (j + 1), pair:]
            ones.append(jnp.where(low_half, even, pltpu.roll(odd, pair // 2, 1)))
            twos.append(jnp.where(low_half, pltpu.roll(even, pair // 2, 1), odd))
        stacked += [jnp.concatenate(ones, axis=1), jnp.concatenate(twos, axis=1)]
    pixels = mm(jnp.concatenate(stacked, axis=0).astype(BF16), table[...], NT)
    size = stacked[0].shape[0]
    return [
        jnp.concatenate(
            [pixels[2 * n * size : (2 * n + 1) * size], pixels[(2 * n + 1) * size : (2 * n + 2) * size]],
            axis=1,
        )
        for n in range(len(groups))
    ]


def first_kernel(dims, count, *refs):
    frames, rows, pair = dims
    sources, targets = refs[:count], refs[count : 2 * count - 1]
    inside, outside, backward, x, dact, raw, sems = refs[2 * count - 1 :]
    copies = [
        pltpu.make_async_copy(source, target, sems.at[n])
        for n, (source, target) in enumerate(zip(sources, (raw, *targets)))
    ]
    for copy in copies:
        copy.start()
    own, table, rows_own, down_weight, cotangent = targets[:5]
    copies[0].wait()
    for a in range(3):
        for b in range(3):
            for d in range(3):
                at = CH * (3 * b + a)
                backward[at : at + CH, WIDTH * d : WIDTH * (d + 1)] = raw[9 * a + 3 * b + d]
        taps = raw[9 * a : 9 * a + 9].reshape(3 * TAPS, WIDTH).astype(F32)
        at = slice(WIDTH * a, WIDTH * (a + 1))
        inside[0, at] = taps[TAPS:].T.astype(BF16)
        inside[1, at] = taps[: 2 * TAPS].T.astype(BF16)
        outside[0, at] = taps[:TAPS].T.astype(BF16)
        outside[1, at] = taps[2 * TAPS :].T.astype(BF16)
    for copy in copies[1:]:
        copy.wait()
    where = [(f, r) for f in range(frames) for r in range(rows)]
    analyse([own[...]], table, [rows_own], x, [where], pair)
    for f in range(frames):
        dact[f] = mm(down_weight[...], cotangent[f, 0], NT)


def pack_kernel(own, earlier, chosen, inner, outer):
    core, _ = position()
    both = mm(chosen[core], jnp.concatenate([earlier[...], own[...]], axis=0)).astype(BF16)
    size = inner.shape[0]
    inner[...] = both[:size]
    outer[...] = both[size:]


def taps_of(frame, frames):
    return [(f, frame - f) for f in range(frames) if 0 <= frame - f < 3]


def convolve(total, weights, values, frame, frames):
    used = taps_of(frame, frames)
    first = min(a for _, a in used)
    last = max(a for _, a in used)
    part = mm(weights[WIDTH * first : WIDTH * (last + 1)], values)
    for f, a in used:
        here = part[WIDTH * (a - first) : WIDTH * (a - first + 1)]
        total[f] = here if total[f] is None else total[f] + here


def early_kernel(dims, earlier, table, rows_own, inside, conv_bias, x_own, x, pre):
    frames, rows, pair = dims
    where = [(f, r) for f in range(2) for r in range(rows)]
    analyse([earlier[...]], table, [rows_own], x, [where], pair)
    bias = jnp.broadcast_to(conv_bias[...], (WIDTH, WIDTH)).T
    bias = jnp.concatenate([bias] * (2 * pair // WIDTH), axis=1)
    for r in range(rows):
        total = [bias] * frames
        for frame in range(frames + 2):
            values = (x[frame] if frame < 2 else x_own[frame - 2]).reshape(rows * TAPS, 2 * pair)
            convolve(total, inside[r], values, frame, frames)
        for f in range(frames):
            pre[f, r] = total[f]


def main_kernel(
    dims,
    inner,
    outer,
    table,
    rows_halo,
    x_early,
    x_own,
    pre_own,
    dact,
    outside,
    cotangent,
    keep,
    give,
    acts,
    slopes,
    x,
    packed,
):
    frames, rows, pair = dims
    core, plane = position()
    inner_row = jnp.where(core == 0, rows + 1, 0)
    outer_row = jnp.where(core == 0, 0, rows + 1)
    for frame in range(frames + 2):
        x[frame, 1 : rows + 1] = x_early[frame] if frame < 2 else x_own[frame - 2]
    places = [
        [(f, inner_row) for f in range(frames + 2)],
        [(f, outer_row) for f in range(frames + 2)],
    ]
    analyse([inner[...], outer[...]], table, [rows_halo, rows_halo], x, places, pair)

    for r in range(rows):
        total = [pre_own[f, r] for f in range(frames)]
        edge = 0 if r == 0 else rows + 1
        for frame in range(frames + 2):
            convolve(total, outside[r], x[frame, edge], frame, frames)
        for f in range(frames):
            pre = total[f]
            sig = jax.nn.sigmoid(pre)
            act = pre * sig
            at = 2 * WIDTH * r
            acts[f, at : at + WIDTH] = act[:, :pair].astype(BF16)
            acts[f, at + WIDTH : at + 2 * WIDTH] = act[:, pair:].astype(BF16)
            here = jnp.concatenate(
                [dact[f, at : at + WIDTH], dact[f, at + WIDTH : at + 2 * WIDTH]], axis=1
            )
            slope = here * sig * (1.0 + pre * (1.0 - sig))
            slopes[WIDTH * f : WIDTH * (f + 1), 2 * pair * r : 2 * pair * (r + 1)] = slope.astype(BF16)

    conv_total = [None] * 3
    for frame in range(frames + 2):
        used = taps_of(frame, frames)
        first, last = used[0][0], used[-1][0]
        values = jnp.concatenate(
            [x[frame, r : r + 3].reshape(3 * TAPS, 2 * pair) for r in range(rows)], axis=1
        )
        part = mm(values, slopes[WIDTH * first : WIDTH * (last + 1)], NT)
        for f, a in used:
            here = part[:, WIDTH * (f - first) : WIDTH * (f - first + 1)]
            conv_total[a] = here if conv_total[a] is None else conv_total[a] + here
    down_total = None
    cot_total = None
    ones = jnp.ones((8, 2 * pair * rows), BF16)
    for f in range(frames):
        part = mm(acts[f], cotangent[f, 0])
        down_total = part if down_total is None else down_total + part
        part = mm(ones[:, :pair], cotangent[f, 0])
        cot_total = part if cot_total is None else cot_total + part
    slope_total = mm(ones, slopes[...], NT)
    slope_total = sum(slope_total[0:1, WIDTH * f : WIDTH * (f + 1)] for f in range(frames))

    chunk = keep.shape[1]
    half = 27 * CH // 2
    conv = jnp.concatenate(conv_total, axis=0)
    sums = [slope_total, cot_total[0:1, :WIDTH], cot_total[0:1, WIDTH:]]
    highs = [value.astype(BF16).astype(F32) for value in sums]
    lows = [value - high for value, high in zip(sums, highs)]
    sums = jnp.concatenate(highs + lows + [jnp.zeros((2, WIDTH), F32)], axis=0)
    down_rows = 2 * rows * WIDTH
    for h in range(2):
        packed[h, :half] = conv[half * h : half * (h + 1)]
        packed[h, half : half + down_rows] = down_total[:, WIDTH * h : WIDTH * (h + 1)]
        packed[h, half + down_rows : half + down_rows + 8] = sums if h == 0 else jnp.zeros_like(sums)
        rest = 4 * chunk - half - down_rows - 8
        if rest:
            packed[h, half + down_rows + 8 :] = jnp.zeros((rest, WIDTH), F32)
    for m in range(4):
        at = pl.multiple_of(jnp.bitwise_xor(plane, m) * chunk, 8)
        keep[m] = packed[core, pl.ds(at, chunk)]
        give[m] = packed[1 - core, pl.ds(at, chunk)].astype(BF16)


def shifted_slope(slopes, f, r, pair):
    left, right = shifts(pair)
    slope = slopes[WIDTH * f : WIDTH * (f + 1), 2 * pair * r : 2 * pair * (r + 1)]
    even, odd = slope[:, :pair].astype(F32), slope[:, pair:].astype(F32)
    return jnp.concatenate(
        [
            jnp.concatenate([odd, left(even)], axis=1).astype(BF16),
            slope,
            jnp.concatenate([right(odd), even], axis=1).astype(BF16),
        ],
        axis=0,
    )


def spread_slope(total, slopes, backward, frames, reach, pair):
    for f in range(frames):
        for r in sorted({r for r, _, _ in reach}):
            taps = [(b, row) for here, b, row in reach if here == r]
            first, last = min(taps)[0], max(taps)[0]
            part = mm(backward[TAPS * first : TAPS * (last + 1)], shifted_slope(slopes, f, r, pair))
            for b, row in taps:
                for a in range(3):
                    at = TAPS * (b - first) + CH * a
                    here = part[at : at + CH]
                    key = (f + a, row)
                    total[key] = here if key not in total else total[key] + here


def edge_kernel(dims, slopes, backward, table, rows_halo, send_inner, send_outer):
    frames, rows, pair = dims
    core, _ = position()
    total = {}
    spread_slope(total, slopes, backward, frames, [(0, 0, 0), (rows - 1, 2, 1)], pair)
    groups = [
        jnp.concatenate([total[frame, row] for frame in range(frames + 2)], axis=0) for row in range(2)
    ]
    above, below = synthesise(groups, table, [rows_halo, rows_halo], pair)
    send_inner[...] = jnp.where(core == 0, below, above).astype(BF16)
    send_outer[...] = jnp.where(core == 0, above, below).astype(BF16)


def late_kernel(
    dims,
    acts,
    slopes,
    backward,
    down_weight,
    down_bias,
    table,
    rows_own,
    features,
    pixels_own,
    pixels_early,
):
    frames, rows, pair = dims
    total = {}
    reach = [(r, b, r + b - 1) for r in range(rows) for b in range(3) if 0 <= r + b - 1 < rows]
    spread_slope(total, slopes, backward, frames, reach, pair)
    groups = [
        jnp.concatenate([total[first + f, r] for f in range(frames) for r in range(rows)], axis=0)
        for first in (0, 2)
    ]
    pixels_early[...], pixels_own[...] = synthesise(groups, table, [rows_own, rows_own], pair)
    for f in range(frames):
        turned = jnp.concatenate(
            [acts[f, WIDTH * n : WIDTH * (n + 1)].astype(F32).T.astype(BF16) for n in range(4)], axis=1
        )
        features[f, 0] = (mm(turned, down_weight[...]) + down_bias[...]).astype(BF16)


def finish_kernel(scale, other, *refs):
    pieces, (conv, conv_bias, down, down_bias, flat, sums, sems) = refs[:4], refs[-7:]
    if other:
        pieces = [refs[0].at[m] for m in range(4)]
    core, plane = position()
    which = 1 - core if other else core
    chunk = pieces[0].shape[0]
    for m in range(4):
        at = pl.multiple_of(jnp.bitwise_xor(plane, m) * chunk, 8)
        flat[pl.ds(at, chunk)] = pieces[m][...].astype(F32) * scale
    half, down_rows = conv.shape[0] // 2, down.shape[0]
    at = pl.multiple_of(half * which, 8)
    copies = [
        pltpu.make_async_copy(flat.at[pl.ds(0, half)], conv.at[pl.ds(at, half)], sems.at[0]),
        pltpu.make_async_copy(
            flat.at[pl.ds(half, down_rows)],
            down.at[:, pl.ds(pl.multiple_of(WIDTH * which, WIDTH), WIDTH)],
            sems.at[1],
        ),
    ]
    for copy in copies:
        copy.start()

    @pl.when(which == 0)
    def _():
        at = half + down_rows
        total = flat[at : at + 8]
        total = total[0:3] + total[3:6]
        for n in range(3):
            sums[n] = total[n : n + 1]
        targets = [conv_bias, down_bias.at[:, pl.ds(0, WIDTH)], down_bias.at[:, pl.ds(WIDTH, WIDTH)]]
        small = [
            pltpu.make_async_copy(sums.at[n], target, sems.at[2 + n]) for n, target in enumerate(targets)
        ]
        for copy in small:
            copy.start()
        for copy in small:
            copy.wait()

    for copy in copies:
        copy.wait()


def local(axes, pixels, conv_weight, conv_bias, down_weight, down_bias, cotangent):
    times, heights = axes["tm"], axes["height"]
    frames, colors, pixel_rows, pixel_columns = pixels.shape
    rows, columns = pixel_rows // 4, pixel_columns // 4
    assert frames == 2 and rows == 2 and colors == COLORS
    assert conv_weight.shape[3:] == (CH, WIDTH)
    pair = columns // 2
    width2 = down_weight.shape[3]
    core = lax.axis_index("core")
    count_tm, count_height = lax.axis_size(times), lax.axis_size(heights)
    dims = (frames, rows, pair)

    def along_tm(value, step):
        pairs = [(i, i + step) for i in range(count_tm) if 0 <= i + step < count_tm]
        return lax.ppermute(value, times, pairs)

    def swap_inner(value):
        return lax.ppermute(value, "core", [(0, 1), (1, 0)])

    def swap_outer(value):
        pairs = [(i, i + 1) for i in range(1, count_height - 1, 2)]
        return lax.ppermute(value, heights, pairs + [(j, i) for i, j in pairs])

    def exchange(value, axes, mask):
        size = lax.axis_size(axes)
        return lax.ppermute(value, axes, [(i, i ^ mask) for i in range(size)])

    own = pixels.reshape(frames * colors * pixel_rows, pixel_columns)
    earlier = along_tm(own, 1)
    flat_halo = ((frames + 2) * colors * 4, pixel_columns)
    frame_shape = (2 * colors, pixel_rows, pixel_columns)
    sources = [
        conv_weight.reshape(27, CH, WIDTH),
        own,
        jnp.asarray(column_table(pair // 2), BF16),
        jnp.asarray(row_table(frames, rows), BF16),
        down_weight.reshape(4 * WIDTH, width2),
        cotangent,
        jnp.asarray(row_table(frames + 2, 1), BF16),
        jnp.asarray(choose_table(frames, rows), BF16),
        conv_bias.reshape(1, WIDTH),
        down_bias.reshape(1, width2),
    ]
    outs = call(
        functools.partial(first_kernel, dims, len(sources)),
        [(source.shape, source.dtype) for source in sources[1:]]
        + [
            ((2, 3 * WIDTH, 2 * TAPS), BF16),
            ((2, 3 * WIDTH, TAPS), BF16),
            ((9 * CH, 3 * WIDTH), BF16),
            ((frames, rows, TAPS, columns), BF16),
            ((frames, 4 * WIDTH, pair), F32),
        ],
        [HBM] * len(sources),
        [pltpu.VMEM((27, CH, WIDTH), BF16), pltpu.SemaphoreType.DMA((len(sources),))],
        flops=10**9,
    )(*(pltpu.with_memory_space_constraint(source, pltpu.HBM) for source in sources))
    own, table, rows_own, down_flat, cot, rows_halo, chosen, bias, bias2 = outs[:9]
    inside, outside, backward, x_own, dact = outs[9:]
    send_inner, send_outer = call(pack_kernel, [(flat_halo, BF16), (flat_halo, BF16)], [VMEM] * 3)(own, earlier, chosen)
    inner = swap_inner(send_inner)
    outer = swap_outer(send_outer)

    x_early, pre_own = call(
        functools.partial(early_kernel, dims),
        [((2, rows, TAPS, columns), BF16), ((frames, rows, WIDTH, columns), F32)],
        [VMEM] * 6,
        flops=10**9,
    )(earlier, table, rows_own, inside, bias, x_own)

    data_rows = 27 * CH // 2 + 4 * WIDTH + 8
    chunk = -(-data_rows // 32) * 8
    keep, give, acts, slopes = call(
        functools.partial(main_kernel, dims),
        [
            ((4, chunk, WIDTH), F32),
            ((4, chunk, WIDTH), BF16),
            ((frames, 4 * WIDTH, pair), BF16),
            ((frames * WIDTH, rows * columns), BF16),
        ],
        [VMEM] * 10,
        [
            pltpu.VMEM((frames + 2, rows + 2, TAPS, columns), BF16),
            pltpu.VMEM((2, 4 * chunk, WIDTH), F32),
        ],
        flops=10**9,
    )(inner, outer, table, rows_halo, x_early, x_own, pre_own, dact, outside, cot)

    send_inner, send_outer = call(
        functools.partial(edge_kernel, dims), [(flat_halo, BF16), (flat_halo, BF16)], [VMEM] * 4, flops=10**9
    )(slopes, backward, table, rows_halo)
    features, pixels_own, pixels_early = call(
        functools.partial(late_kernel, dims),
        [((frames, rows // 2, pair, width2), BF16), (own.shape, F32), (own.shape, F32)],
        [VMEM] * 7,
        flops=10**9,
    )(acts, slopes, backward, down_flat, bias2, table, rows_own)

    total = keep + swap_inner(give).astype(F32)
    planes = ("tm_lo", "y")
    parts = [exchange(total[m].astype(BF16), planes, m) for m in (1, 2, 3)]
    mine = total[0] + sum(part.astype(F32) for part in parts)
    for axis in axes["rest"]:
        sent = mine.astype(BF16)
        parts = [exchange(sent, axis, m) for m in range(1, lax.axis_size(axis))]
        mine = mine + sum(part.astype(F32) for part in parts)
    mine = mine.astype(BF16)
    pieces = [mine] + [exchange(mine, planes, m) for m in (1, 2, 3)]
    theirs = swap_inner(jnp.stack(pieces))
    count = frames * count_tm * rows * count_height * columns
    scale = 1.0 / math.sqrt(count)
    outs = [
        ((27 * CH, WIDTH), F32),
        ((1, WIDTH), F32),
        ((4 * WIDTH, width2), F32),
        ((1, width2), F32),
    ]
    scratch = [
        pltpu.VMEM((4 * chunk, WIDTH), F32),
        pltpu.VMEM((3, 1, WIDTH), F32),
        pltpu.SemaphoreType.DMA((5,)),
    ]
    grads = call(
        functools.partial(finish_kernel, scale, False), outs, [VMEM] * 4, scratch, out_specs=[HBM] * 4
    )(*pieces)
    grad_conv, grad_conv_bias, grad_down, grad_down_bias = call(
        functools.partial(finish_kernel, scale, True),
        outs,
        [VMEM] + [HBM] * 4,
        scratch,
        out_specs=[HBM] * 4,
        input_output_aliases={1: 0, 2: 1, 3: 2, 4: 3},
    )(theirs, *grads)

    from_inner = swap_inner(send_inner).reshape((frames + 2) * colors, 4, pixel_columns)
    from_outer = swap_outer(send_outer).reshape((frames + 2) * colors, 4, pixel_columns)
    above = jnp.where(core == 0, from_outer, from_inner).astype(F32)
    below = jnp.where(core == 0, from_inner, from_outer).astype(F32)
    halo = jnp.concatenate([above, below], axis=1)
    early = pixels_early.reshape(frame_shape) + halo[: 2 * colors]
    late = pixels_own.reshape(frame_shape) + halo[2 * colors :]
    following = along_tm(early.astype(BF16), -1)
    grad_pixels = late + following.astype(F32)
    return (
        features,
        grad_conv.reshape(conv_weight.shape),
        grad_conv_bias.reshape(WIDTH),
        grad_down.reshape(down_weight.shape),
        grad_down_bias.reshape(width2),
        grad_pixels.reshape(pixels.shape),
    )


def factors(size):
    parts = []
    while size > 1:
        part = 4 if size % 4 == 0 else 2
        assert size % part == 0
        parts.append(part)
        size //= part
    return parts


def solution(mesh):
    count_tm, count_height = mesh.shape["tm"], mesh.shape["height"]
    tm_parts, height_parts = factors(count_tm // 2), factors(count_height // 4)
    tm_names = tuple(f"tm_{n}" for n in range(len(tm_parts)))
    height_names = tuple(f"z_{n}" for n in range(len(height_parts)))
    axes = {
        "tm": tm_names + ("tm_lo",),
        "height": height_names + ("y", "core"),
        "rest": tm_names + height_names,
    }
    fine = Mesh(
        mesh.devices.reshape(tm_parts + [2] + height_parts + [2, 2]), axes["tm"] + axes["height"]
    )
    tm, height = axes["tm"], axes["height"]

    def body(*args):
        return local(axes, *args)

    return jax.shard_map(
        body,
        mesh=fine,
        in_specs=(P(tm, None, height, None), P(), P(), P(), P(), P(tm, height, None, None)),
        out_specs=(
            P(tm, height, None, None),
            P(),
            P(),
            P(),
            P(),
            P(tm, None, height, None),
        ),
        check_vma=False,
    )
```

```python
import functools
import math

import jax
import jax.numpy as jnp
import numpy as np
from jax import lax
from jax.experimental import pallas as pl
from jax.experimental.pallas import tpu as pltpu
from jax.sharding import Mesh, PartitionSpec as P


BF16, F32 = jnp.bfloat16, jnp.float32
HAAR = np.kron(np.array([[1.0, 1.0], [1.0, -1.0]]), np.array([[1.0, 1.0], [1.0, -1.0]])) * 0.5
VMEM = pl.BlockSpec(memory_space=pltpu.VMEM)
HBM = pl.BlockSpec(memory_space=pltpu.HBM)
NN = (((1,), (0,)), ((), ()))
NT = (((1,), (1,)), ((), ()))
COLORS, CH, WIDTH = 3, 48, 128
TAPS = 3 * CH


def mm(a, b, dims=NN):
    return lax.dot_general(a, b, dims, preferred_element_type=F32)


def split(x):
    high = x.astype(BF16)
    return high, (x - high.astype(F32)).astype(BF16)


def position():
    return lax.axis_index("core"), 2 * lax.axis_index("tm_lo") + lax.axis_index("y")


def call(body, outs, ins, scratch=(), flops=0, grant=24, **more):
    shapes = [jax.ShapeDtypeStruct(shape, dtype) for shape, dtype in outs]
    return pl.pallas_call(
        body,
        out_shape=shapes,
        scratch_shapes=list(scratch),
        cost_estimate=pl.CostEstimate(flops=flops, bytes_accessed=1 << 20, transcendentals=0),
        compiler_params=pltpu.CompilerParams(vmem_limit_bytes=grant << 20),
        in_specs=ins,
        **{"out_specs": [VMEM] * len(outs), **more},
    )


def column_table(quarter):
    table = np.zeros((8 * quarter, 4, 2, quarter), np.float32)
    for parity in range(2):
        for pair in range(quarter):
            for v in range(4):
                table[8 * pair + 4 * parity + v, :, parity, pair] = HAAR[:, v]
    return table.reshape(8 * quarter, 8 * quarter)


def row_table(frames, rows):
    table = np.zeros((frames, rows, COLORS, 4, 4, 4, frames, COLORS, rows, 4), np.float32)
    for f in range(frames):
        for r in range(rows):
            for k in range(COLORS):
                for j in range(4):
                    table[f, r, k, :, j, j, f, k, r, :] = HAAR
    return table.reshape(frames * rows * CH, 4 * frames * COLORS * rows * 4)


def choose_table(frames, rows):
    table = np.zeros((2, 2, frames + 2, COLORS, 4, frames + 2, COLORS, 4 * rows), np.float32)
    for core in range(2):
        for way in range(2):
            at = 4 * rows - 4 if core == way else 0
            for f in range(frames + 2):
                for k in range(COLORS):
                    for u in range(4):
                        table[core, way, f, k, u, f, k, at + u] = 1.0
    return table.reshape(2, 2 * (frames + 2) * COLORS * 4, (frames + 2) * COLORS * 4 * rows)


def shifts(pair):
    lane = lax.broadcasted_iota(jnp.int32, (1, pair), 1)

    def left(value):
        return jnp.where(lane == pair - 1, 0.0, pltpu.roll(value, pair - 1, 1))

    def right(value):
        return jnp.where(lane == 0, 0.0, pltpu.roll(value, 1, 1))

    return left, right


def analyse(groups, table, rows_tables, x, places, pair):
    left, right = shifts(pair)
    low_half = lax.broadcasted_iota(jnp.int32, (1, pair), 1) < pair // 2
    size, width = groups[0].shape
    stacked = [group[:, half * width // 2 : (half + 1) * width // 2] for group in groups for half in range(2)]
    columns = mm(jnp.concatenate(stacked, axis=0), table[...])
    for n, (rows_table, where) in enumerate(zip(rows_tables, places)):
        blocks = []
        for j in range(4):
            one = columns[2 * n * size : (2 * n + 1) * size, pair * j : pair * (j + 1)]
            two = columns[(2 * n + 1) * size : (2 * n + 2) * size, pair * j : pair * (j + 1)]
            even = jnp.where(low_half, one, pltpu.roll(two, pair // 2, 1))
            odd = jnp.where(low_half, pltpu.roll(one, pair // 2, 1), two)
            blocks.append(jnp.concatenate([even, odd], axis=1))
        high, low = split(jnp.concatenate(blocks, axis=0))
        cells = (mm(rows_table[...], high) + mm(rows_table[...], low)).astype(BF16)
        even, odd = cells[:, :pair].astype(F32), cells[:, pair:].astype(F32)
        taps = (
            jnp.concatenate([right(odd), even], axis=1).astype(BF16),
            cells,
            jnp.concatenate([odd, left(even)], axis=1).astype(BF16),
        )
        for block, (f, r) in enumerate(where):
            for d in range(3):
                x[f, r, CH * d : CH * (d + 1)] = taps[d][CH * block : CH * (block + 1)]


def synthesise(groups, table, rows_tables, pair):
    low_half = lax.broadcasted_iota(jnp.int32, (1, pair), 1) < pair // 2
    stacked = []
    for cells, rows_table in zip(groups, rows_tables):
        turned = mm(rows_table[...], cells.astype(BF16), (((0,), (0,)), ((), ())))
        size = turned.shape[0] // 4
        ones, twos = [], []
        for j in range(4):
            even = turned[size * j : size * (j + 1), :pair]
            odd = turned[size * j : size * (j + 1), pair:]
            ones.append(jnp.where(low_half, even, pltpu.roll(odd, pair // 2, 1)))
            twos.append(jnp.where(low_half, pltpu.roll(even, pair // 2, 1), odd))
        stacked += [jnp.concatenate(ones, axis=1), jnp.concatenate(twos, axis=1)]
    pixels = mm(jnp.concatenate(stacked, axis=0).astype(BF16), table[...], NT)
    size = stacked[0].shape[0]
    return [
        jnp.concatenate(
            [pixels[2 * n * size : (2 * n + 1) * size], pixels[(2 * n + 1) * size : (2 * n + 2) * size]],
            axis=1,
        )
        for n in range(len(groups))
    ]


def first_kernel(dims, count, *refs):
    frames, rows, pair = dims
    sources, targets = refs[:count], refs[count : 2 * count - 1]
    inside, outside, backward, x, dact, raw, sems = refs[2 * count - 1 :]
    copies = [
        pltpu.make_async_copy(source, target, sems.at[n])
        for n, (source, target) in enumerate(zip(sources, (raw, *targets)))
    ]
    for copy in copies:
        copy.start()
    own, table, rows_own, down_weight, cotangent = targets[:5]
    copies[0].wait()
    for a in range(3):
        for b in range(3):
            for d in range(3):
                at = CH * (3 * b + a)
                backward[at : at + CH, WIDTH * d : WIDTH * (d + 1)] = raw[9 * a + 3 * b + d]
        taps = raw[9 * a : 9 * a + 9].reshape(3 * TAPS, WIDTH).astype(F32)
        at = slice(WIDTH * a, WIDTH * (a + 1))
        inside[0, at] = taps[TAPS:].T.astype(BF16)
        inside[1, at] = taps[: 2 * TAPS].T.astype(BF16)
        outside[0, at] = taps[:TAPS].T.astype(BF16)
        outside[1, at] = taps[2 * TAPS :].T.astype(BF16)
    for copy in copies[1:]:
        copy.wait()
    where = [(f, r) for f in range(frames) for r in range(rows)]
    analyse([own[...]], table, [rows_own], x, [where], pair)
    for f in range(frames):
        dact[f] = mm(down_weight[...], cotangent[f, 0], NT)


def pack_kernel(times, own, came, chosen, inner, outer, earlier):
    core, _ = position()
    used = jnp.where(lax.axis_index(times) == 0, 0.0, 1.0)
    earlier[...] = (came[...].astype(F32) * used).astype(BF16)
    both = mm(chosen[core], jnp.concatenate([earlier[...], own[...]], axis=0)).astype(BF16)
    size = inner.shape[0]
    inner[...] = both[:size]
    outer[...] = both[size:]


def taps_of(frame, frames):
    return [(f, frame - f) for f in range(frames) if 0 <= frame - f < 3]


def convolve(total, weights, values, frame, frames):
    used = taps_of(frame, frames)
    first = min(a for _, a in used)
    last = max(a for _, a in used)
    part = mm(weights[WIDTH * first : WIDTH * (last + 1)], values)
    for f, a in used:
        here = part[WIDTH * (a - first) : WIDTH * (a - first + 1)]
        total[f] = here if total[f] is None else total[f] + here


def early_kernel(dims, earlier, table, rows_own, inside, conv_bias, x_own, x, pre):
    frames, rows, pair = dims
    where = [(f, r) for f in range(2) for r in range(rows)]
    analyse([earlier[...]], table, [rows_own], x, [where], pair)
    bias = jnp.broadcast_to(conv_bias[...], (WIDTH, WIDTH)).T
    bias = jnp.concatenate([bias] * (2 * pair // WIDTH), axis=1)
    for r in range(rows):
        total = [bias] * frames
        for frame in range(frames + 2):
            values = (x[frame] if frame < 2 else x_own[frame - 2]).reshape(rows * TAPS, 2 * pair)
            convolve(total, inside[r], values, frame, frames)
        for f in range(frames):
            pre[f, r] = total[f]


def one_row(dims, r, halo, table, rows_halo, x_early, x_own, pre_own, dact, outside, cotangent, acts, slopes, x):
    frames, rows, pair = dims
    for frame in range(frames + 2):
        here = x_early[frame] if frame < 2 else x_own[frame - 2]
        x[frame, pl.ds(1 - r, rows)] = here
    analyse([halo], table, [rows_halo], x, [[(f, 2 * r) for f in range(frames + 2)]], pair)
    total = [pre_own[f, r] for f in range(frames)]
    for frame in range(frames + 2):
        convolve(total, outside[r], x[frame, 2 * r], frame, frames)
    down_total = None
    for f in range(frames):
        pre = total[f]
        sig = jax.nn.sigmoid(pre)
        act = pre * sig
        acts[f, :WIDTH] = act[:, :pair].astype(BF16)
        acts[f, WIDTH:] = act[:, pair:].astype(BF16)
        here = dact[f, pl.ds(pl.multiple_of(2 * WIDTH * r, 2 * WIDTH), 2 * WIDTH)]
        here = jnp.concatenate([here[:WIDTH], here[WIDTH:]], axis=1)
        slope = here * sig * (1.0 + pre * (1.0 - sig))
        slopes[WIDTH * f : WIDTH * (f + 1)] = slope.astype(BF16)
        part = mm(acts[f], cotangent[f, 0])
        down_total = part if down_total is None else down_total + part
    conv_total = [None] * 3
    for frame in range(frames + 2):
        used = taps_of(frame, frames)
        first, last = used[0][0], used[-1][0]
        values = x[frame].reshape(3 * TAPS, 2 * pair)
        part = mm(values, slopes[WIDTH * first : WIDTH * (last + 1)], NT)
        for f, a in used:
            here = part[:, WIDTH * (f - first) : WIDTH * (f - first + 1)]
            conv_total[a] = here if conv_total[a] is None else conv_total[a] + here
    slope_total = mm(jnp.ones((8, 2 * pair), BF16), slopes[...], NT)
    slope_total = sum(slope_total[:, WIDTH * f : WIDTH * (f + 1)] for f in range(frames))
    return jnp.concatenate(conv_total, axis=0), down_total, slope_total


def mid_kernel(dims, halo, *refs):
    table, rows_halo, x_early, x_own, pre_own, dact, outside, cotangent = refs[:8]
    acts, slopes, conv, down, total, x = refs[8:]
    core, _ = position()
    conv[...], down[...], total[...] = one_row(
        dims, 1 - core, halo[...], *refs[:8], acts, slopes, x
    )


def at_end(heights):
    height = lax.axis_index(heights)
    return (height == 0) | (height == lax.axis_size(heights) - 1)


def main_kernel(dims, heights, halo, *refs):
    frames, rows, pair = dims
    _, _, _, _, _, _, _, cotangent = refs[:8]
    acts_in, slopes_in, conv_in, down_in, total_in, mine, keep, give, acts, slopes, x, packed = refs[8:]
    core, plane = position()
    halo = (halo[...].astype(F32) * jnp.where(at_end(heights), 0.0, 1.0)).astype(BF16)
    acts[1 - core] = acts_in[...]
    slopes[1 - core] = slopes_in[...]
    conv, down, total = one_row(
        dims, core, halo, *refs[:8], acts.at[core], slopes.at[core], x
    )
    conv = conv + conv_in[...]
    slope_total = (total + total_in[...])[0:1]
    ones = jnp.ones((8, pair), BF16)
    cot_total = sum(mm(ones, cotangent[f, 0]) for f in range(frames))

    chunk = keep.shape[1]
    half = 27 * CH // 2
    sums = [slope_total, cot_total[0:1, :WIDTH], cot_total[0:1, WIDTH:]]
    highs = [value.astype(BF16).astype(F32) for value in sums]
    lows = [value - high for value, high in zip(sums, highs)]
    sums = jnp.concatenate(highs + lows + [jnp.zeros((2, WIDTH), F32)], axis=0)
    down_rows = 2 * rows * WIDTH
    for h in range(2):
        columns = slice(WIDTH * h, WIDTH * (h + 1))
        packed[h, :half] = conv[half * h : half * (h + 1)]
        for r, part in ((1 - core, down_in[:, columns]), (core, down[:, columns])):
            packed[h, pl.ds(pl.multiple_of(half + 2 * WIDTH * r, 8), 2 * WIDTH)] = part
        packed[h, half + down_rows : half + down_rows + 8] = sums if h == 0 else jnp.zeros_like(sums)
        rest = 4 * chunk - half - down_rows - 8
        if rest:
            packed[h, half + down_rows + 8 :] = jnp.zeros((rest, WIDTH), F32)
    for m in range(4):
        at = pl.multiple_of(jnp.bitwise_xor(plane, m) * chunk, 8)
        if m:
            keep[m - 1] = packed[core, pl.ds(at, chunk)]
        else:
            mine[...] = packed[core, pl.ds(at, chunk)]
        give[m] = packed[1 - core, pl.ds(at, chunk)].astype(BF16)


def shifted_slope(slopes, f, r, pair):
    left, right = shifts(pair)
    slope = slopes[r, WIDTH * f : WIDTH * (f + 1)]
    even, odd = slope[:, :pair].astype(F32), slope[:, pair:].astype(F32)
    return jnp.concatenate(
        [
            jnp.concatenate([odd, left(even)], axis=1).astype(BF16),
            slope,
            jnp.concatenate([right(odd), even], axis=1).astype(BF16),
        ],
        axis=0,
    )


def spread_slope(total, slopes, backward, frames, reach, pair):
    for f in range(frames):
        for r in sorted({r for r, _, _ in reach}):
            taps = [(b, row) for here, b, row in reach if here == r]
            first, last = min(taps)[0], max(taps)[0]
            part = mm(backward[TAPS * first : TAPS * (last + 1)], shifted_slope(slopes, f, r, pair))
            for b, row in taps:
                for a in range(3):
                    at = TAPS * (b - first) + CH * a
                    here = part[at : at + CH]
                    key = (f + a, row)
                    total[key] = here if key not in total else total[key] + here


def edge_kernel(dims, slopes, backward, table, rows_halo, send_inner, send_outer):
    frames, rows, pair = dims
    core, _ = position()
    total = {}
    spread_slope(total, slopes, backward, frames, [(0, 0, 0), (rows - 1, 2, 1)], pair)
    groups = [
        jnp.concatenate([total[frame, row] for frame in range(frames + 2)], axis=0) for row in range(2)
    ]
    above, below = synthesise(groups, table, [rows_halo, rows_halo], pair)
    send_inner[...] = jnp.where(core == 0, below, above).astype(BF16)
    send_outer[...] = jnp.where(core == 0, above, below).astype(BF16)


def late_kernel(
    dims,
    acts,
    slopes,
    backward,
    down_weight,
    down_bias,
    table,
    rows_own,
    features,
    pixels_own,
    pixels_early,
):
    frames, rows, pair = dims
    total = {}
    reach = [(r, b, r + b - 1) for r in range(rows) for b in range(3) if 0 <= r + b - 1 < rows]
    spread_slope(total, slopes, backward, frames, reach, pair)
    groups = [
        jnp.concatenate([total[first + f, r] for f in range(frames) for r in range(rows)], axis=0)
        for first in (0, 2)
    ]
    pixels_early[...], pixels_own[...] = synthesise(groups, table, [rows_own, rows_own], pair)
    for f in range(frames):
        blocks = [acts[u, f, WIDTH * v : WIDTH * (v + 1)] for u in range(2) for v in range(2)]
        turned = jnp.concatenate([block.astype(F32).T.astype(BF16) for block in blocks], axis=1)
        features[f, 0] = (mm(turned, down_weight[...]) + down_bias[...]).astype(BF16)


def finish_kernel(scale, other, *refs):
    pieces, (conv, conv_bias, down, down_bias, flat, sums, sems) = refs[:4], refs[-7:]
    if other:
        pieces = [refs[0].at[m] for m in range(4)]
    core, plane = position()
    which = 1 - core if other else core
    chunk = pieces[0].shape[0]
    for m in range(4):
        at = pl.multiple_of(jnp.bitwise_xor(plane, m) * chunk, 8)
        flat[pl.ds(at, chunk)] = pieces[m][...].astype(F32) * scale
    half, down_rows = conv.shape[0] // 2, down.shape[0]
    at = pl.multiple_of(half * which, 8)
    copies = [
        pltpu.make_async_copy(flat.at[pl.ds(0, half)], conv.at[pl.ds(at, half)], sems.at[0]),
        pltpu.make_async_copy(
            flat.at[pl.ds(half, down_rows)],
            down.at[:, pl.ds(pl.multiple_of(WIDTH * which, WIDTH), WIDTH)],
            sems.at[1],
        ),
    ]
    for copy in copies:
        copy.start()

    @pl.when(which == 0)
    def _():
        at = half + down_rows
        total = flat[at : at + 8]
        total = total[0:3] + total[3:6]
        for n in range(3):
            sums[n] = total[n : n + 1]
        targets = [conv_bias, down_bias.at[:, pl.ds(0, WIDTH)], down_bias.at[:, pl.ds(WIDTH, WIDTH)]]
        small = [
            pltpu.make_async_copy(sums.at[n], target, sems.at[2 + n]) for n, target in enumerate(targets)
        ]
        for copy in small:
            copy.start()
        for copy in small:
            copy.wait()

    for copy in copies:
        copy.wait()


def local(axes, pixels, conv_weight, conv_bias, down_weight, down_bias, cotangent):
    times, heights = axes["tm"], axes["height"]
    frames, colors, pixel_rows, pixel_columns = pixels.shape
    rows, columns = pixel_rows // 4, pixel_columns // 4
    assert frames == 2 and rows == 2 and colors == COLORS
    assert conv_weight.shape[3:] == (CH, WIDTH)
    pair = columns // 2
    width2 = down_weight.shape[3]
    core = lax.axis_index("core")
    count_tm, count_height = lax.axis_size(times), lax.axis_size(heights)
    dims = (frames, rows, pair)

    def along_tm(value, step):
        pairs = [(i, (i + step) % count_tm) for i in range(count_tm)]
        return lax.ppermute(value, times, pairs)

    def swap_inner(value):
        return lax.ppermute(value, "core", [(0, 1), (1, 0)])

    def swap_outer(value):
        inside = [(i, i + 1) for i in range(1, count_height - 1, 2)]
        inside += [(j, i) for i, j in inside]
        pairs = [(count_height * t + i, count_height * t + j) for t in range(count_tm) for i, j in inside]
        for end in (0, count_height - 1):
            pairs += [(count_height * t + end, count_height * (t ^ 1) + end) for t in range(count_tm)]
        return lax.ppermute(value, times + heights, pairs)

    def exchange(value, axes, mask):
        size = lax.axis_size(axes)
        return lax.ppermute(value, axes, [(i, i ^ mask) for i in range(size)])

    own = pixels.reshape(frames * colors * pixel_rows, pixel_columns)
    came = along_tm(own, 1)
    flat_halo = ((frames + 2) * colors * 4, pixel_columns)
    frame_shape = (2 * colors, pixel_rows, pixel_columns)
    sources = [
        conv_weight.reshape(27, CH, WIDTH),
        own,
        jnp.asarray(column_table(pair // 2), BF16),
        jnp.asarray(row_table(frames, rows), BF16),
        down_weight.reshape(4 * WIDTH, width2),
        cotangent,
        jnp.asarray(row_table(frames + 2, 1), BF16),
        jnp.asarray(choose_table(frames, rows), BF16),
        conv_bias.reshape(1, WIDTH),
        down_bias.reshape(1, width2),
    ]
    outs = call(
        functools.partial(first_kernel, dims, len(sources)),
        [(source.shape, source.dtype) for source in sources[1:]]
        + [
            ((2, 3 * WIDTH, 2 * TAPS), BF16),
            ((2, 3 * WIDTH, TAPS), BF16),
            ((9 * CH, 3 * WIDTH), BF16),
            ((frames, rows, TAPS, columns), BF16),
            ((frames, 4 * WIDTH, pair), F32),
        ],
        [HBM] * len(sources),
        [pltpu.VMEM((27, CH, WIDTH), BF16), pltpu.SemaphoreType.DMA((len(sources),))],
        flops=10**9,
    )(*(pltpu.with_memory_space_constraint(source, pltpu.HBM) for source in sources))
    own, table, rows_own, down_flat, cot, rows_halo, chosen, bias, bias2 = outs[:9]
    inside, outside, backward, x_own, dact = outs[9:]
    send_inner, send_outer, earlier = call(
        functools.partial(pack_kernel, times), [(flat_halo, BF16), (flat_halo, BF16), (own.shape, BF16)], [VMEM] * 3
    )(own, came, chosen)
    inner = swap_inner(send_inner)
    outer = swap_outer(send_outer)

    x_early, pre_own = call(
        functools.partial(early_kernel, dims),
        [((2, rows, TAPS, columns), BF16), ((frames, rows, WIDTH, columns), F32)],
        [VMEM] * 6,
        flops=10**9,
    )(earlier, table, rows_own, inside, bias, x_own)

    data_rows = 27 * CH // 2 + 4 * WIDTH + 8
    chunk = -(-data_rows // 32) * 8
    common = (table, rows_halo, x_early, x_own, pre_own, dact, outside, cot)
    rows_scratch = pltpu.VMEM((frames + 2, 3, TAPS, columns), BF16)
    acts_shape = (frames, 2 * WIDTH, pair)
    slopes_shape = (frames * WIDTH, columns)
    inside_parts = call(
        functools.partial(mid_kernel, dims),
        [
            (acts_shape, BF16),
            (slopes_shape, BF16),
            ((27 * CH, WIDTH), F32),
            ((2 * WIDTH, width2), F32),
            ((8, WIDTH), F32),
        ],
        [VMEM] * 9,
        [rows_scratch],
        flops=10**9,
    )(inner, *common)
    mine, keep, give, acts, slopes = call(
        functools.partial(main_kernel, dims, heights),
        [
            ((chunk, WIDTH), F32),
            ((3, chunk, WIDTH), F32),
            ((4, chunk, WIDTH), BF16),
            ((rows, *acts_shape), BF16),
            ((rows, *slopes_shape), BF16),
        ],
        [VMEM] * 14,
        [rows_scratch, pltpu.VMEM((2, 4 * chunk, WIDTH), F32)],
        flops=10**9,
    )(outer, *common, *inside_parts)

    send_inner, send_outer = call(
        functools.partial(edge_kernel, dims), [(flat_halo, BF16), (flat_halo, BF16)], [VMEM] * 4, flops=10**9
    )(slopes, backward, table, rows_halo)
    features, pixels_own, pixels_early = call(
        functools.partial(late_kernel, dims),
        [((frames, rows // 2, pair, width2), BF16), (own.shape, F32), (own.shape, F32)],
        [VMEM] * 7,
        flops=10**9,
    )(acts, slopes, backward, down_flat, bias2, table, rows_own)

    given = swap_inner(give)
    rest = (keep + given[1:].astype(F32)).astype(BF16)
    planes = ("tm_lo", "y")
    parts = [exchange(rest[m - 1], planes, m) for m in (1, 2, 3)]
    mine = mine + given[0].astype(F32) + sum(part.astype(F32) for part in parts)
    mine = mine.astype(BF16)
    for axis in axes["rest"]:
        parts = [exchange(mine, axis, m) for m in range(1, lax.axis_size(axis))]
        mine = mine.astype(F32) + sum(part.astype(F32) for part in parts)
        mine = mine.astype(BF16)
    pieces = [mine] + [exchange(mine, planes, m) for m in (1, 2, 3)]
    theirs = swap_inner(jnp.stack(pieces))
    count = frames * count_tm * rows * count_height * columns
    scale = 1.0 / math.sqrt(count)
    outs = [
        ((27 * CH, WIDTH), F32),
        ((1, WIDTH), F32),
        ((4 * WIDTH, width2), F32),
        ((1, width2), F32),
    ]
    scratch = [
        pltpu.VMEM((4 * chunk, WIDTH), F32),
        pltpu.VMEM((3, 1, WIDTH), F32),
        pltpu.SemaphoreType.DMA((5,)),
    ]
    grads = call(
        functools.partial(finish_kernel, scale, False), outs, [VMEM] * 4, scratch, out_specs=[HBM] * 4
    )(*pieces)
    grad_conv, grad_conv_bias, grad_down, grad_down_bias = call(
        functools.partial(finish_kernel, scale, True),
        outs,
        [VMEM] + [HBM] * 4,
        scratch,
        out_specs=[HBM] * 4,
        input_output_aliases={1: 0, 2: 1, 3: 2, 4: 3},
    )(theirs, *grads)

    from_inner = swap_inner(send_inner).reshape((frames + 2) * colors, 4, pixel_columns)
    from_outer = swap_outer(send_outer).reshape((frames + 2) * colors, 4, pixel_columns)
    from_outer = jnp.where(at_end(heights), 0, from_outer)
    above = jnp.where(core == 0, from_outer, from_inner).astype(F32)
    below = jnp.where(core == 0, from_inner, from_outer).astype(F32)
    halo = jnp.concatenate([above, below], axis=1)
    early = pixels_early.reshape(frame_shape) + halo[: 2 * colors]
    late = pixels_own.reshape(frame_shape) + halo[2 * colors :]
    following = along_tm(early.astype(BF16), -1)
    last = lax.axis_index(times) == count_tm - 1
    grad_pixels = late + jnp.where(last, 0.0, following.astype(F32))
    return (
        features,
        grad_conv.reshape(conv_weight.shape),
        grad_conv_bias.reshape(WIDTH),
        grad_down.reshape(down_weight.shape),
        grad_down_bias.reshape(width2),
        grad_pixels.reshape(pixels.shape),
    )


def factors(size):
    parts = []
    while size > 1:
        part = 4 if size % 4 == 0 else 2
        assert size % part == 0
        parts.append(part)
        size //= part
    return parts


def solution(mesh):
    count_tm, count_height = mesh.shape["tm"], mesh.shape["height"]
    tm_parts, height_parts = factors(count_tm // 2), factors(count_height // 4)
    tm_names = tuple(f"tm_{n}" for n in range(len(tm_parts)))
    height_names = tuple(f"z_{n}" for n in range(len(height_parts)))
    axes = {
        "tm": tm_names + ("tm_lo",),
        "height": height_names + ("y", "core"),
        "rest": tm_names + height_names,
    }
    fine = Mesh(
        mesh.devices.reshape(tm_parts + [2] + height_parts + [2, 2]), axes["tm"] + axes["height"]
    )
    tm, height = axes["tm"], axes["height"]

    def body(*args):
        return local(axes, *args)

    return jax.shard_map(
        body,
        mesh=fine,
        in_specs=(P(tm, None, height, None), P(), P(), P(), P(), P(tm, height, None, None)),
        out_specs=(
            P(tm, height, None, None),
            P(),
            P(),
            P(),
            P(),
            P(tm, None, height, None),
        ),
        check_vma=False,
    )
```

```python
import functools
import math

import jax
import jax.numpy as jnp
import numpy as np
from jax import lax
from jax.experimental import pallas as pl
from jax.experimental.pallas import tpu as pltpu
from jax.sharding import Mesh, PartitionSpec as P


BF16, F32 = jnp.bfloat16, jnp.float32
HAAR = np.kron(np.array([[1.0, 1.0], [1.0, -1.0]]), np.array([[1.0, 1.0], [1.0, -1.0]])) * 0.5
VMEM = pl.BlockSpec(memory_space=pltpu.VMEM)
HBM = pl.BlockSpec(memory_space=pltpu.HBM)
NN = (((1,), (0,)), ((), ()))
NT = (((1,), (1,)), ((), ()))
COLORS, CH, WIDTH = 3, 48, 128
TAPS = 3 * CH


def mm(a, b, dims=NN):
    return lax.dot_general(a, b, dims, preferred_element_type=F32)


def split(x):
    high = x.astype(BF16)
    return high, (x - high.astype(F32)).astype(BF16)


def order_of(core):
    plane = 2 * lax.axis_index("tm_lo") + lax.axis_index("y")
    return jnp.where(core == 0, plane, lax.axis_index("z_0"))


def call(body, outs, ins, scratch=(), flops=0, grant=24, **more):
    shapes = [jax.ShapeDtypeStruct(shape, dtype) for shape, dtype in outs]
    return pl.pallas_call(
        body,
        out_shape=shapes,
        scratch_shapes=list(scratch),
        cost_estimate=pl.CostEstimate(flops=flops, bytes_accessed=1 << 20, transcendentals=0),
        compiler_params=pltpu.CompilerParams(vmem_limit_bytes=grant << 20),
        in_specs=ins,
        **{"out_specs": [VMEM] * len(outs), **more},
    )


def column_table(quarter):
    table = np.zeros((8 * quarter, 4, 2, quarter), np.float32)
    for parity in range(2):
        for pair in range(quarter):
            for v in range(4):
                table[8 * pair + 4 * parity + v, :, parity, pair] = HAAR[:, v]
    return table.reshape(8 * quarter, 8 * quarter)


def row_table(frames, rows):
    table = np.zeros((frames, rows, COLORS, 4, 4, 4, frames, COLORS, rows, 4), np.float32)
    for f in range(frames):
        for r in range(rows):
            for k in range(COLORS):
                for j in range(4):
                    table[f, r, k, :, j, j, f, k, r, :] = HAAR
    return table.reshape(frames * rows * CH, 4 * frames * COLORS * rows * 4)


def choose_table(frames, rows):
    table = np.zeros((2, 2, frames + 2, COLORS, 4, frames + 2, COLORS, 4 * rows), np.float32)
    for core in range(2):
        for way in range(2):
            at = 4 * rows - 4 if core == way else 0
            for f in range(frames + 2):
                for k in range(COLORS):
                    for u in range(4):
                        table[core, way, f, k, u, f, k, at + u] = 1.0
    return table.reshape(2, 2 * (frames + 2) * COLORS * 4, (frames + 2) * COLORS * 4 * rows)


def shifts(pair):
    lane = lax.broadcasted_iota(jnp.int32, (1, pair), 1)

    def left(value):
        return jnp.where(lane == pair - 1, 0.0, pltpu.roll(value, pair - 1, 1))

    def right(value):
        return jnp.where(lane == 0, 0.0, pltpu.roll(value, 1, 1))

    return left, right


def analyse(groups, table, rows_tables, x, places, pair):
    left, right = shifts(pair)
    low_half = lax.broadcasted_iota(jnp.int32, (1, pair), 1) < pair // 2
    size, width = groups[0].shape
    stacked = [group[:, half * width // 2 : (half + 1) * width // 2] for group in groups for half in range(2)]
    columns = mm(jnp.concatenate(stacked, axis=0), table[...])
    for n, (rows_table, where) in enumerate(zip(rows_tables, places)):
        blocks = []
        for j in range(4):
            one = columns[2 * n * size : (2 * n + 1) * size, pair * j : pair * (j + 1)]
            two = columns[(2 * n + 1) * size : (2 * n + 2) * size, pair * j : pair * (j + 1)]
            even = jnp.where(low_half, one, pltpu.roll(two, pair // 2, 1))
            odd = jnp.where(low_half, pltpu.roll(one, pair // 2, 1), two)
            blocks.append(jnp.concatenate([even, odd], axis=1))
        high, low = split(jnp.concatenate(blocks, axis=0))
        cells = (mm(rows_table[...], high) + mm(rows_table[...], low)).astype(BF16)
        even, odd = cells[:, :pair].astype(F32), cells[:, pair:].astype(F32)
        taps = (
            jnp.concatenate([right(odd), even], axis=1).astype(BF16),
            cells,
            jnp.concatenate([odd, left(even)], axis=1).astype(BF16),
        )
        for block, (f, r) in enumerate(where):
            for d in range(3):
                x[f, r, CH * d : CH * (d + 1)] = taps[d][CH * block : CH * (block + 1)]


def synthesise(groups, table, rows_tables, pair):
    low_half = lax.broadcasted_iota(jnp.int32, (1, pair), 1) < pair // 2
    stacked = []
    for cells, rows_table in zip(groups, rows_tables):
        turned = mm(rows_table[...], cells.astype(BF16), (((0,), (0,)), ((), ())))
        size = turned.shape[0] // 4
        ones, twos = [], []
        for j in range(4):
            even = turned[size * j : size * (j + 1), :pair]
            odd = turned[size * j : size * (j + 1), pair:]
            ones.append(jnp.where(low_half, even, pltpu.roll(odd, pair // 2, 1)))
            twos.append(jnp.where(low_half, pltpu.roll(even, pair // 2, 1), odd))
        stacked += [jnp.concatenate(ones, axis=1), jnp.concatenate(twos, axis=1)]
    pixels = mm(jnp.concatenate(stacked, axis=0).astype(BF16), table[...], NT)
    size = stacked[0].shape[0]
    return [
        jnp.concatenate(
            [pixels[2 * n * size : (2 * n + 1) * size], pixels[(2 * n + 1) * size : (2 * n + 2) * size]],
            axis=1,
        )
        for n in range(len(groups))
    ]


def first_kernel(dims, count, *refs):
    frames, rows, pair = dims
    sources, targets = refs[:count], refs[count : 2 * count - 1]
    inside, outside, backward, x, dact, raw, sems = refs[2 * count - 1 :]
    copies = [
        pltpu.make_async_copy(source, target, sems.at[n])
        for n, (source, target) in enumerate(zip(sources, (raw, *targets)))
    ]
    for copy in copies:
        copy.start()
    own, table, rows_own, down_weight, cotangent = targets[:5]
    copies[0].wait()
    for a in range(3):
        for b in range(3):
            for d in range(3):
                at = CH * (3 * b + a)
                backward[at : at + CH, WIDTH * d : WIDTH * (d + 1)] = raw[9 * a + 3 * b + d]
        taps = raw[9 * a : 9 * a + 9].reshape(3 * TAPS, WIDTH).astype(F32)
        at = slice(WIDTH * a, WIDTH * (a + 1))
        inside[0, at] = taps[TAPS:].T.astype(BF16)
        inside[1, at] = taps[: 2 * TAPS].T.astype(BF16)
        outside[0, at] = taps[:TAPS].T.astype(BF16)
        outside[1, at] = taps[2 * TAPS :].T.astype(BF16)
    for copy in copies[1:]:
        copy.wait()
    where = [(f, r) for f in range(frames) for r in range(rows)]
    analyse([own[...]], table, [rows_own], x, [where], pair)
    for f in range(frames):
        dact[f] = mm(down_weight[...], cotangent[f, 0], NT)


def pack_kernel(times, own, came, chosen, inner, outer, earlier):
    core = lax.axis_index("core")
    used = jnp.where(lax.axis_index(times) == 0, 0.0, 1.0)
    earlier[...] = (came[...].astype(F32) * used).astype(BF16)
    both = mm(chosen[core], jnp.concatenate([earlier[...], own[...]], axis=0)).astype(BF16)
    size = inner.shape[0]
    inner[...] = both[:size]
    outer[...] = both[size:]


def taps_of(frame, frames):
    return [(f, frame - f) for f in range(frames) if 0 <= frame - f < 3]


def convolve(total, weights, values, frame, frames):
    used = taps_of(frame, frames)
    first = min(a for _, a in used)
    last = max(a for _, a in used)
    part = mm(weights[WIDTH * first : WIDTH * (last + 1)], values)
    for f, a in used:
        here = part[WIDTH * (a - first) : WIDTH * (a - first + 1)]
        total[f] = here if total[f] is None else total[f] + here


def early_kernel(dims, earlier, table, rows_own, inside, conv_bias, x_own, x, pre):
    frames, rows, pair = dims
    where = [(f, r) for f in range(2) for r in range(rows)]
    analyse([earlier[...]], table, [rows_own], x, [where], pair)
    bias = jnp.broadcast_to(conv_bias[...], (WIDTH, WIDTH)).T
    bias = jnp.concatenate([bias] * (2 * pair // WIDTH), axis=1)
    for r in range(rows):
        total = [bias] * frames
        for frame in range(frames + 2):
            values = (x[frame] if frame < 2 else x_own[frame - 2]).reshape(rows * TAPS, 2 * pair)
            convolve(total, inside[r], values, frame, frames)
        for f in range(frames):
            pre[f, r] = total[f]


def one_row(dims, r, halo, table, rows_halo, x_early, x_own, pre_own, dact, outside, cotangent, acts, slopes, x):
    frames, rows, pair = dims
    for frame in range(frames + 2):
        here = x_early[frame] if frame < 2 else x_own[frame - 2]
        x[frame, pl.ds(1 - r, rows)] = here
    analyse([halo], table, [rows_halo], x, [[(f, 2 * r) for f in range(frames + 2)]], pair)
    total = [pre_own[f, r] for f in range(frames)]
    for frame in range(frames + 2):
        convolve(total, outside[r], x[frame, 2 * r], frame, frames)
    down_total = None
    for f in range(frames):
        pre = total[f]
        sig = jax.nn.sigmoid(pre)
        act = pre * sig
        acts[f, :WIDTH] = act[:, :pair].astype(BF16)
        acts[f, WIDTH:] = act[:, pair:].astype(BF16)
        here = dact[f, pl.ds(pl.multiple_of(2 * WIDTH * r, 2 * WIDTH), 2 * WIDTH)]
        here = jnp.concatenate([here[:WIDTH], here[WIDTH:]], axis=1)
        slope = here * sig * (1.0 + pre * (1.0 - sig))
        slopes[WIDTH * f : WIDTH * (f + 1)] = slope.astype(BF16)
        part = mm(acts[f], cotangent[f, 0])
        down_total = part if down_total is None else down_total + part
    conv_total = [None] * 3
    for frame in range(frames + 2):
        used = taps_of(frame, frames)
        first, last = used[0][0], used[-1][0]
        values = x[frame].reshape(3 * TAPS, 2 * pair)
        part = mm(values, slopes[WIDTH * first : WIDTH * (last + 1)], NT)
        for f, a in used:
            here = part[:, WIDTH * (f - first) : WIDTH * (f - first + 1)]
            conv_total[a] = here if conv_total[a] is None else conv_total[a] + here
    slope_total = mm(jnp.ones((8, 2 * pair), BF16), slopes[...], NT)
    slope_total = sum(slope_total[:, WIDTH * f : WIDTH * (f + 1)] for f in range(frames))
    return jnp.concatenate(conv_total, axis=0), down_total, slope_total


def mid_kernel(dims, halo, *refs):
    table, rows_halo, x_early, x_own, pre_own, dact, outside, cotangent = refs[:8]
    acts, slopes, conv, down, total, x = refs[8:]
    core = lax.axis_index("core")
    conv[...], down[...], total[...] = one_row(
        dims, 1 - core, halo[...], *refs[:8], acts, slopes, x
    )


def at_end(heights):
    height = lax.axis_index(heights)
    return (height == 0) | (height == lax.axis_size(heights) - 1)


def main_kernel(dims, heights, halo, *refs):
    frames, rows, pair = dims
    _, _, _, _, _, _, _, cotangent = refs[:8]
    acts_in, slopes_in, conv_in, down_in, total_in, mine, keep, give, acts, slopes, x, packed = refs[8:]
    core = lax.axis_index("core")
    halo = (halo[...].astype(F32) * jnp.where(at_end(heights), 0.0, 1.0)).astype(BF16)
    acts[1 - core] = acts_in[...]
    slopes[1 - core] = slopes_in[...]
    conv, down, total = one_row(
        dims, core, halo, *refs[:8], acts.at[core], slopes.at[core], x
    )
    conv = conv + conv_in[...]
    slope_total = (total + total_in[...])[0:1]
    ones = jnp.ones((8, pair), BF16)
    cot_total = sum(mm(ones, cotangent[f, 0]) for f in range(frames))

    chunk = keep.shape[1]
    half = 27 * CH // 2
    sums = [slope_total, cot_total[0:1, :WIDTH], cot_total[0:1, WIDTH:]]
    highs = [value.astype(BF16).astype(F32) for value in sums]
    lows = [value - high for value, high in zip(sums, highs)]
    sums = jnp.concatenate(highs + lows + [jnp.zeros((2, WIDTH), F32)], axis=0)
    down_rows = 2 * rows * WIDTH
    for h in range(2):
        columns = slice(WIDTH * h, WIDTH * (h + 1))
        packed[h, :half] = conv[half * h : half * (h + 1)]
        for r, part in ((1 - core, down_in[:, columns]), (core, down[:, columns])):
            packed[h, pl.ds(pl.multiple_of(half + 2 * WIDTH * r, 8), 2 * WIDTH)] = part
        packed[h, half + down_rows : half + down_rows + 8] = sums if h == 0 else jnp.zeros_like(sums)
        rest = 4 * chunk - half - down_rows - 8
        if rest:
            packed[h, half + down_rows + 8 :] = jnp.zeros((rest, WIDTH), F32)
    for m in range(4):
        at = pl.multiple_of(jnp.bitwise_xor(order_of(core), m) * chunk, 8)
        if m:
            keep[m - 1] = packed[core, pl.ds(at, chunk)]
        else:
            mine[...] = packed[core, pl.ds(at, chunk)]
        at = pl.multiple_of(jnp.bitwise_xor(order_of(1 - core), m) * chunk, 8)
        give[m] = packed[1 - core, pl.ds(at, chunk)].astype(BF16)


def shifted_slope(slopes, f, r, pair):
    left, right = shifts(pair)
    slope = slopes[r, WIDTH * f : WIDTH * (f + 1)]
    even, odd = slope[:, :pair].astype(F32), slope[:, pair:].astype(F32)
    return jnp.concatenate(
        [
            jnp.concatenate([odd, left(even)], axis=1).astype(BF16),
            slope,
            jnp.concatenate([right(odd), even], axis=1).astype(BF16),
        ],
        axis=0,
    )


def spread_slope(total, slopes, backward, frames, reach, pair):
    for f in range(frames):
        for r in sorted({r for r, _, _ in reach}):
            taps = [(b, row) for here, b, row in reach if here == r]
            first, last = min(taps)[0], max(taps)[0]
            part = mm(backward[TAPS * first : TAPS * (last + 1)], shifted_slope(slopes, f, r, pair))
            for b, row in taps:
                for a in range(3):
                    at = TAPS * (b - first) + CH * a
                    here = part[at : at + CH]
                    key = (f + a, row)
                    total[key] = here if key not in total else total[key] + here


def edge_kernel(dims, slopes, backward, table, rows_halo, send_inner, send_outer):
    frames, rows, pair = dims
    core = lax.axis_index("core")
    total = {}
    spread_slope(total, slopes, backward, frames, [(0, 0, 0), (rows - 1, 2, 1)], pair)
    groups = [
        jnp.concatenate([total[frame, row] for frame in range(frames + 2)], axis=0) for row in range(2)
    ]
    above, below = synthesise(groups, table, [rows_halo, rows_halo], pair)
    send_inner[...] = jnp.where(core == 0, below, above).astype(BF16)
    send_outer[...] = jnp.where(core == 0, above, below).astype(BF16)


def late_kernel(
    dims,
    acts,
    slopes,
    backward,
    down_weight,
    down_bias,
    table,
    rows_own,
    features,
    pixels_own,
    pixels_early,
):
    frames, rows, pair = dims
    total = {}
    reach = [(r, b, r + b - 1) for r in range(rows) for b in range(3) if 0 <= r + b - 1 < rows]
    spread_slope(total, slopes, backward, frames, reach, pair)
    groups = [
        jnp.concatenate([total[first + f, r] for f in range(frames) for r in range(rows)], axis=0)
        for first in (0, 2)
    ]
    pixels_early[...], pixels_own[...] = synthesise(groups, table, [rows_own, rows_own], pair)
    for f in range(frames):
        blocks = [acts[u, f, WIDTH * v : WIDTH * (v + 1)] for u in range(2) for v in range(2)]
        turned = jnp.concatenate([block.astype(F32).T.astype(BF16) for block in blocks], axis=1)
        features[f, 0] = (mm(turned, down_weight[...]) + down_bias[...]).astype(BF16)


def finish_kernel(scale, other, *refs):
    pieces, (conv, conv_bias, down, down_bias, flat, sums, sems) = refs[:4], refs[-7:]
    if other:
        pieces = [refs[0].at[m] for m in range(4)]
    core = lax.axis_index("core")
    which = 1 - core if other else core
    chunk = pieces[0].shape[0]
    for m in range(4):
        at = pl.multiple_of(jnp.bitwise_xor(order_of(which), m) * chunk, 8)
        flat[pl.ds(at, chunk)] = pieces[m][...].astype(F32) * scale
    half, down_rows = conv.shape[0] // 2, down.shape[0]
    at = pl.multiple_of(half * which, 8)
    copies = [
        pltpu.make_async_copy(flat.at[pl.ds(0, half)], conv.at[pl.ds(at, half)], sems.at[0]),
        pltpu.make_async_copy(
            flat.at[pl.ds(half, down_rows)],
            down.at[:, pl.ds(pl.multiple_of(WIDTH * which, WIDTH), WIDTH)],
            sems.at[1],
        ),
    ]
    for copy in copies:
        copy.start()

    @pl.when(which == 0)
    def _():
        at = half + down_rows
        total = flat[at : at + 8]
        total = total[0:3] + total[3:6]
        for n in range(3):
            sums[n] = total[n : n + 1]
        targets = [conv_bias, down_bias.at[:, pl.ds(0, WIDTH)], down_bias.at[:, pl.ds(WIDTH, WIDTH)]]
        small = [
            pltpu.make_async_copy(sums.at[n], target, sems.at[2 + n]) for n, target in enumerate(targets)
        ]
        for copy in small:
            copy.start()
        for copy in small:
            copy.wait()

    for copy in copies:
        copy.wait()


def local(axes, pixels, conv_weight, conv_bias, down_weight, down_bias, cotangent):
    times, heights = axes["tm"], axes["height"]
    frames, colors, pixel_rows, pixel_columns = pixels.shape
    rows, columns = pixel_rows // 4, pixel_columns // 4
    assert frames == 2 and rows == 2 and colors == COLORS
    assert conv_weight.shape[3:] == (CH, WIDTH)
    pair = columns // 2
    width2 = down_weight.shape[3]
    core = lax.axis_index("core")
    count_tm, count_height = lax.axis_size(times), lax.axis_size(heights)
    dims = (frames, rows, pair)

    def along_tm(value, step):
        pairs = [(i, (i + step) % count_tm) for i in range(count_tm)]
        return lax.ppermute(value, times, pairs)

    def swap_inner(value):
        return lax.ppermute(value, "core", [(0, 1), (1, 0)])

    def swap_outer(value):
        inside = [(i, i + 1) for i in range(1, count_height - 1, 2)]
        inside += [(j, i) for i, j in inside]
        pairs = [(count_height * t + i, count_height * t + j) for t in range(count_tm) for i, j in inside]
        for end in (0, count_height - 1):
            pairs += [(count_height * t + end, count_height * (t ^ 1) + end) for t in range(count_tm)]
        return lax.ppermute(value, times + heights, pairs)

    def exchange(value, axes, mask):
        size = lax.axis_size(axes)
        return lax.ppermute(value, axes, [(i, i ^ mask) for i in range(size)])

    own = pixels.reshape(frames * colors * pixel_rows, pixel_columns)
    came = along_tm(own, 1)
    flat_halo = ((frames + 2) * colors * 4, pixel_columns)
    frame_shape = (2 * colors, pixel_rows, pixel_columns)
    sources = [
        conv_weight.reshape(27, CH, WIDTH),
        own,
        jnp.asarray(column_table(pair // 2), BF16),
        jnp.asarray(row_table(frames, rows), BF16),
        down_weight.reshape(4 * WIDTH, width2),
        cotangent,
        jnp.asarray(row_table(frames + 2, 1), BF16),
        jnp.asarray(choose_table(frames, rows), BF16),
        conv_bias.reshape(1, WIDTH),
        down_bias.reshape(1, width2),
    ]
    outs = call(
        functools.partial(first_kernel, dims, len(sources)),
        [(source.shape, source.dtype) for source in sources[1:]]
        + [
            ((2, 3 * WIDTH, 2 * TAPS), BF16),
            ((2, 3 * WIDTH, TAPS), BF16),
            ((9 * CH, 3 * WIDTH), BF16),
            ((frames, rows, TAPS, columns), BF16),
            ((frames, 4 * WIDTH, pair), F32),
        ],
        [HBM] * len(sources),
        [pltpu.VMEM((27, CH, WIDTH), BF16), pltpu.SemaphoreType.DMA((len(sources),))],
        flops=10**9,
    )(*(pltpu.with_memory_space_constraint(source, pltpu.HBM) for source in sources))
    own, table, rows_own, down_flat, cot, rows_halo, chosen, bias, bias2 = outs[:9]
    inside, outside, backward, x_own, dact = outs[9:]
    send_inner, send_outer, earlier = call(
        functools.partial(pack_kernel, times), [(flat_halo, BF16), (flat_halo, BF16), (own.shape, BF16)], [VMEM] * 3
    )(own, came, chosen)
    inner = swap_inner(send_inner)
    outer = swap_outer(send_outer)

    x_early, pre_own = call(
        functools.partial(early_kernel, dims),
        [((2, rows, TAPS, columns), BF16), ((frames, rows, WIDTH, columns), F32)],
        [VMEM] * 6,
        flops=10**9,
    )(earlier, table, rows_own, inside, bias, x_own)

    data_rows = 27 * CH // 2 + 4 * WIDTH + 8
    chunk = -(-data_rows // 32) * 8
    common = (table, rows_halo, x_early, x_own, pre_own, dact, outside, cot)
    rows_scratch = pltpu.VMEM((frames + 2, 3, TAPS, columns), BF16)
    acts_shape = (frames, 2 * WIDTH, pair)
    slopes_shape = (frames * WIDTH, columns)
    inside_parts = call(
        functools.partial(mid_kernel, dims),
        [
            (acts_shape, BF16),
            (slopes_shape, BF16),
            ((27 * CH, WIDTH), F32),
            ((2 * WIDTH, width2), F32),
            ((8, WIDTH), F32),
        ],
        [VMEM] * 9,
        [rows_scratch],
        flops=10**9,
    )(inner, *common)
    mine, keep, give, acts, slopes = call(
        functools.partial(main_kernel, dims, heights),
        [
            ((chunk, WIDTH), F32),
            ((3, chunk, WIDTH), F32),
            ((4, chunk, WIDTH), BF16),
            ((rows, *acts_shape), BF16),
            ((rows, *slopes_shape), BF16),
        ],
        [VMEM] * 14,
        [rows_scratch, pltpu.VMEM((2, 4 * chunk, WIDTH), F32)],
        flops=10**9,
    )(outer, *common, *inside_parts)

    send_inner, send_outer = call(
        functools.partial(edge_kernel, dims), [(flat_halo, BF16), (flat_halo, BF16)], [VMEM] * 4, flops=10**9
    )(slopes, backward, table, rows_halo)
    features, pixels_own, pixels_early = call(
        functools.partial(late_kernel, dims),
        [((frames, rows // 2, pair, width2), BF16), (own.shape, F32), (own.shape, F32)],
        [VMEM] * 7,
        flops=10**9,
    )(acts, slopes, backward, down_flat, bias2, table, rows_own)

    def cross(value, mask, first):
        names = times + heights
        sizes = [lax.axis_size(axis) for axis in names]
        pairs = []
        for source in range(math.prod(sizes)):
            at = dict(zip(names, np.unravel_index(source, sizes)))
            if (at["core"] == 0) == first:
                at["tm_lo"], at["y"] = at["tm_lo"] ^ (mask >> 1), at["y"] ^ (mask & 1)
            else:
                at["z_0"] ^= mask
            target = np.ravel_multi_index([at[axis] for axis in names], sizes)
            pairs.append((source, int(target)))
        return lax.ppermute(value, names, pairs)

    given = swap_inner(give)
    rest = (keep + given[1:].astype(F32)).astype(BF16)
    steps = (1, 2, 3)
    parts = [cross(rest[m - 1], m, True) for m in steps]
    mine = mine + given[0].astype(F32) + sum(part.astype(F32) for part in parts)
    mine = mine.astype(BF16)
    parts = [cross(mine, m, False) for m in steps]
    mine = (mine.astype(F32) + sum(part.astype(F32) for part in parts)).astype(BF16)
    for axis in axes["rest"]:
        parts = [exchange(mine, axis, m) for m in range(1, lax.axis_size(axis))]
        mine = (mine.astype(F32) + sum(part.astype(F32) for part in parts)).astype(BF16)
    pieces = [mine] + [cross(mine, m, True) for m in steps]
    theirs = swap_inner(jnp.stack(pieces))
    count = frames * count_tm * rows * count_height * columns
    scale = 1.0 / math.sqrt(count)
    outs = [
        ((27 * CH, WIDTH), F32),
        ((1, WIDTH), F32),
        ((4 * WIDTH, width2), F32),
        ((1, width2), F32),
    ]
    scratch = [
        pltpu.VMEM((4 * chunk, WIDTH), F32),
        pltpu.VMEM((3, 1, WIDTH), F32),
        pltpu.SemaphoreType.DMA((5,)),
    ]
    grads = call(
        functools.partial(finish_kernel, scale, False), outs, [VMEM] * 4, scratch, out_specs=[HBM] * 4
    )(*pieces)
    grad_conv, grad_conv_bias, grad_down, grad_down_bias = call(
        functools.partial(finish_kernel, scale, True),
        outs,
        [VMEM] + [HBM] * 4,
        scratch,
        out_specs=[HBM] * 4,
        input_output_aliases={1: 0, 2: 1, 3: 2, 4: 3},
    )(theirs, *grads)

    from_inner = swap_inner(send_inner).reshape((frames + 2) * colors, 4, pixel_columns)
    from_outer = swap_outer(send_outer).reshape((frames + 2) * colors, 4, pixel_columns)
    from_outer = jnp.where(at_end(heights), 0, from_outer)
    above = jnp.where(core == 0, from_outer, from_inner).astype(F32)
    below = jnp.where(core == 0, from_inner, from_outer).astype(F32)
    halo = jnp.concatenate([above, below], axis=1)
    early = pixels_early.reshape(frame_shape) + halo[: 2 * colors]
    late = pixels_own.reshape(frame_shape) + halo[2 * colors :]
    following = along_tm(early.astype(BF16), -1)
    last = lax.axis_index(times) == count_tm - 1
    grad_pixels = late + jnp.where(last, 0.0, following.astype(F32))
    return (
        features,
        grad_conv.reshape(conv_weight.shape),
        grad_conv_bias.reshape(WIDTH),
        grad_down.reshape(down_weight.shape),
        grad_down_bias.reshape(width2),
        grad_pixels.reshape(pixels.shape),
    )


def factors(size):
    parts = []
    while size > 1:
        part = 4 if size % 4 == 0 else 2
        assert size % part == 0
        parts.append(part)
        size //= part
    return parts


def solution(mesh):
    count_tm, count_height = mesh.shape["tm"], mesh.shape["height"]
    tm_parts, height_parts = factors(count_tm // 2), factors(count_height // 4)
    assert height_parts[0] == 4
    tm_names = tuple(f"tm_{n}" for n in range(len(tm_parts)))
    height_names = tuple(f"z_{n}" for n in range(len(height_parts)))
    axes = {
        "tm": tm_names + ("tm_lo",),
        "height": height_names + ("y", "core"),
        "rest": tm_names + height_names[1:],
    }
    fine = Mesh(
        mesh.devices.reshape(tm_parts + [2] + height_parts + [2, 2]), axes["tm"] + axes["height"]
    )
    tm, height = axes["tm"], axes["height"]

    def body(*args):
        return local(axes, *args)

    return jax.shard_map(
        body,
        mesh=fine,
        in_specs=(P(tm, None, height, None), P(), P(), P(), P(), P(tm, height, None, None)),
        out_specs=(
            P(tm, height, None, None),
            P(),
            P(),
            P(),
            P(),
            P(tm, None, height, None),
        ),
        check_vma=False,
    )
```

```python
import functools
import math

import jax
import jax.numpy as jnp
import numpy as np
from jax import lax
from jax.experimental import pallas as pl
from jax.experimental.pallas import tpu as pltpu
from jax.sharding import Mesh, PartitionSpec as P


BF16, F32 = jnp.bfloat16, jnp.float32
HAAR = np.kron(np.array([[1.0, 1.0], [1.0, -1.0]]), np.array([[1.0, 1.0], [1.0, -1.0]])) * 0.5
VMEM = pl.BlockSpec(memory_space=pltpu.VMEM)
HBM = pl.BlockSpec(memory_space=pltpu.HBM)
NN = (((1,), (0,)), ((), ()))
NT = (((1,), (1,)), ((), ()))
COLORS, CH, WIDTH = 3, 48, 128
TAPS = 3 * CH


def mm(a, b, dims=NN):
    return lax.dot_general(a, b, dims, preferred_element_type=F32)


def split(x):
    high = x.astype(BF16)
    return high, (x - high.astype(F32)).astype(BF16)


def order_of(core):
    plane = 2 * lax.axis_index("tm_lo") + lax.axis_index("y")
    return jnp.where(core == 0, plane, lax.axis_index("z_0"))


def call(body, outs, ins, scratch=(), flops=0, grant=24, **more):
    shapes = [jax.ShapeDtypeStruct(shape, dtype) for shape, dtype in outs]
    return pl.pallas_call(
        body,
        out_shape=shapes,
        scratch_shapes=list(scratch),
        cost_estimate=pl.CostEstimate(flops=flops, bytes_accessed=1 << 20, transcendentals=0),
        compiler_params=pltpu.CompilerParams(vmem_limit_bytes=grant << 20),
        in_specs=ins,
        **{"out_specs": [VMEM] * len(outs), **more},
    )


def column_table(quarter):
    table = np.zeros((8 * quarter, 4, 2, quarter), np.float32)
    for parity in range(2):
        for pair in range(quarter):
            for v in range(4):
                table[8 * pair + 4 * parity + v, :, parity, pair] = HAAR[:, v]
    return table.reshape(8 * quarter, 8 * quarter)


def row_table(frames, rows):
    table = np.zeros((frames, rows, COLORS, 4, 4, 4, frames, COLORS, rows, 4), np.float32)
    for f in range(frames):
        for r in range(rows):
            for k in range(COLORS):
                for j in range(4):
                    table[f, r, k, :, j, j, f, k, r, :] = HAAR
    return table.reshape(frames * rows * CH, 4 * frames * COLORS * rows * 4)


def choose_table(frames, rows):
    table = np.zeros((2, 2, frames + 2, COLORS, 4, frames + 2, COLORS, 4 * rows), np.float32)
    for core in range(2):
        for way in range(2):
            at = 4 * rows - 4 if core == way else 0
            for f in range(frames + 2):
                for k in range(COLORS):
                    for u in range(4):
                        table[core, way, f, k, u, f, k, at + u] = 1.0
    return table.reshape(2, 2 * (frames + 2) * COLORS * 4, (frames + 2) * COLORS * 4 * rows)


def shifts(pair):
    lane = lax.broadcasted_iota(jnp.int32, (1, pair), 1)

    def left(value):
        return jnp.where(lane == pair - 1, 0.0, pltpu.roll(value, pair - 1, 1))

    def right(value):
        return jnp.where(lane == 0, 0.0, pltpu.roll(value, 1, 1))

    return left, right


def analyse(groups, table, rows_tables, x, places, pair):
    left, right = shifts(pair)
    low_half = lax.broadcasted_iota(jnp.int32, (1, pair), 1) < pair // 2
    size, width = groups[0].shape
    stacked = [group[:, half * width // 2 : (half + 1) * width // 2] for group in groups for half in range(2)]
    columns = mm(jnp.concatenate(stacked, axis=0), table[...])
    for n, (rows_table, where) in enumerate(zip(rows_tables, places)):
        blocks = []
        for j in range(4):
            one = columns[2 * n * size : (2 * n + 1) * size, pair * j : pair * (j + 1)]
            two = columns[(2 * n + 1) * size : (2 * n + 2) * size, pair * j : pair * (j + 1)]
            even = jnp.where(low_half, one, pltpu.roll(two, pair // 2, 1))
            odd = jnp.where(low_half, pltpu.roll(one, pair // 2, 1), two)
            blocks.append(jnp.concatenate([even, odd], axis=1))
        high, low = split(jnp.concatenate(blocks, axis=0))
        cells = (mm(rows_table[...], high) + mm(rows_table[...], low)).astype(BF16)
        even, odd = cells[:, :pair].astype(F32), cells[:, pair:].astype(F32)
        taps = (
            jnp.concatenate([right(odd), even], axis=1).astype(BF16),
            cells,
            jnp.concatenate([odd, left(even)], axis=1).astype(BF16),
        )
        for block, (f, r) in enumerate(where):
            for d in range(3):
                x[f, r, CH * d : CH * (d + 1)] = taps[d][CH * block : CH * (block + 1)]


def synthesise(groups, table, rows_tables, pair):
    low_half = lax.broadcasted_iota(jnp.int32, (1, pair), 1) < pair // 2
    stacked = []
    for cells, rows_table in zip(groups, rows_tables):
        turned = mm(rows_table[...], cells.astype(BF16), (((0,), (0,)), ((), ())))
        size = turned.shape[0] // 4
        ones, twos = [], []
        for j in range(4):
            even = turned[size * j : size * (j + 1), :pair]
            odd = turned[size * j : size * (j + 1), pair:]
            ones.append(jnp.where(low_half, even, pltpu.roll(odd, pair // 2, 1)))
            twos.append(jnp.where(low_half, pltpu.roll(even, pair // 2, 1), odd))
        stacked += [jnp.concatenate(ones, axis=1), jnp.concatenate(twos, axis=1)]
    pixels = mm(jnp.concatenate(stacked, axis=0).astype(BF16), table[...], NT)
    size = stacked[0].shape[0]
    return [
        jnp.concatenate(
            [pixels[2 * n * size : (2 * n + 1) * size], pixels[(2 * n + 1) * size : (2 * n + 2) * size]],
            axis=1,
        )
        for n in range(len(groups))
    ]


def first_kernel(dims, count, *refs):
    frames, rows, pair = dims
    sources, targets = refs[:count], refs[count : 2 * count - 1]
    inside, outside, backward, x, dact, raw, sems = refs[2 * count - 1 :]
    copies = [
        pltpu.make_async_copy(source, target, sems.at[n])
        for n, (source, target) in enumerate(zip(sources, (raw, *targets)))
    ]
    for copy in copies:
        copy.start()
    own, table, rows_own, down_weight, cotangent = targets[:5]
    copies[0].wait()
    for a in range(3):
        for b in range(3):
            for d in range(3):
                at = CH * (3 * b + a)
                backward[at : at + CH, WIDTH * d : WIDTH * (d + 1)] = raw[9 * a + 3 * b + d]
        taps = raw[9 * a : 9 * a + 9].reshape(3 * TAPS, WIDTH).astype(F32)
        at = slice(WIDTH * a, WIDTH * (a + 1))
        inside[0, at] = taps[TAPS:].T.astype(BF16)
        inside[1, at] = taps[: 2 * TAPS].T.astype(BF16)
        outside[0, at] = taps[:TAPS].T.astype(BF16)
        outside[1, at] = taps[2 * TAPS :].T.astype(BF16)
    for copy in copies[1:]:
        copy.wait()
    where = [(f, r) for f in range(frames) for r in range(rows)]
    analyse([own[...]], table, [rows_own], x, [where], pair)
    for f in range(frames):
        dact[f] = mm(down_weight[...], cotangent[f, 0], NT)


def pack_kernel(times, own, came, chosen, inner, outer, earlier):
    core = lax.axis_index("core")
    used = jnp.where(lax.axis_index(times) == 0, 0.0, 1.0)
    earlier[...] = (came[...].astype(F32) * used).astype(BF16)
    both = mm(chosen[core], jnp.concatenate([earlier[...], own[...]], axis=0)).astype(BF16)
    size = inner.shape[0]
    inner[...] = both[:size]
    outer[...] = both[size:]


def taps_of(frame, frames):
    return [(f, frame - f) for f in range(frames) if 0 <= frame - f < 3]


def convolve(total, weights, values, frame, frames):
    used = taps_of(frame, frames)
    first = min(a for _, a in used)
    last = max(a for _, a in used)
    part = mm(weights[WIDTH * first : WIDTH * (last + 1)], values)
    for f, a in used:
        here = part[WIDTH * (a - first) : WIDTH * (a - first + 1)]
        total[f] = here if total[f] is None else total[f] + here


def early_kernel(dims, earlier, table, rows_own, inside, conv_bias, x_own, x, pre):
    frames, rows, pair = dims
    where = [(f, r) for f in range(2) for r in range(rows)]
    analyse([earlier[...]], table, [rows_own], x, [where], pair)
    bias = jnp.broadcast_to(conv_bias[...], (WIDTH, WIDTH)).T
    bias = jnp.concatenate([bias] * (2 * pair // WIDTH), axis=1)
    for r in range(rows):
        total = [bias] * frames
        for frame in range(frames + 2):
            values = (x[frame] if frame < 2 else x_own[frame - 2]).reshape(rows * TAPS, 2 * pair)
            convolve(total, inside[r], values, frame, frames)
        for f in range(frames):
            pre[f, r] = total[f]


def one_row(dims, r, halo, table, rows_halo, x_early, x_own, pre_own, dact, outside, cotangent, acts, slopes, x):
    frames, rows, pair = dims
    for frame in range(frames + 2):
        here = x_early[frame] if frame < 2 else x_own[frame - 2]
        x[frame, pl.ds(1 - r, rows)] = here
    analyse([halo], table, [rows_halo], x, [[(f, 2 * r) for f in range(frames + 2)]], pair)
    total = [pre_own[f, r] for f in range(frames)]
    for frame in range(frames + 2):
        convolve(total, outside[r], x[frame, 2 * r], frame, frames)
    down_total = None
    for f in range(frames):
        pre = total[f]
        sig = jax.nn.sigmoid(pre)
        act = pre * sig
        acts[f, :WIDTH] = act[:, :pair].astype(BF16)
        acts[f, WIDTH:] = act[:, pair:].astype(BF16)
        here = dact[f, pl.ds(pl.multiple_of(2 * WIDTH * r, 2 * WIDTH), 2 * WIDTH)]
        here = jnp.concatenate([here[:WIDTH], here[WIDTH:]], axis=1)
        slope = here * sig * (1.0 + pre * (1.0 - sig))
        slopes[WIDTH * f : WIDTH * (f + 1)] = slope.astype(BF16)
        part = mm(acts[f], cotangent[f, 0])
        down_total = part if down_total is None else down_total + part
    conv_total = [None] * 3
    for frame in range(frames + 2):
        used = taps_of(frame, frames)
        first, last = used[0][0], used[-1][0]
        values = x[frame].reshape(3 * TAPS, 2 * pair)
        part = mm(values, slopes[WIDTH * first : WIDTH * (last + 1)], NT)
        for f, a in used:
            here = part[:, WIDTH * (f - first) : WIDTH * (f - first + 1)]
            conv_total[a] = here if conv_total[a] is None else conv_total[a] + here
    slope_total = mm(jnp.ones((8, 2 * pair), BF16), slopes[...], NT)
    slope_total = sum(slope_total[:, WIDTH * f : WIDTH * (f + 1)] for f in range(frames))
    return jnp.concatenate(conv_total, axis=0), down_total, slope_total


def mid_kernel(dims, halo, *refs):
    table, rows_halo, x_early, x_own, pre_own, dact, outside, cotangent = refs[:8]
    acts, slopes, conv, down, total, x = refs[8:]
    core = lax.axis_index("core")
    conv[...], down[...], total[...] = one_row(
        dims, 1 - core, halo[...], *refs[:8], acts, slopes, x
    )


def at_end(heights):
    height = lax.axis_index(heights)
    return (height == 0) | (height == lax.axis_size(heights) - 1)


def main_kernel(dims, heights, halo, *refs):
    frames, rows, pair = dims
    _, _, _, _, _, _, _, cotangent = refs[:8]
    acts_in, slopes_in, conv_in, down_in, total_in, mine, keep, give_mine, give, acts, slopes, x, packed = refs[8:]
    core = lax.axis_index("core")
    halo = (halo[...].astype(F32) * jnp.where(at_end(heights), 0.0, 1.0)).astype(BF16)
    acts[1 - core] = acts_in[...]
    slopes[1 - core] = slopes_in[...]
    conv, down, total = one_row(
        dims, core, halo, *refs[:8], acts.at[core], slopes.at[core], x
    )
    conv = conv + conv_in[...]
    slope_total = (total + total_in[...])[0:1]
    ones = jnp.ones((8, pair), BF16)
    cot_total = sum(mm(ones, cotangent[f, 0]) for f in range(frames))

    chunk = keep.shape[1]
    half = 27 * CH // 2
    sums = [slope_total, cot_total[0:1, :WIDTH], cot_total[0:1, WIDTH:]]
    highs = [value.astype(BF16).astype(F32) for value in sums]
    lows = [value - high for value, high in zip(sums, highs)]
    sums = jnp.concatenate(highs + lows + [jnp.zeros((2, WIDTH), F32)], axis=0)
    down_rows = 2 * rows * WIDTH
    for h in range(2):
        columns = slice(WIDTH * h, WIDTH * (h + 1))
        packed[h, :half] = conv[half * h : half * (h + 1)]
        for r, part in ((1 - core, down_in[:, columns]), (core, down[:, columns])):
            packed[h, pl.ds(pl.multiple_of(half + 2 * WIDTH * r, 8), 2 * WIDTH)] = part
        packed[h, half + down_rows : half + down_rows + 8] = sums if h == 0 else jnp.zeros_like(sums)
        rest = 4 * chunk - half - down_rows - 8
        if rest:
            packed[h, half + down_rows + 8 :] = jnp.zeros((rest, WIDTH), F32)
    for m in range(4):
        at = pl.multiple_of(jnp.bitwise_xor(order_of(core), m) * chunk, 8)
        if m:
            keep[m - 1] = packed[core, pl.ds(at, chunk)]
        else:
            mine[...] = packed[core, pl.ds(at, chunk)]
        at = pl.multiple_of(jnp.bitwise_xor(order_of(1 - core), m) * chunk, 8)
        if m:
            give[m - 1] = packed[1 - core, pl.ds(at, chunk)].astype(BF16)
        else:
            give_mine[...] = packed[1 - core, pl.ds(at, chunk)].astype(BF16)


def shifted_slope(slopes, f, r, pair):
    left, right = shifts(pair)
    slope = slopes[r, WIDTH * f : WIDTH * (f + 1)]
    even, odd = slope[:, :pair].astype(F32), slope[:, pair:].astype(F32)
    return jnp.concatenate(
        [
            jnp.concatenate([odd, left(even)], axis=1).astype(BF16),
            slope,
            jnp.concatenate([right(odd), even], axis=1).astype(BF16),
        ],
        axis=0,
    )


def spread_slope(total, slopes, backward, frames, reach, pair):
    for f in range(frames):
        for r in sorted({r for r, _, _ in reach}):
            taps = [(b, row) for here, b, row in reach if here == r]
            first, last = min(taps)[0], max(taps)[0]
            part = mm(backward[TAPS * first : TAPS * (last + 1)], shifted_slope(slopes, f, r, pair))
            for b, row in taps:
                for a in range(3):
                    at = TAPS * (b - first) + CH * a
                    here = part[at : at + CH]
                    key = (f + a, row)
                    total[key] = here if key not in total else total[key] + here


def edge_kernel(dims, slopes, backward, table, rows_halo, send_inner, send_outer):
    frames, rows, pair = dims
    core = lax.axis_index("core")
    total = {}
    spread_slope(total, slopes, backward, frames, [(0, 0, 0), (rows - 1, 2, 1)], pair)
    groups = [
        jnp.concatenate([total[frame, row] for frame in range(frames + 2)], axis=0) for row in range(2)
    ]
    above, below = synthesise(groups, table, [rows_halo, rows_halo], pair)
    send_inner[...] = jnp.where(core == 0, below, above).astype(BF16)
    send_outer[...] = jnp.where(core == 0, above, below).astype(BF16)


def late_kernel(
    dims,
    acts,
    slopes,
    backward,
    down_weight,
    down_bias,
    table,
    rows_own,
    features,
    pixels_own,
    pixels_early,
):
    frames, rows, pair = dims
    total = {}
    reach = [(r, b, r + b - 1) for r in range(rows) for b in range(3) if 0 <= r + b - 1 < rows]
    spread_slope(total, slopes, backward, frames, reach, pair)
    groups = [
        jnp.concatenate([total[first + f, r] for f in range(frames) for r in range(rows)], axis=0)
        for first in (0, 2)
    ]
    pixels_early[...], pixels_own[...] = synthesise(groups, table, [rows_own, rows_own], pair)
    for f in range(frames):
        blocks = [acts[u, f, WIDTH * v : WIDTH * (v + 1)] for u in range(2) for v in range(2)]
        turned = jnp.concatenate([block.astype(F32).T.astype(BF16) for block in blocks], axis=1)
        features[f, 0] = (mm(turned, down_weight[...]) + down_bias[...]).astype(BF16)


def finish_kernel(scale, other, *refs):
    pieces, (conv, conv_bias, down, down_bias, flat, sums, sems) = refs[:4], refs[-7:]
    if other:
        pieces = [refs[0].at[m] for m in range(4)]
    core = lax.axis_index("core")
    which = 1 - core if other else core
    chunk = pieces[0].shape[0]
    for m in range(4):
        at = pl.multiple_of(jnp.bitwise_xor(order_of(which), m) * chunk, 8)
        flat[pl.ds(at, chunk)] = pieces[m][...].astype(F32) * scale
    half, down_rows = conv.shape[0] // 2, down.shape[0]
    at = pl.multiple_of(half * which, 8)
    copies = [
        pltpu.make_async_copy(flat.at[pl.ds(0, half)], conv.at[pl.ds(at, half)], sems.at[0]),
        pltpu.make_async_copy(
            flat.at[pl.ds(half, down_rows)],
            down.at[:, pl.ds(pl.multiple_of(WIDTH * which, WIDTH), WIDTH)],
            sems.at[1],
        ),
    ]
    for copy in copies:
        copy.start()

    @pl.when(which == 0)
    def _():
        at = half + down_rows
        total = flat[at : at + 8]
        total = total[0:3] + total[3:6]
        for n in range(3):
            sums[n] = total[n : n + 1]
        targets = [conv_bias, down_bias.at[:, pl.ds(0, WIDTH)], down_bias.at[:, pl.ds(WIDTH, WIDTH)]]
        small = [
            pltpu.make_async_copy(sums.at[n], target, sems.at[2 + n]) for n, target in enumerate(targets)
        ]
        for copy in small:
            copy.start()
        for copy in small:
            copy.wait()

    for copy in copies:
        copy.wait()


def local(axes, pixels, conv_weight, conv_bias, down_weight, down_bias, cotangent):
    times, heights = axes["tm"], axes["height"]
    frames, colors, pixel_rows, pixel_columns = pixels.shape
    rows, columns = pixel_rows // 4, pixel_columns // 4
    assert frames == 2 and rows == 2 and colors == COLORS
    assert conv_weight.shape[3:] == (CH, WIDTH)
    pair = columns // 2
    width2 = down_weight.shape[3]
    core = lax.axis_index("core")
    count_tm, count_height = lax.axis_size(times), lax.axis_size(heights)
    dims = (frames, rows, pair)

    def along_tm(value, step):
        pairs = [(i, (i + step) % count_tm) for i in range(count_tm)]
        return lax.ppermute(value, times, pairs)

    def swap_inner(value):
        return lax.ppermute(value, "core", [(0, 1), (1, 0)])

    def swap_outer(value):
        inside = [(i, i + 1) for i in range(1, count_height - 1, 2)]
        inside += [(j, i) for i, j in inside]
        pairs = [(count_height * t + i, count_height * t + j) for t in range(count_tm) for i, j in inside]
        for end in (0, count_height - 1):
            pairs += [(count_height * t + end, count_height * (t ^ 1) + end) for t in range(count_tm)]
        return lax.ppermute(value, times + heights, pairs)

    def exchange(value, axes, mask):
        size = lax.axis_size(axes)
        return lax.ppermute(value, axes, [(i, i ^ mask) for i in range(size)])

    own = pixels.reshape(frames * colors * pixel_rows, pixel_columns)
    came = along_tm(own, 1)
    flat_halo = ((frames + 2) * colors * 4, pixel_columns)
    frame_shape = (2 * colors, pixel_rows, pixel_columns)
    sources = [
        conv_weight.reshape(27, CH, WIDTH),
        own,
        jnp.asarray(column_table(pair // 2), BF16),
        jnp.asarray(row_table(frames, rows), BF16),
        down_weight.reshape(4 * WIDTH, width2),
        cotangent,
        jnp.asarray(row_table(frames + 2, 1), BF16),
        jnp.asarray(choose_table(frames, rows), BF16),
        conv_bias.reshape(1, WIDTH),
        down_bias.reshape(1, width2),
    ]
    outs = call(
        functools.partial(first_kernel, dims, len(sources)),
        [(source.shape, source.dtype) for source in sources[1:]]
        + [
            ((2, 3 * WIDTH, 2 * TAPS), BF16),
            ((2, 3 * WIDTH, TAPS), BF16),
            ((9 * CH, 3 * WIDTH), BF16),
            ((frames, rows, TAPS, columns), BF16),
            ((frames, 4 * WIDTH, pair), F32),
        ],
        [HBM] * len(sources),
        [pltpu.VMEM((27, CH, WIDTH), BF16), pltpu.SemaphoreType.DMA((len(sources),))],
        flops=10**9,
    )(*(pltpu.with_memory_space_constraint(source, pltpu.HBM) for source in sources))
    own, table, rows_own, down_flat, cot, rows_halo, chosen, bias, bias2 = outs[:9]
    inside, outside, backward, x_own, dact = outs[9:]
    send_inner, send_outer, earlier = call(
        functools.partial(pack_kernel, times), [(flat_halo, BF16), (flat_halo, BF16), (own.shape, BF16)], [VMEM] * 3
    )(own, came, chosen)
    inner = swap_inner(send_inner)
    outer = swap_outer(send_outer)

    x_early, pre_own = call(
        functools.partial(early_kernel, dims),
        [((2, rows, TAPS, columns), BF16), ((frames, rows, WIDTH, columns), F32)],
        [VMEM] * 6,
        flops=10**9,
    )(earlier, table, rows_own, inside, bias, x_own)

    data_rows = 27 * CH // 2 + 4 * WIDTH + 8
    chunk = -(-data_rows // 32) * 8
    common = (table, rows_halo, x_early, x_own, pre_own, dact, outside, cot)
    rows_scratch = pltpu.VMEM((frames + 2, 3, TAPS, columns), BF16)
    acts_shape = (frames, 2 * WIDTH, pair)
    slopes_shape = (frames * WIDTH, columns)
    inside_parts = call(
        functools.partial(mid_kernel, dims),
        [
            (acts_shape, BF16),
            (slopes_shape, BF16),
            ((27 * CH, WIDTH), F32),
            ((2 * WIDTH, width2), F32),
            ((8, WIDTH), F32),
        ],
        [VMEM] * 9,
        [rows_scratch],
        flops=10**9,
    )(inner, *common)
    mine, keep, give_mine, give, acts, slopes = call(
        functools.partial(main_kernel, dims, heights),
        [
            ((chunk, WIDTH), F32),
            ((3, chunk, WIDTH), F32),
            ((chunk, WIDTH), BF16),
            ((3, chunk, WIDTH), BF16),
            ((rows, *acts_shape), BF16),
            ((rows, *slopes_shape), BF16),
        ],
        [VMEM] * 14,
        [rows_scratch, pltpu.VMEM((2, 4 * chunk, WIDTH), F32)],
        flops=10**9,
    )(outer, *common, *inside_parts)

    send_inner, send_outer = call(
        functools.partial(edge_kernel, dims), [(flat_halo, BF16), (flat_halo, BF16)], [VMEM] * 4, flops=10**9
    )(slopes, backward, table, rows_halo)
    features, pixels_own, pixels_early = call(
        functools.partial(late_kernel, dims),
        [((frames, rows // 2, pair, width2), BF16), (own.shape, F32), (own.shape, F32)],
        [VMEM] * 7,
        flops=10**9,
    )(acts, slopes, backward, down_flat, bias2, table, rows_own)

    def cross(value, mask, first):
        names = times + heights
        sizes = [lax.axis_size(axis) for axis in names]
        pairs = []
        for source in range(math.prod(sizes)):
            at = dict(zip(names, np.unravel_index(source, sizes)))
            if (at["core"] == 0) == first:
                at["tm_lo"], at["y"] = at["tm_lo"] ^ (mask >> 1), at["y"] ^ (mask & 1)
            else:
                at["z_0"] ^= mask
            target = np.ravel_multi_index([at[axis] for axis in names], sizes)
            pairs.append((source, int(target)))
        return lax.ppermute(value, names, pairs)

    given = swap_inner(give)
    given_mine = swap_inner(give_mine)
    rest = (keep + given.astype(F32)).astype(BF16)
    steps = (1, 2, 3)
    parts = [cross(rest[m - 1], m, True) for m in steps]
    mine = mine + given_mine.astype(F32) + sum(part.astype(F32) for part in parts)
    mine = mine.astype(BF16)
    parts = [cross(mine, m, False) for m in steps]
    mine = (mine.astype(F32) + sum(part.astype(F32) for part in parts)).astype(BF16)
    for axis in axes["rest"]:
        parts = [exchange(mine, axis, m) for m in range(1, lax.axis_size(axis))]
        mine = (mine.astype(F32) + sum(part.astype(F32) for part in parts)).astype(BF16)
    pieces = [mine] + [cross(mine, m, True) for m in steps]
    theirs = swap_inner(jnp.stack(pieces))
    count = frames * count_tm * rows * count_height * columns
    scale = 1.0 / math.sqrt(count)
    outs = [
        ((27 * CH, WIDTH), F32),
        ((1, WIDTH), F32),
        ((4 * WIDTH, width2), F32),
        ((1, width2), F32),
    ]
    scratch = [
        pltpu.VMEM((4 * chunk, WIDTH), F32),
        pltpu.VMEM((3, 1, WIDTH), F32),
        pltpu.SemaphoreType.DMA((5,)),
    ]
    grads = call(
        functools.partial(finish_kernel, scale, False), outs, [VMEM] * 4, scratch, out_specs=[HBM] * 4
    )(*pieces)
    grad_conv, grad_conv_bias, grad_down, grad_down_bias = call(
        functools.partial(finish_kernel, scale, True),
        outs,
        [VMEM] + [HBM] * 4,
        scratch,
        out_specs=[HBM] * 4,
        input_output_aliases={1: 0, 2: 1, 3: 2, 4: 3},
    )(theirs, *grads)

    from_inner = swap_inner(send_inner).reshape((frames + 2) * colors, 4, pixel_columns)
    from_outer = swap_outer(send_outer).reshape((frames + 2) * colors, 4, pixel_columns)
    from_outer = jnp.where(at_end(heights), 0, from_outer)
    above = jnp.where(core == 0, from_outer, from_inner).astype(F32)
    below = jnp.where(core == 0, from_inner, from_outer).astype(F32)
    halo = jnp.concatenate([above, below], axis=1)
    early = pixels_early.reshape(frame_shape) + halo[: 2 * colors]
    late = pixels_own.reshape(frame_shape) + halo[2 * colors :]
    following = along_tm(early.astype(BF16), -1)
    last = lax.axis_index(times) == count_tm - 1
    grad_pixels = late + jnp.where(last, 0.0, following.astype(F32))
    return (
        features,
        grad_conv.reshape(conv_weight.shape),
        grad_conv_bias.reshape(WIDTH),
        grad_down.reshape(down_weight.shape),
        grad_down_bias.reshape(width2),
        grad_pixels.reshape(pixels.shape),
    )


def factors(size):
    parts = []
    while size > 1:
        part = 4 if size % 4 == 0 else 2
        assert size % part == 0
        parts.append(part)
        size //= part
    return parts


def solution(mesh):
    count_tm, count_height = mesh.shape["tm"], mesh.shape["height"]
    tm_parts, height_parts = factors(count_tm // 2), factors(count_height // 4)
    assert height_parts[0] == 4
    tm_names = tuple(f"tm_{n}" for n in range(len(tm_parts)))
    height_names = tuple(f"z_{n}" for n in range(len(height_parts)))
    axes = {
        "tm": tm_names + ("tm_lo",),
        "height": height_names + ("y", "core"),
        "rest": tm_names + height_names[1:],
    }
    fine = Mesh(
        mesh.devices.reshape(tm_parts + [2] + height_parts + [2, 2]), axes["tm"] + axes["height"]
    )
    tm, height = axes["tm"], axes["height"]

    def body(*args):
        return local(axes, *args)

    return jax.shard_map(
        body,
        mesh=fine,
        in_specs=(P(tm, None, height, None), P(), P(), P(), P(), P(tm, height, None, None)),
        out_specs=(
            P(tm, height, None, None),
            P(),
            P(),
            P(),
            P(),
            P(tm, None, height, None),
        ),
        check_vma=False,
    )
```

```python
import functools
import math

import jax
import jax.numpy as jnp
import numpy as np
from jax import lax
from jax.experimental import pallas as pl
from jax.experimental.pallas import tpu as pltpu
from jax.sharding import Mesh, PartitionSpec as P


BF16, F32 = jnp.bfloat16, jnp.float32
HAAR = np.kron(np.array([[1.0, 1.0], [1.0, -1.0]]), np.array([[1.0, 1.0], [1.0, -1.0]])) * 0.5
VMEM = pl.BlockSpec(memory_space=pltpu.VMEM)
HBM = pl.BlockSpec(memory_space=pltpu.HBM)
NN = (((1,), (0,)), ((), ()))
NT = (((1,), (1,)), ((), ()))
COLORS, CH, WIDTH = 3, 48, 128
TAPS = 3 * CH


def mm(a, b, dims=NN):
    return lax.dot_general(a, b, dims, preferred_element_type=F32)


def split(x):
    high = x.astype(BF16)
    return high, (x - high.astype(F32)).astype(BF16)


def order_of(core):
    plane = 2 * lax.axis_index("tm_lo") + lax.axis_index("y")
    return jnp.where(core == 0, plane, lax.axis_index("z_0"))


def call(body, outs, ins, scratch=(), flops=0, grant=24, **more):
    shapes = [jax.ShapeDtypeStruct(shape, dtype) for shape, dtype in outs]
    return pl.pallas_call(
        body,
        out_shape=shapes,
        scratch_shapes=list(scratch),
        cost_estimate=pl.CostEstimate(flops=flops, bytes_accessed=1 << 20, transcendentals=0),
        compiler_params=pltpu.CompilerParams(vmem_limit_bytes=grant << 20),
        in_specs=ins,
        **{"out_specs": [VMEM] * len(outs), **more},
    )


def column_table(quarter):
    table = np.zeros((8 * quarter, 4, 2, quarter), np.float32)
    for parity in range(2):
        for pair in range(quarter):
            for v in range(4):
                table[8 * pair + 4 * parity + v, :, parity, pair] = HAAR[:, v]
    return table.reshape(8 * quarter, 8 * quarter)


def row_table(frames, rows):
    table = np.zeros((frames, rows, COLORS, 4, 4, 4, frames, COLORS, rows, 4), np.float32)
    for f in range(frames):
        for r in range(rows):
            for k in range(COLORS):
                for j in range(4):
                    table[f, r, k, :, j, j, f, k, r, :] = HAAR
    return table.reshape(frames * rows * CH, 4 * frames * COLORS * rows * 4)


def choose_table(frames, rows):
    table = np.zeros((2, 2, frames + 2, COLORS, 4, frames + 2, COLORS, 4 * rows), np.float32)
    for core in range(2):
        for way in range(2):
            at = 4 * rows - 4 if core == way else 0
            for f in range(frames + 2):
                for k in range(COLORS):
                    for u in range(4):
                        table[core, way, f, k, u, f, k, at + u] = 1.0
    return table.reshape(2, 2 * (frames + 2) * COLORS * 4, (frames + 2) * COLORS * 4 * rows)


def shifts(pair):
    lane = lax.broadcasted_iota(jnp.int32, (1, pair), 1)

    def left(value):
        return jnp.where(lane == pair - 1, 0.0, pltpu.roll(value, pair - 1, 1))

    def right(value):
        return jnp.where(lane == 0, 0.0, pltpu.roll(value, 1, 1))

    return left, right


def analyse(groups, table, rows_tables, x, places, pair):
    left, right = shifts(pair)
    low_half = lax.broadcasted_iota(jnp.int32, (1, pair), 1) < pair // 2
    size, width = groups[0].shape
    stacked = [group[:, half * width // 2 : (half + 1) * width // 2] for group in groups for half in range(2)]
    columns = mm(jnp.concatenate(stacked, axis=0), table[...])
    for n, (rows_table, where) in enumerate(zip(rows_tables, places)):
        blocks = []
        for j in range(4):
            one = columns[2 * n * size : (2 * n + 1) * size, pair * j : pair * (j + 1)]
            two = columns[(2 * n + 1) * size : (2 * n + 2) * size, pair * j : pair * (j + 1)]
            even = jnp.where(low_half, one, pltpu.roll(two, pair // 2, 1))
            odd = jnp.where(low_half, pltpu.roll(one, pair // 2, 1), two)
            blocks.append(jnp.concatenate([even, odd], axis=1))
        high, low = split(jnp.concatenate(blocks, axis=0))
        cells = (mm(rows_table[...], high) + mm(rows_table[...], low)).astype(BF16)
        even, odd = cells[:, :pair].astype(F32), cells[:, pair:].astype(F32)
        taps = (
            jnp.concatenate([right(odd), even], axis=1).astype(BF16),
            cells,
            jnp.concatenate([odd, left(even)], axis=1).astype(BF16),
        )
        for block, (f, r) in enumerate(where):
            for d in range(3):
                x[f, r, CH * d : CH * (d + 1)] = taps[d][CH * block : CH * (block + 1)]


def synthesise(groups, table, rows_tables, pair):
    low_half = lax.broadcasted_iota(jnp.int32, (1, pair), 1) < pair // 2
    stacked = []
    for cells, rows_table in zip(groups, rows_tables):
        turned = mm(rows_table[...], cells.astype(BF16), (((0,), (0,)), ((), ())))
        size = turned.shape[0] // 4
        ones, twos = [], []
        for j in range(4):
            even = turned[size * j : size * (j + 1), :pair]
            odd = turned[size * j : size * (j + 1), pair:]
            ones.append(jnp.where(low_half, even, pltpu.roll(odd, pair // 2, 1)))
            twos.append(jnp.where(low_half, pltpu.roll(even, pair // 2, 1), odd))
        stacked += [jnp.concatenate(ones, axis=1), jnp.concatenate(twos, axis=1)]
    pixels = mm(jnp.concatenate(stacked, axis=0).astype(BF16), table[...], NT)
    size = stacked[0].shape[0]
    return [
        jnp.concatenate(
            [pixels[2 * n * size : (2 * n + 1) * size], pixels[(2 * n + 1) * size : (2 * n + 2) * size]],
            axis=1,
        )
        for n in range(len(groups))
    ]


def first_kernel(dims, count, *refs):
    frames, rows, pair = dims
    sources, targets = refs[:count], refs[count : 2 * count - 1]
    inside, outside, backward, x, dact, raw, sems = refs[2 * count - 1 :]
    copies = [
        pltpu.make_async_copy(source, target, sems.at[n])
        for n, (source, target) in enumerate(zip(sources, (raw, *targets)))
    ]
    for copy in copies:
        copy.start()
    own, table, rows_own, down_weight, cotangent = targets[:5]
    copies[0].wait()
    for a in range(3):
        for b in range(3):
            for d in range(3):
                at = CH * (3 * b + a)
                backward[at : at + CH, WIDTH * d : WIDTH * (d + 1)] = raw[9 * a + 3 * b + d]
        taps = raw[9 * a : 9 * a + 9].reshape(3 * TAPS, WIDTH).astype(F32)
        at = slice(WIDTH * a, WIDTH * (a + 1))
        inside[0, at] = taps[TAPS:].T.astype(BF16)
        inside[1, at] = taps[: 2 * TAPS].T.astype(BF16)
        outside[0, at] = taps[:TAPS].T.astype(BF16)
        outside[1, at] = taps[2 * TAPS :].T.astype(BF16)
    for copy in copies[1:]:
        copy.wait()
    where = [(f, r) for f in range(frames) for r in range(rows)]
    analyse([own[...]], table, [rows_own], x, [where], pair)
    for f in range(frames):
        dact[f] = mm(down_weight[...], cotangent[f, 0], NT)


def pack_kernel(times, own, came, chosen, inner, outer, earlier):
    core = lax.axis_index("core")
    used = jnp.where(lax.axis_index(times) == 0, 0.0, 1.0)
    earlier[...] = (came[...].astype(F32) * used).astype(BF16)
    both = mm(chosen[core], jnp.concatenate([earlier[...], own[...]], axis=0)).astype(BF16)
    size = inner.shape[0]
    inner[...] = both[:size]
    outer[...] = both[size:]


def taps_of(frame, frames):
    return [(f, frame - f) for f in range(frames) if 0 <= frame - f < 3]


def convolve(total, weights, values, frame, frames):
    used = taps_of(frame, frames)
    first = min(a for _, a in used)
    last = max(a for _, a in used)
    part = mm(weights[WIDTH * first : WIDTH * (last + 1)], values)
    for f, a in used:
        here = part[WIDTH * (a - first) : WIDTH * (a - first + 1)]
        total[f] = here if total[f] is None else total[f] + here


def early_kernel(dims, earlier, table, rows_own, inside, conv_bias, x_own, x, pre):
    frames, rows, pair = dims
    where = [(f, r) for f in range(2) for r in range(rows)]
    analyse([earlier[...]], table, [rows_own], x, [where], pair)
    bias = jnp.broadcast_to(conv_bias[...], (WIDTH, WIDTH)).T
    bias = jnp.concatenate([bias] * (2 * pair // WIDTH), axis=1)
    for r in range(rows):
        total = [bias] * frames
        for frame in range(frames + 2):
            values = (x[frame] if frame < 2 else x_own[frame - 2]).reshape(rows * TAPS, 2 * pair)
            convolve(total, inside[r], values, frame, frames)
        for f in range(frames):
            pre[f, r] = total[f]


def one_row(dims, r, halo, table, rows_halo, x_early, x_own, pre_own, dact, outside, cotangent, acts, slopes, x):
    frames, rows, pair = dims
    for frame in range(frames + 2):
        here = x_early[frame] if frame < 2 else x_own[frame - 2]
        x[frame, pl.ds(1 - r, rows)] = here
    analyse([halo], table, [rows_halo], x, [[(f, 2 * r) for f in range(frames + 2)]], pair)
    total = [pre_own[f, r] for f in range(frames)]
    for frame in range(frames + 2):
        convolve(total, outside[r], x[frame, 2 * r], frame, frames)
    down_total = None
    for f in range(frames):
        pre = total[f]
        sig = jax.nn.sigmoid(pre)
        act = pre * sig
        acts[f, :WIDTH] = act[:, :pair].astype(BF16)
        acts[f, WIDTH:] = act[:, pair:].astype(BF16)
        here = dact[f, pl.ds(pl.multiple_of(2 * WIDTH * r, 2 * WIDTH), 2 * WIDTH)]
        here = jnp.concatenate([here[:WIDTH], here[WIDTH:]], axis=1)
        slope = here * sig * (1.0 + pre * (1.0 - sig))
        slopes[WIDTH * f : WIDTH * (f + 1)] = slope.astype(BF16)
        part = mm(acts[f], cotangent[f, 0])
        down_total = part if down_total is None else down_total + part
    conv_total = [None] * 3
    for frame in range(frames + 2):
        used = taps_of(frame, frames)
        first, last = used[0][0], used[-1][0]
        values = x[frame].reshape(3 * TAPS, 2 * pair)
        part = mm(values, slopes[WIDTH * first : WIDTH * (last + 1)], NT)
        for f, a in used:
            here = part[:, WIDTH * (f - first) : WIDTH * (f - first + 1)]
            conv_total[a] = here if conv_total[a] is None else conv_total[a] + here
    slope_total = mm(jnp.ones((8, 2 * pair), BF16), slopes[...], NT)
    slope_total = sum(slope_total[:, WIDTH * f : WIDTH * (f + 1)] for f in range(frames))
    return jnp.concatenate(conv_total, axis=0), down_total, slope_total


def mid_kernel(dims, halo, *refs):
    table, rows_halo, x_early, x_own, pre_own, dact, outside, cotangent = refs[:8]
    acts, slopes, conv, down, total, x = refs[8:]
    core = lax.axis_index("core")
    conv[...], down[...], total[...] = one_row(
        dims, 1 - core, halo[...], *refs[:8], acts, slopes, x
    )


def at_end(heights):
    height = lax.axis_index(heights)
    return (height == 0) | (height == lax.axis_size(heights) - 1)


def main_kernel(dims, heights, halo, *refs):
    frames, rows, pair = dims
    _, _, _, _, _, _, _, cotangent = refs[:8]
    acts_in, slopes_in, conv_in, down_in, total_in, mine, keep, give, acts, slopes, x, packed = refs[8:]
    core = lax.axis_index("core")
    halo = (halo[...].astype(F32) * jnp.where(at_end(heights), 0.0, 1.0)).astype(BF16)
    acts[1 - core] = acts_in[...]
    slopes[1 - core] = slopes_in[...]
    conv, down, total = one_row(
        dims, core, halo, *refs[:8], acts.at[core], slopes.at[core], x
    )
    conv = conv + conv_in[...]
    slope_total = (total + total_in[...])[0:1]
    ones = jnp.ones((8, pair), BF16)
    cot_total = sum(mm(ones, cotangent[f, 0]) for f in range(frames))

    chunk = keep.shape[1]
    half = 27 * CH // 2
    sums = [slope_total, cot_total[0:1, :WIDTH], cot_total[0:1, WIDTH:]]
    highs = [value.astype(BF16).astype(F32) for value in sums]
    lows = [value - high for value, high in zip(sums, highs)]
    sums = jnp.concatenate(highs + lows + [jnp.zeros((2, WIDTH), F32)], axis=0)
    down_rows = 2 * rows * WIDTH
    for h in range(2):
        columns = slice(WIDTH * h, WIDTH * (h + 1))
        packed[h, :half] = conv[half * h : half * (h + 1)]
        for r, part in ((1 - core, down_in[:, columns]), (core, down[:, columns])):
            packed[h, pl.ds(pl.multiple_of(half + 2 * WIDTH * r, 8), 2 * WIDTH)] = part
        packed[h, half + down_rows : half + down_rows + 8] = sums if h == 0 else jnp.zeros_like(sums)
        rest = 4 * chunk - half - down_rows - 8
        if rest:
            packed[h, half + down_rows + 8 :] = jnp.zeros((rest, WIDTH), F32)
    for m in range(4):
        at = pl.multiple_of(jnp.bitwise_xor(order_of(core), m) * chunk, 8)
        if m:
            keep[m - 1] = packed[core, pl.ds(at, chunk)]
        else:
            mine[...] = packed[core, pl.ds(at, chunk)]
        at = pl.multiple_of(jnp.bitwise_xor(order_of(1 - core), m) * chunk, 8)
        give[m] = packed[1 - core, pl.ds(at, chunk)].astype(BF16)


def shifted_slope(slopes, f, r, pair):
    left, right = shifts(pair)
    slope = slopes[r, WIDTH * f : WIDTH * (f + 1)]
    even, odd = slope[:, :pair].astype(F32), slope[:, pair:].astype(F32)
    return jnp.concatenate(
        [
            jnp.concatenate([odd, left(even)], axis=1).astype(BF16),
            slope,
            jnp.concatenate([right(odd), even], axis=1).astype(BF16),
        ],
        axis=0,
    )


def spread_slope(total, slopes, backward, frames, reach, pair):
    for f in range(frames):
        for r in sorted({r for r, _, _ in reach}):
            taps = [(b, row) for here, b, row in reach if here == r]
            first, last = min(taps)[0], max(taps)[0]
            part = mm(backward[TAPS * first : TAPS * (last + 1)], shifted_slope(slopes, f, r, pair))
            for b, row in taps:
                for a in range(3):
                    at = TAPS * (b - first) + CH * a
                    here = part[at : at + CH]
                    key = (f + a, row)
                    total[key] = here if key not in total else total[key] + here


def edge_kernel(dims, slopes, backward, table, rows_halo, send_inner, send_outer):
    frames, rows, pair = dims
    core = lax.axis_index("core")
    total = {}
    spread_slope(total, slopes, backward, frames, [(0, 0, 0), (rows - 1, 2, 1)], pair)
    groups = [
        jnp.concatenate([total[frame, row] for frame in range(frames + 2)], axis=0) for row in range(2)
    ]
    above, below = synthesise(groups, table, [rows_halo, rows_halo], pair)
    send_inner[...] = jnp.where(core == 0, below, above).astype(BF16)
    send_outer[...] = jnp.where(core == 0, above, below).astype(BF16)


def late_kernel(
    dims,
    acts,
    slopes,
    backward,
    down_weight,
    down_bias,
    table,
    rows_own,
    features,
    pixels_own,
    pixels_early,
):
    frames, rows, pair = dims
    total = {}
    reach = [(r, b, r + b - 1) for r in range(rows) for b in range(3) if 0 <= r + b - 1 < rows]
    spread_slope(total, slopes, backward, frames, reach, pair)
    groups = [
        jnp.concatenate([total[first + f, r] for f in range(frames) for r in range(rows)], axis=0)
        for first in (0, 2)
    ]
    pixels_early[...], pixels_own[...] = synthesise(groups, table, [rows_own, rows_own], pair)
    for f in range(frames):
        blocks = [acts[u, f, WIDTH * v : WIDTH * (v + 1)] for u in range(2) for v in range(2)]
        turned = jnp.concatenate([block.astype(F32).T.astype(BF16) for block in blocks], axis=1)
        features[f, 0] = (mm(turned, down_weight[...]) + down_bias[...]).astype(BF16)


def finish_kernel(scale, other, *refs):
    pieces, (conv, conv_bias, down, down_bias, flat, sums, sems) = refs[:4], refs[-7:]
    if other:
        pieces = [refs[0], *(refs[1].at[m] for m in range(3))]
    core = lax.axis_index("core")
    which = 1 - core if other else core
    chunk = pieces[0].shape[0]
    for m in range(4):
        at = pl.multiple_of(jnp.bitwise_xor(order_of(which), m) * chunk, 8)
        flat[pl.ds(at, chunk)] = pieces[m][...].astype(F32) * scale
    half, down_rows = conv.shape[0] // 2, down.shape[0]
    at = pl.multiple_of(half * which, 8)
    copies = [
        pltpu.make_async_copy(flat.at[pl.ds(0, half)], conv.at[pl.ds(at, half)], sems.at[0]),
        pltpu.make_async_copy(
            flat.at[pl.ds(half, down_rows)],
            down.at[:, pl.ds(pl.multiple_of(WIDTH * which, WIDTH), WIDTH)],
            sems.at[1],
        ),
    ]
    for copy in copies:
        copy.start()

    @pl.when(which == 0)
    def _():
        at = half + down_rows
        total = flat[at : at + 8]
        total = total[0:3] + total[3:6]
        for n in range(3):
            sums[n] = total[n : n + 1]
        targets = [conv_bias, down_bias.at[:, pl.ds(0, WIDTH)], down_bias.at[:, pl.ds(WIDTH, WIDTH)]]
        small = [
            pltpu.make_async_copy(sums.at[n], target, sems.at[2 + n]) for n, target in enumerate(targets)
        ]
        for copy in small:
            copy.start()
        for copy in small:
            copy.wait()

    for copy in copies:
        copy.wait()


def local(axes, pixels, conv_weight, conv_bias, down_weight, down_bias, cotangent):
    times, heights = axes["tm"], axes["height"]
    frames, colors, pixel_rows, pixel_columns = pixels.shape
    rows, columns = pixel_rows // 4, pixel_columns // 4
    assert frames == 2 and rows == 2 and colors == COLORS
    assert conv_weight.shape[3:] == (CH, WIDTH)
    pair = columns // 2
    width2 = down_weight.shape[3]
    core = lax.axis_index("core")
    count_tm, count_height = lax.axis_size(times), lax.axis_size(heights)
    dims = (frames, rows, pair)

    def along_tm(value, step):
        pairs = [(i, (i + step) % count_tm) for i in range(count_tm)]
        return lax.ppermute(value, times, pairs)

    def swap_inner(value):
        return lax.ppermute(value, "core", [(0, 1), (1, 0)])

    def swap_outer(value):
        inside = [(i, i + 1) for i in range(1, count_height - 1, 2)]
        inside += [(j, i) for i, j in inside]
        pairs = [(count_height * t + i, count_height * t + j) for t in range(count_tm) for i, j in inside]
        for end in (0, count_height - 1):
            pairs += [(count_height * t + end, count_height * (t ^ 1) + end) for t in range(count_tm)]
        return lax.ppermute(value, times + heights, pairs)

    def exchange(value, axes, mask):
        size = lax.axis_size(axes)
        return lax.ppermute(value, axes, [(i, i ^ mask) for i in range(size)])

    own = pixels.reshape(frames * colors * pixel_rows, pixel_columns)
    came = along_tm(own, 1)
    flat_halo = ((frames + 2) * colors * 4, pixel_columns)
    frame_shape = (2 * colors, pixel_rows, pixel_columns)
    sources = [
        conv_weight.reshape(27, CH, WIDTH),
        own,
        jnp.asarray(column_table(pair // 2), BF16),
        jnp.asarray(row_table(frames, rows), BF16),
        down_weight.reshape(4 * WIDTH, width2),
        cotangent,
        jnp.asarray(row_table(frames + 2, 1), BF16),
        jnp.asarray(choose_table(frames, rows), BF16),
        conv_bias.reshape(1, WIDTH),
        down_bias.reshape(1, width2),
    ]
    outs = call(
        functools.partial(first_kernel, dims, len(sources)),
        [(source.shape, source.dtype) for source in sources[1:]]
        + [
            ((2, 3 * WIDTH, 2 * TAPS), BF16),
            ((2, 3 * WIDTH, TAPS), BF16),
            ((9 * CH, 3 * WIDTH), BF16),
            ((frames, rows, TAPS, columns), BF16),
            ((frames, 4 * WIDTH, pair), F32),
        ],
        [HBM] * len(sources),
        [pltpu.VMEM((27, CH, WIDTH), BF16), pltpu.SemaphoreType.DMA((len(sources),))],
        flops=10**9,
    )(*(pltpu.with_memory_space_constraint(source, pltpu.HBM) for source in sources))
    own, table, rows_own, down_flat, cot, rows_halo, chosen, bias, bias2 = outs[:9]
    inside, outside, backward, x_own, dact = outs[9:]
    send_inner, send_outer, earlier = call(
        functools.partial(pack_kernel, times), [(flat_halo, BF16), (flat_halo, BF16), (own.shape, BF16)], [VMEM] * 3
    )(own, came, chosen)
    inner = swap_inner(send_inner)
    outer = swap_outer(send_outer)

    x_early, pre_own = call(
        functools.partial(early_kernel, dims),
        [((2, rows, TAPS, columns), BF16), ((frames, rows, WIDTH, columns), F32)],
        [VMEM] * 6,
        flops=10**9,
    )(earlier, table, rows_own, inside, bias, x_own)

    data_rows = 27 * CH // 2 + 4 * WIDTH + 8
    chunk = -(-data_rows // 32) * 8
    common = (table, rows_halo, x_early, x_own, pre_own, dact, outside, cot)
    rows_scratch = pltpu.VMEM((frames + 2, 3, TAPS, columns), BF16)
    acts_shape = (frames, 2 * WIDTH, pair)
    slopes_shape = (frames * WIDTH, columns)
    inside_parts = call(
        functools.partial(mid_kernel, dims),
        [
            (acts_shape, BF16),
            (slopes_shape, BF16),
            ((27 * CH, WIDTH), F32),
            ((2 * WIDTH, width2), F32),
            ((8, WIDTH), F32),
        ],
        [VMEM] * 9,
        [rows_scratch],
        flops=10**9,
    )(inner, *common)
    mine, keep, give, acts, slopes = call(
        functools.partial(main_kernel, dims, heights),
        [
            ((chunk, WIDTH), F32),
            ((3, chunk, WIDTH), F32),
            ((4, chunk, WIDTH), BF16),
            ((rows, *acts_shape), BF16),
            ((rows, *slopes_shape), BF16),
        ],
        [VMEM] * 14,
        [rows_scratch, pltpu.VMEM((2, 4 * chunk, WIDTH), F32)],
        flops=10**9,
    )(outer, *common, *inside_parts)

    send_inner, send_outer = call(
        functools.partial(edge_kernel, dims), [(flat_halo, BF16), (flat_halo, BF16)], [VMEM] * 4, flops=10**9
    )(slopes, backward, table, rows_halo)
    features, pixels_own, pixels_early = call(
        functools.partial(late_kernel, dims),
        [((frames, rows // 2, pair, width2), BF16), (own.shape, F32), (own.shape, F32)],
        [VMEM] * 7,
        flops=10**9,
    )(acts, slopes, backward, down_flat, bias2, table, rows_own)

    def cross(value, mask, first):
        names = times + heights
        sizes = [lax.axis_size(axis) for axis in names]
        pairs = []
        for source in range(math.prod(sizes)):
            at = dict(zip(names, np.unravel_index(source, sizes)))
            if (at["core"] == 0) == first:
                at["tm_lo"], at["y"] = at["tm_lo"] ^ (mask >> 1), at["y"] ^ (mask & 1)
            else:
                at["z_0"] ^= mask
            target = np.ravel_multi_index([at[axis] for axis in names], sizes)
            pairs.append((source, int(target)))
        return lax.ppermute(value, names, pairs)

    given = swap_inner(give)
    rest = (keep + given[1:].astype(F32)).astype(BF16)
    steps = (1, 2, 3)
    parts = [cross(rest[m - 1], m, True) for m in steps]
    mine = mine + given[0].astype(F32) + sum(part.astype(F32) for part in parts)
    mine = mine.astype(BF16)
    parts = [cross(mine, m, False) for m in steps]
    mine = (mine.astype(F32) + sum(part.astype(F32) for part in parts)).astype(BF16)
    for axis in axes["rest"]:
        parts = [exchange(mine, axis, m) for m in range(1, lax.axis_size(axis))]
        mine = (mine.astype(F32) + sum(part.astype(F32) for part in parts)).astype(BF16)
    pieces = [mine] + [cross(mine, m, True) for m in steps]
    theirs_mine = swap_inner(mine)
    theirs = swap_inner(jnp.stack(pieces[1:]))
    count = frames * count_tm * rows * count_height * columns
    scale = 1.0 / math.sqrt(count)
    outs = [
        ((27 * CH, WIDTH), F32),
        ((1, WIDTH), F32),
        ((4 * WIDTH, width2), F32),
        ((1, width2), F32),
    ]
    scratch = [
        pltpu.VMEM((4 * chunk, WIDTH), F32),
        pltpu.VMEM((3, 1, WIDTH), F32),
        pltpu.SemaphoreType.DMA((5,)),
    ]
    grads = call(
        functools.partial(finish_kernel, scale, False), outs, [VMEM] * 4, scratch, out_specs=[HBM] * 4
    )(*pieces)
    grad_conv, grad_conv_bias, grad_down, grad_down_bias = call(
        functools.partial(finish_kernel, scale, True),
        outs,
        [VMEM] * 2 + [HBM] * 4,
        scratch,
        out_specs=[HBM] * 4,
        input_output_aliases={2: 0, 3: 1, 4: 2, 5: 3},
    )(theirs_mine, theirs, *grads)

    from_inner = swap_inner(send_inner).reshape((frames + 2) * colors, 4, pixel_columns)
    from_outer = swap_outer(send_outer).reshape((frames + 2) * colors, 4, pixel_columns)
    from_outer = jnp.where(at_end(heights), 0, from_outer)
    above = jnp.where(core == 0, from_outer, from_inner).astype(F32)
    below = jnp.where(core == 0, from_inner, from_outer).astype(F32)
    halo = jnp.concatenate([above, below], axis=1)
    early = pixels_early.reshape(frame_shape) + halo[: 2 * colors]
    late = pixels_own.reshape(frame_shape) + halo[2 * colors :]
    following = along_tm(early.astype(BF16), -1)
    last = lax.axis_index(times) == count_tm - 1
    grad_pixels = late + jnp.where(last, 0.0, following.astype(F32))
    return (
        features,
        grad_conv.reshape(conv_weight.shape),
        grad_conv_bias.reshape(WIDTH),
        grad_down.reshape(down_weight.shape),
        grad_down_bias.reshape(width2),
        grad_pixels.reshape(pixels.shape),
    )


def factors(size):
    parts = []
    while size > 1:
        part = 4 if size % 4 == 0 else 2
        assert size % part == 0
        parts.append(part)
        size //= part
    return parts


def solution(mesh):
    count_tm, count_height = mesh.shape["tm"], mesh.shape["height"]
    tm_parts, height_parts = factors(count_tm // 2), factors(count_height // 4)
    assert height_parts[0] == 4
    tm_names = tuple(f"tm_{n}" for n in range(len(tm_parts)))
    height_names = tuple(f"z_{n}" for n in range(len(height_parts)))
    axes = {
        "tm": tm_names + ("tm_lo",),
        "height": height_names + ("y", "core"),
        "rest": tm_names + height_names[1:],
    }
    fine = Mesh(
        mesh.devices.reshape(tm_parts + [2] + height_parts + [2, 2]), axes["tm"] + axes["height"]
    )
    tm, height = axes["tm"], axes["height"]

    def body(*args):
        return local(axes, *args)

    return jax.shard_map(
        body,
        mesh=fine,
        in_specs=(P(tm, None, height, None), P(), P(), P(), P(), P(tm, height, None, None)),
        out_specs=(
            P(tm, height, None, None),
            P(),
            P(),
            P(),
            P(),
            P(tm, None, height, None),
        ),
        check_vma=False,
    )
```

```python
import functools
import math

import jax
import jax.numpy as jnp
import numpy as np
from jax import lax
from jax.experimental import pallas as pl
from jax.experimental.pallas import tpu as pltpu
from jax.sharding import Mesh, PartitionSpec as P


BF16, F32 = jnp.bfloat16, jnp.float32
HAAR = np.kron(np.array([[1.0, 1.0], [1.0, -1.0]]), np.array([[1.0, 1.0], [1.0, -1.0]])) * 0.5
VMEM = pl.BlockSpec(memory_space=pltpu.VMEM)
HBM = pl.BlockSpec(memory_space=pltpu.HBM)
NN = (((1,), (0,)), ((), ()))
NT = (((1,), (1,)), ((), ()))
COLORS, CH, WIDTH = 3, 48, 128
TAPS = 3 * CH


def mm(a, b, dims=NN):
    return lax.dot_general(a, b, dims, preferred_element_type=F32)


def split(x):
    high = x.astype(BF16)
    return high, (x - high.astype(F32)).astype(BF16)


def order_of(core):
    plane = 2 * lax.axis_index("tm_lo") + lax.axis_index("y")
    return jnp.where(core == 0, plane, lax.axis_index("z_0"))


def call(body, outs, ins, scratch=(), flops=0, grant=24, **more):
    shapes = [jax.ShapeDtypeStruct(shape, dtype) for shape, dtype in outs]
    return pl.pallas_call(
        body,
        out_shape=shapes,
        scratch_shapes=list(scratch),
        cost_estimate=pl.CostEstimate(flops=flops, bytes_accessed=1 << 20, transcendentals=0),
        compiler_params=pltpu.CompilerParams(vmem_limit_bytes=grant << 20),
        in_specs=ins,
        **{"out_specs": [VMEM] * len(outs), **more},
    )


def column_table(quarter):
    table = np.zeros((8 * quarter, 4, 2, quarter), np.float32)
    for parity in range(2):
        for pair in range(quarter):
            for v in range(4):
                table[8 * pair + 4 * parity + v, :, parity, pair] = HAAR[:, v]
    return table.reshape(8 * quarter, 8 * quarter)


def row_table(frames, rows):
    table = np.zeros((frames, rows, COLORS, 4, 4, 4, frames, COLORS, rows, 4), np.float32)
    for f in range(frames):
        for r in range(rows):
            for k in range(COLORS):
                for j in range(4):
                    table[f, r, k, :, j, j, f, k, r, :] = HAAR
    return table.reshape(frames * rows * CH, 4 * frames * COLORS * rows * 4)


def choose_table(frames, rows):
    table = np.zeros((2, 2, frames + 2, COLORS, 4, frames + 2, COLORS, 4 * rows), np.float32)
    for core in range(2):
        for way in range(2):
            at = 4 * rows - 4 if core == way else 0
            for f in range(frames + 2):
                for k in range(COLORS):
                    for u in range(4):
                        table[core, way, f, k, u, f, k, at + u] = 1.0
    return table.reshape(2, 2 * (frames + 2) * COLORS * 4, (frames + 2) * COLORS * 4 * rows)


def shifts(pair):
    lane = lax.broadcasted_iota(jnp.int32, (1, pair), 1)

    def left(value):
        return jnp.where(lane == pair - 1, 0.0, pltpu.roll(value, pair - 1, 1))

    def right(value):
        return jnp.where(lane == 0, 0.0, pltpu.roll(value, 1, 1))

    return left, right


def analyse(groups, table, rows_tables, x, places, pair):
    left, right = shifts(pair)
    low_half = lax.broadcasted_iota(jnp.int32, (1, pair), 1) < pair // 2
    size, width = groups[0].shape
    stacked = [group[:, half * width // 2 : (half + 1) * width // 2] for group in groups for half in range(2)]
    columns = mm(jnp.concatenate(stacked, axis=0), table[...])
    for n, (rows_table, where) in enumerate(zip(rows_tables, places)):
        blocks = []
        for j in range(4):
            one = columns[2 * n * size : (2 * n + 1) * size, pair * j : pair * (j + 1)]
            two = columns[(2 * n + 1) * size : (2 * n + 2) * size, pair * j : pair * (j + 1)]
            even = jnp.where(low_half, one, pltpu.roll(two, pair // 2, 1))
            odd = jnp.where(low_half, pltpu.roll(one, pair // 2, 1), two)
            blocks.append(jnp.concatenate([even, odd], axis=1))
        high, low = split(jnp.concatenate(blocks, axis=0))
        cells = (mm(rows_table[...], high) + mm(rows_table[...], low)).astype(BF16)
        even, odd = cells[:, :pair].astype(F32), cells[:, pair:].astype(F32)
        taps = (
            jnp.concatenate([right(odd), even], axis=1).astype(BF16),
            cells,
            jnp.concatenate([odd, left(even)], axis=1).astype(BF16),
        )
        for block, (f, r) in enumerate(where):
            for d in range(3):
                x[f, r, CH * d : CH * (d + 1)] = taps[d][CH * block : CH * (block + 1)]


def synthesise(groups, table, rows_tables, pair):
    low_half = lax.broadcasted_iota(jnp.int32, (1, pair), 1) < pair // 2
    stacked = []
    for cells, rows_table in zip(groups, rows_tables):
        turned = mm(rows_table[...], cells.astype(BF16), (((0,), (0,)), ((), ())))
        size = turned.shape[0] // 4
        ones, twos = [], []
        for j in range(4):
            even = turned[size * j : size * (j + 1), :pair]
            odd = turned[size * j : size * (j + 1), pair:]
            ones.append(jnp.where(low_half, even, pltpu.roll(odd, pair // 2, 1)))
            twos.append(jnp.where(low_half, pltpu.roll(even, pair // 2, 1), odd))
        stacked += [jnp.concatenate(ones, axis=1), jnp.concatenate(twos, axis=1)]
    pixels = mm(jnp.concatenate(stacked, axis=0).astype(BF16), table[...], NT)
    size = stacked[0].shape[0]
    return [
        jnp.concatenate(
            [pixels[2 * n * size : (2 * n + 1) * size], pixels[(2 * n + 1) * size : (2 * n + 2) * size]],
            axis=1,
        )
        for n in range(len(groups))
    ]


def first_kernel(dims, count, *refs):
    frames, rows, pair = dims
    sources, targets = refs[:count], refs[count : 2 * count - 1]
    inside, outside, backward, x, dact, cot_sum, raw, sems = refs[2 * count - 1 :]
    copies = [
        pltpu.make_async_copy(source, target, sems.at[n])
        for n, (source, target) in enumerate(zip(sources, (raw, *targets)))
    ]
    for copy in copies:
        copy.start()
    own, table, rows_own, down_weight, cotangent = targets[:5]
    copies[0].wait()
    for a in range(3):
        for b in range(3):
            for d in range(3):
                at = CH * (3 * b + a)
                backward[at : at + CH, WIDTH * d : WIDTH * (d + 1)] = raw[9 * a + 3 * b + d]
        taps = raw[9 * a : 9 * a + 9].reshape(3 * TAPS, WIDTH).astype(F32)
        at = slice(WIDTH * a, WIDTH * (a + 1))
        inside[0, at] = taps[TAPS:].T.astype(BF16)
        inside[1, at] = taps[: 2 * TAPS].T.astype(BF16)
        outside[0, at] = taps[:TAPS].T.astype(BF16)
        outside[1, at] = taps[2 * TAPS :].T.astype(BF16)
    for copy in copies[1:]:
        copy.wait()
    where = [(f, r) for f in range(frames) for r in range(rows)]
    analyse([own[...]], table, [rows_own], x, [where], pair)
    for f in range(frames):
        dact[f] = mm(down_weight[...], cotangent[f, 0], NT)
    ones = jnp.ones((8, pair), BF16)
    cot_sum[...] = sum(mm(ones, cotangent[f, 0]) for f in range(frames))


def pack_kernel(times, own, came, chosen, inner, outer, earlier):
    core = lax.axis_index("core")
    used = jnp.where(lax.axis_index(times) == 0, 0.0, 1.0)
    earlier[...] = (came[...].astype(F32) * used).astype(BF16)
    both = mm(chosen[core], jnp.concatenate([earlier[...], own[...]], axis=0)).astype(BF16)
    size = inner.shape[0]
    inner[...] = both[:size]
    outer[...] = both[size:]


def taps_of(frame, frames):
    return [(f, frame - f) for f in range(frames) if 0 <= frame - f < 3]


def convolve(total, weights, values, frame, frames):
    used = taps_of(frame, frames)
    first = min(a for _, a in used)
    last = max(a for _, a in used)
    part = mm(weights[WIDTH * first : WIDTH * (last + 1)], values)
    for f, a in used:
        here = part[WIDTH * (a - first) : WIDTH * (a - first + 1)]
        total[f] = here if total[f] is None else total[f] + here


def early_kernel(dims, earlier, table, rows_own, inside, conv_bias, x_own, x, pre):
    frames, rows, pair = dims
    where = [(f, r) for f in range(2) for r in range(rows)]
    analyse([earlier[...]], table, [rows_own], x, [where], pair)
    bias = jnp.broadcast_to(conv_bias[...], (WIDTH, WIDTH)).T
    bias = jnp.concatenate([bias] * (2 * pair // WIDTH), axis=1)
    for r in range(rows):
        total = [bias] * frames
        for frame in range(frames + 2):
            values = (x[frame] if frame < 2 else x_own[frame - 2]).reshape(rows * TAPS, 2 * pair)
            convolve(total, inside[r], values, frame, frames)
        for f in range(frames):
            pre[f, r] = total[f]


def one_row(dims, r, halo, table, rows_halo, x_early, x_own, pre_own, dact, outside, cotangent, acts, slopes, x):
    frames, rows, pair = dims
    for frame in range(frames + 2):
        here = x_early[frame] if frame < 2 else x_own[frame - 2]
        x[frame, pl.ds(1 - r, rows)] = here
    analyse([halo], table, [rows_halo], x, [[(f, 2 * r) for f in range(frames + 2)]], pair)
    total = [pre_own[f, r] for f in range(frames)]
    for frame in range(frames + 2):
        convolve(total, outside[r], x[frame, 2 * r], frame, frames)
    down_total = None
    for f in range(frames):
        pre = total[f]
        sig = jax.nn.sigmoid(pre)
        act = pre * sig
        acts[f, :WIDTH] = act[:, :pair].astype(BF16)
        acts[f, WIDTH:] = act[:, pair:].astype(BF16)
        here = dact[f, pl.ds(pl.multiple_of(2 * WIDTH * r, 2 * WIDTH), 2 * WIDTH)]
        here = jnp.concatenate([here[:WIDTH], here[WIDTH:]], axis=1)
        slope = here * sig * (1.0 + pre * (1.0 - sig))
        slopes[WIDTH * f : WIDTH * (f + 1)] = slope.astype(BF16)
        part = mm(acts[f], cotangent[f, 0])
        down_total = part if down_total is None else down_total + part
    conv_total = [None] * 3
    for frame in range(frames + 2):
        used = taps_of(frame, frames)
        first, last = used[0][0], used[-1][0]
        values = x[frame].reshape(3 * TAPS, 2 * pair)
        part = mm(values, slopes[WIDTH * first : WIDTH * (last + 1)], NT)
        for f, a in used:
            here = part[:, WIDTH * (f - first) : WIDTH * (f - first + 1)]
            conv_total[a] = here if conv_total[a] is None else conv_total[a] + here
    slope_total = mm(jnp.ones((8, 2 * pair), BF16), slopes[...], NT)
    slope_total = sum(slope_total[:, WIDTH * f : WIDTH * (f + 1)] for f in range(frames))
    return jnp.concatenate(conv_total, axis=0), down_total, slope_total


def mid_kernel(dims, halo, *refs):
    table, rows_halo, x_early, x_own, pre_own, dact, outside, cotangent = refs[:8]
    acts, slopes, conv, down, total, x = refs[8:]
    core = lax.axis_index("core")
    conv[...], down[...], total[...] = one_row(
        dims, 1 - core, halo[...], *refs[:8], acts, slopes, x
    )


def at_end(heights):
    height = lax.axis_index(heights)
    return (height == 0) | (height == lax.axis_size(heights) - 1)


def main_kernel(dims, heights, halo, *refs):
    _, rows, _ = dims
    table, rows_halo, x_early, x_own, pre_own, dact, outside, cotangent = refs[:8]
    cot_sum, acts_in, slopes_in, conv_in, down_in, total_in, mine, keep, give, acts, slopes, x, packed = refs[8:]
    core = lax.axis_index("core")
    halo = (halo[...].astype(F32) * jnp.where(at_end(heights), 0.0, 1.0)).astype(BF16)
    acts[1 - core] = acts_in[...]
    slopes[1 - core] = slopes_in[...]
    conv, down, total = one_row(
        dims, core, halo, *refs[:8], acts.at[core], slopes.at[core], x
    )
    conv = conv + conv_in[...]
    slope_total = (total + total_in[...])[0:1]
    cot_total = cot_sum[...]

    chunk = keep.shape[1]
    half = 27 * CH // 2
    sums = [slope_total, cot_total[0:1, :WIDTH], cot_total[0:1, WIDTH:]]
    highs = [value.astype(BF16).astype(F32) for value in sums]
    lows = [value - high for value, high in zip(sums, highs)]
    sums = jnp.concatenate(highs + lows + [jnp.zeros((2, WIDTH), F32)], axis=0)
    down_rows = 2 * rows * WIDTH
    for h in range(2):
        columns = slice(WIDTH * h, WIDTH * (h + 1))
        packed[h, :half] = conv[half * h : half * (h + 1)]
        for r, part in ((1 - core, down_in[:, columns]), (core, down[:, columns])):
            packed[h, pl.ds(pl.multiple_of(half + 2 * WIDTH * r, 8), 2 * WIDTH)] = part
        packed[h, half + down_rows : half + down_rows + 8] = sums if h == 0 else jnp.zeros_like(sums)
        rest = 4 * chunk - half - down_rows - 8
        if rest:
            packed[h, half + down_rows + 8 :] = jnp.zeros((rest, WIDTH), F32)
    for m in range(4):
        at = pl.multiple_of(jnp.bitwise_xor(order_of(core), m) * chunk, 8)
        if m:
            keep[m - 1] = packed[core, pl.ds(at, chunk)]
        else:
            mine[...] = packed[core, pl.ds(at, chunk)]
        at = pl.multiple_of(jnp.bitwise_xor(order_of(1 - core), m) * chunk, 8)
        give[m] = packed[1 - core, pl.ds(at, chunk)].astype(BF16)


def shifted_slope(slopes, f, r, pair):
    left, right = shifts(pair)
    slope = slopes[r, WIDTH * f : WIDTH * (f + 1)]
    even, odd = slope[:, :pair].astype(F32), slope[:, pair:].astype(F32)
    return jnp.concatenate(
        [
            jnp.concatenate([odd, left(even)], axis=1).astype(BF16),
            slope,
            jnp.concatenate([right(odd), even], axis=1).astype(BF16),
        ],
        axis=0,
    )


def spread_slope(total, slopes, backward, frames, reach, pair):
    for f in range(frames):
        for r in sorted({r for r, _, _ in reach}):
            taps = [(b, row) for here, b, row in reach if here == r]
            first, last = min(taps)[0], max(taps)[0]
            part = mm(backward[TAPS * first : TAPS * (last + 1)], shifted_slope(slopes, f, r, pair))
            for b, row in taps:
                for a in range(3):
                    at = TAPS * (b - first) + CH * a
                    here = part[at : at + CH]
                    key = (f + a, row)
                    total[key] = here if key not in total else total[key] + here


def edge_kernel(dims, slopes, backward, table, rows_halo, send_inner, send_outer):
    frames, rows, pair = dims
    core = lax.axis_index("core")
    total = {}
    spread_slope(total, slopes, backward, frames, [(0, 0, 0), (rows - 1, 2, 1)], pair)
    groups = [
        jnp.concatenate([total[frame, row] for frame in range(frames + 2)], axis=0) for row in range(2)
    ]
    above, below = synthesise(groups, table, [rows_halo, rows_halo], pair)
    send_inner[...] = jnp.where(core == 0, below, above).astype(BF16)
    send_outer[...] = jnp.where(core == 0, above, below).astype(BF16)


def late_kernel(
    dims,
    acts,
    slopes,
    backward,
    down_weight,
    down_bias,
    table,
    rows_own,
    features,
    pixels_own,
    pixels_early,
):
    frames, rows, pair = dims
    total = {}
    reach = [(r, b, r + b - 1) for r in range(rows) for b in range(3) if 0 <= r + b - 1 < rows]
    spread_slope(total, slopes, backward, frames, reach, pair)
    groups = [
        jnp.concatenate([total[first + f, r] for f in range(frames) for r in range(rows)], axis=0)
        for first in (0, 2)
    ]
    pixels_early[...], pixels_own[...] = synthesise(groups, table, [rows_own, rows_own], pair)
    for f in range(frames):
        blocks = [acts[u, f, WIDTH * v : WIDTH * (v + 1)] for u in range(2) for v in range(2)]
        turned = jnp.concatenate([block.astype(F32).T.astype(BF16) for block in blocks], axis=1)
        features[f, 0] = (mm(turned, down_weight[...]) + down_bias[...]).astype(BF16)


def finish_kernel(scale, other, *refs):
    pieces, (conv, conv_bias, down, down_bias, flat, sums, sems) = refs[:4], refs[-7:]
    if other:
        pieces = [refs[0], *(refs[1].at[m] for m in range(3))]
    core = lax.axis_index("core")
    which = 1 - core if other else core
    chunk = pieces[0].shape[0]
    for m in range(4):
        at = pl.multiple_of(jnp.bitwise_xor(order_of(which), m) * chunk, 8)
        flat[pl.ds(at, chunk)] = pieces[m][...].astype(F32) * scale
    half, down_rows = conv.shape[0] // 2, down.shape[0]
    at = pl.multiple_of(half * which, 8)
    copies = [
        pltpu.make_async_copy(flat.at[pl.ds(0, half)], conv.at[pl.ds(at, half)], sems.at[0]),
        pltpu.make_async_copy(
            flat.at[pl.ds(half, down_rows)],
            down.at[:, pl.ds(pl.multiple_of(WIDTH * which, WIDTH), WIDTH)],
            sems.at[1],
        ),
    ]
    for copy in copies:
        copy.start()

    @pl.when(which == 0)
    def _():
        at = half + down_rows
        total = flat[at : at + 8]
        total = total[0:3] + total[3:6]
        for n in range(3):
            sums[n] = total[n : n + 1]
        targets = [conv_bias, down_bias.at[:, pl.ds(0, WIDTH)], down_bias.at[:, pl.ds(WIDTH, WIDTH)]]
        small = [
            pltpu.make_async_copy(sums.at[n], target, sems.at[2 + n]) for n, target in enumerate(targets)
        ]
        for copy in small:
            copy.start()
        for copy in small:
            copy.wait()

    for copy in copies:
        copy.wait()


def local(axes, pixels, conv_weight, conv_bias, down_weight, down_bias, cotangent):
    times, heights = axes["tm"], axes["height"]
    frames, colors, pixel_rows, pixel_columns = pixels.shape
    rows, columns = pixel_rows // 4, pixel_columns // 4
    assert frames == 2 and rows == 2 and colors == COLORS
    assert conv_weight.shape[3:] == (CH, WIDTH)
    pair = columns // 2
    width2 = down_weight.shape[3]
    core = lax.axis_index("core")
    count_tm, count_height = lax.axis_size(times), lax.axis_size(heights)
    dims = (frames, rows, pair)

    def along_tm(value, step):
        pairs = [(i, (i + step) % count_tm) for i in range(count_tm)]
        return lax.ppermute(value, times, pairs)

    def swap_inner(value):
        return lax.ppermute(value, "core", [(0, 1), (1, 0)])

    def swap_outer(value):
        inside = [(i, i + 1) for i in range(1, count_height - 1, 2)]
        inside += [(j, i) for i, j in inside]
        pairs = [(count_height * t + i, count_height * t + j) for t in range(count_tm) for i, j in inside]
        for end in (0, count_height - 1):
            pairs += [(count_height * t + end, count_height * (t ^ 1) + end) for t in range(count_tm)]
        return lax.ppermute(value, times + heights, pairs)

    def exchange(value, axes, mask):
        size = lax.axis_size(axes)
        return lax.ppermute(value, axes, [(i, i ^ mask) for i in range(size)])

    own = pixels.reshape(frames * colors * pixel_rows, pixel_columns)
    came = along_tm(own, 1)
    flat_halo = ((frames + 2) * colors * 4, pixel_columns)
    frame_shape = (2 * colors, pixel_rows, pixel_columns)
    sources = [
        conv_weight.reshape(27, CH, WIDTH),
        own,
        jnp.asarray(column_table(pair // 2), BF16),
        jnp.asarray(row_table(frames, rows), BF16),
        down_weight.reshape(4 * WIDTH, width2),
        cotangent,
        jnp.asarray(row_table(frames + 2, 1), BF16),
        jnp.asarray(choose_table(frames, rows), BF16),
        conv_bias.reshape(1, WIDTH),
        down_bias.reshape(1, width2),
    ]
    outs = call(
        functools.partial(first_kernel, dims, len(sources)),
        [(source.shape, source.dtype) for source in sources[1:]]
        + [
            ((2, 3 * WIDTH, 2 * TAPS), BF16),
            ((2, 3 * WIDTH, TAPS), BF16),
            ((9 * CH, 3 * WIDTH), BF16),
            ((frames, rows, TAPS, columns), BF16),
            ((frames, 4 * WIDTH, pair), F32),
            ((8, width2), F32),
        ],
        [HBM] * len(sources),
        [pltpu.VMEM((27, CH, WIDTH), BF16), pltpu.SemaphoreType.DMA((len(sources),))],
        flops=10**9,
    )(*(pltpu.with_memory_space_constraint(source, pltpu.HBM) for source in sources))
    own, table, rows_own, down_flat, cot, rows_halo, chosen, bias, bias2 = outs[:9]
    inside, outside, backward, x_own, dact, cot_sum = outs[9:]
    send_inner, send_outer, earlier = call(
        functools.partial(pack_kernel, times), [(flat_halo, BF16), (flat_halo, BF16), (own.shape, BF16)], [VMEM] * 3
    )(own, came, chosen)
    inner = swap_inner(send_inner)
    outer = swap_outer(send_outer)

    x_early, pre_own = call(
        functools.partial(early_kernel, dims),
        [((2, rows, TAPS, columns), BF16), ((frames, rows, WIDTH, columns), F32)],
        [VMEM] * 6,
        flops=10**9,
    )(earlier, table, rows_own, inside, bias, x_own)

    data_rows = 27 * CH // 2 + 4 * WIDTH + 8
    chunk = -(-data_rows // 32) * 8
    common = (table, rows_halo, x_early, x_own, pre_own, dact, outside, cot)
    rows_scratch = pltpu.VMEM((frames + 2, 3, TAPS, columns), BF16)
    acts_shape = (frames, 2 * WIDTH, pair)
    slopes_shape = (frames * WIDTH, columns)
    inside_parts = call(
        functools.partial(mid_kernel, dims),
        [
            (acts_shape, BF16),
            (slopes_shape, BF16),
            ((27 * CH, WIDTH), F32),
            ((2 * WIDTH, width2), F32),
            ((8, WIDTH), F32),
        ],
        [VMEM] * 9,
        [rows_scratch],
        flops=10**9,
    )(inner, *common)
    mine, keep, give, acts, slopes = call(
        functools.partial(main_kernel, dims, heights),
        [
            ((chunk, WIDTH), F32),
            ((3, chunk, WIDTH), F32),
            ((4, chunk, WIDTH), BF16),
            ((rows, *acts_shape), BF16),
            ((rows, *slopes_shape), BF16),
        ],
        [VMEM] * 15,
        [rows_scratch, pltpu.VMEM((2, 4 * chunk, WIDTH), F32)],
        flops=10**9,
    )(outer, *common, cot_sum, *inside_parts)

    send_inner, send_outer = call(
        functools.partial(edge_kernel, dims), [(flat_halo, BF16), (flat_halo, BF16)], [VMEM] * 4, flops=10**9
    )(slopes, backward, table, rows_halo)
    features, pixels_own, pixels_early = call(
        functools.partial(late_kernel, dims),
        [((frames, rows // 2, pair, width2), BF16), (own.shape, F32), (own.shape, F32)],
        [VMEM] * 7,
        flops=10**9,
    )(acts, slopes, backward, down_flat, bias2, table, rows_own)

    def cross(value, mask, first):
        names = times + heights
        sizes = [lax.axis_size(axis) for axis in names]
        pairs = []
        for source in range(math.prod(sizes)):
            at = dict(zip(names, np.unravel_index(source, sizes)))
            if (at["core"] == 0) == first:
                at["tm_lo"], at["y"] = at["tm_lo"] ^ (mask >> 1), at["y"] ^ (mask & 1)
            else:
                at["z_0"] ^= mask
            target = np.ravel_multi_index([at[axis] for axis in names], sizes)
            pairs.append((source, int(target)))
        return lax.ppermute(value, names, pairs)

    given = swap_inner(give)
    rest = (keep + given[1:].astype(F32)).astype(BF16)
    steps = (1, 2, 3)
    parts = [cross(rest[m - 1], m, True) for m in steps]
    mine = mine + given[0].astype(F32) + sum(part.astype(F32) for part in parts)
    mine = mine.astype(BF16)
    parts = [cross(mine, m, False) for m in steps]
    mine = (mine.astype(F32) + sum(part.astype(F32) for part in parts)).astype(BF16)
    for axis in axes["rest"]:
        parts = [exchange(mine, axis, m) for m in range(1, lax.axis_size(axis))]
        mine = (mine.astype(F32) + sum(part.astype(F32) for part in parts)).astype(BF16)
    pieces = [mine] + [cross(mine, m, True) for m in steps]
    theirs_mine = swap_inner(mine)
    theirs = swap_inner(jnp.stack(pieces[1:]))
    count = frames * count_tm * rows * count_height * columns
    scale = 1.0 / math.sqrt(count)
    outs = [
        ((27 * CH, WIDTH), F32),
        ((1, WIDTH), F32),
        ((4 * WIDTH, width2), F32),
        ((1, width2), F32),
    ]
    scratch = [
        pltpu.VMEM((4 * chunk, WIDTH), F32),
        pltpu.VMEM((3, 1, WIDTH), F32),
        pltpu.SemaphoreType.DMA((5,)),
    ]
    grads = call(
        functools.partial(finish_kernel, scale, False), outs, [VMEM] * 4, scratch, out_specs=[HBM] * 4
    )(*pieces)
    grad_conv, grad_conv_bias, grad_down, grad_down_bias = call(
        functools.partial(finish_kernel, scale, True),
        outs,
        [VMEM] * 2 + [HBM] * 4,
        scratch,
        out_specs=[HBM] * 4,
        input_output_aliases={2: 0, 3: 1, 4: 2, 5: 3},
    )(theirs_mine, theirs, *grads)

    from_inner = swap_inner(send_inner).reshape((frames + 2) * colors, 4, pixel_columns)
    from_outer = swap_outer(send_outer).reshape((frames + 2) * colors, 4, pixel_columns)
    from_outer = jnp.where(at_end(heights), 0, from_outer)
    above = jnp.where(core == 0, from_outer, from_inner).astype(F32)
    below = jnp.where(core == 0, from_inner, from_outer).astype(F32)
    halo = jnp.concatenate([above, below], axis=1)
    early = pixels_early.reshape(frame_shape) + halo[: 2 * colors]
    late = pixels_own.reshape(frame_shape) + halo[2 * colors :]
    following = along_tm(early.astype(BF16), -1)
    last = lax.axis_index(times) == count_tm - 1
    grad_pixels = late + jnp.where(last, 0.0, following.astype(F32))
    return (
        features,
        grad_conv.reshape(conv_weight.shape),
        grad_conv_bias.reshape(WIDTH),
        grad_down.reshape(down_weight.shape),
        grad_down_bias.reshape(width2),
        grad_pixels.reshape(pixels.shape),
    )


def factors(size):
    parts = []
    while size > 1:
        part = 4 if size % 4 == 0 else 2
        assert size % part == 0
        parts.append(part)
        size //= part
    return parts


def solution(mesh):
    count_tm, count_height = mesh.shape["tm"], mesh.shape["height"]
    tm_parts, height_parts = factors(count_tm // 2), factors(count_height // 4)
    assert height_parts[0] == 4
    tm_names = tuple(f"tm_{n}" for n in range(len(tm_parts)))
    height_names = tuple(f"z_{n}" for n in range(len(height_parts)))
    axes = {
        "tm": tm_names + ("tm_lo",),
        "height": height_names + ("y", "core"),
        "rest": tm_names + height_names[1:],
    }
    fine = Mesh(
        mesh.devices.reshape(tm_parts + [2] + height_parts + [2, 2]), axes["tm"] + axes["height"]
    )
    tm, height = axes["tm"], axes["height"]

    def body(*args):
        return local(axes, *args)

    return jax.shard_map(
        body,
        mesh=fine,
        in_specs=(P(tm, None, height, None), P(), P(), P(), P(), P(tm, height, None, None)),
        out_specs=(
            P(tm, height, None, None),
            P(),
            P(),
            P(),
            P(),
            P(tm, None, height, None),
        ),
        check_vma=False,
    )
```
